32 devices in a mesh: dp: 8 (over y, x, core), tensor: 4 (over z).
Axes of the slice: x: 2, y: 2, z: 4, core: 2. Of those that a mesh axis runs over, the one named last changes fastest.
Arguments:
- tokens: bfloat16 [16384, 3072], P(('dp', 'tensor')), may hold values from -6 to 6
- cotangent: bfloat16 [16384, 3072], P(('dp', 'tensor')), may hold values from -6 to 6
- segments: int32 [16384], P(('dp', 'tensor')), may hold values from 0 to 2, as said below
- positions: int32 [16384], P(('dp', 'tensor')), may hold values from 0 to 2046, as said below
- counts: int32 [8], P('dp'), may hold values from 1536 to 2048, as said below
- query_weight: bfloat16 [3072, 3072], P('dp', 'tensor'), may hold values from -0.109375 to 0.109375
- key_projection_weight: bfloat16 [3072, 1024], P('dp', 'tensor'), may hold values from -0.109375 to 0.109375
- value_projection_weight: bfloat16 [3072, 1024], P('dp', 'tensor'), may hold values from -0.109375 to 0.109375
- out_weight: bfloat16 [3072, 3072], P('tensor', 'dp'), may hold values from -2.5 to 2.5
- attn_gain: bfloat16 [3072], P('dp'), may hold values from 0.099609375 to 1.8984375
- gate_weight: bfloat16 [3072, 8192], P('dp', 'tensor'), may hold values from -0.109375 to 0.109375
- up_weight: bfloat16 [3072, 8192], P('dp', 'tensor'), may hold values from -0.109375 to 0.109375
- down_weight: bfloat16 [8192, 3072], P('tensor', 'dp'), may hold values from -0.0625 to 0.0625
- mlp_gain: bfloat16 [3072], P('dp'), may hold values from 0.099609375 to 1.8984375
Outputs:
- output: bfloat16 [16384, 3072], P(('dp', 'tensor'))
- grad_tokens: float32 [16384, 3072], P(('dp', 'tensor'))
- grad_query_weight: float32 [3072, 3072], P('dp', 'tensor')
- grad_key_weight: float32 [3072, 1024], P('dp', 'tensor')
- grad_value_weight: float32 [3072, 1024], P('dp', 'tensor')
- grad_out_weight: float32 [3072, 3072], P('tensor', 'dp')
- grad_attn_gain: float32 [3072], P('dp')
- grad_gate_weight: float32 [3072, 8192], P('dp', 'tensor')
- grad_up_weight: float32 [3072, 8192], P('dp', 'tensor')
- grad_down_weight: float32 [8192, 3072], P('tensor', 'dp')
- grad_mlp_gain: float32 [3072], P('dp')
The draws below stay inside these ranges and needn't reach their ends.
Inputs may be any that keep to these rules, and one draw needn't show every extreme that they name: `segments`: within each group of 2048 rows, segment numbers start at 0 and never fall; rows past the group's live count continue its last segment. positions start at 0 at the beginning of each segment and rise by one a row. `counts`: some group is full.
All inputs are finite; a program needn't handle non-finite values.
Results may differ from the reference program's by a relative error of at most 0.013.
Values may be sent and summed in bfloat16 or wider, within the bound.
A program may use at most 384 MiB of HBM per device.

```python
import jax
import jax.numpy as jnp
from jax import lax

MODEL_WIDTH = 3072
QUERY_HEADS = 24
KEY_VALUE_HEADS = 8
HEAD_SIZE = 128
FF = 8192
CAP = 2048
TOKENS = 16384
N_DP = 8


def packing(key):
    count_key = jax.random.fold_in(key, 11)
    cut_key = jax.random.fold_in(key, 12)
    pick_key = jax.random.fold_in(key, 13)
    group_index = jnp.arange(N_DP, dtype=jnp.int32)
    live_counts = jax.random.randint(count_key, (N_DP,), 3 * CAP // 4, CAP + 1)
    chosen = jax.random.randint(pick_key, (), 0, N_DP).astype(jnp.int32)
    other = (chosen + 1) % N_DP
    live_counts = jnp.where(group_index == other, 3 * CAP // 4, live_counts)
    live_counts = jnp.where(group_index == chosen, CAP, live_counts).astype(jnp.int32)
    cut_points = jax.random.randint(cut_key, (N_DP, 2), 1, live_counts[:, None]).astype(jnp.int32)
    cut_points = jnp.where((group_index == chosen)[:, None], CAP - 1, cut_points).astype(jnp.int32)
    lower_cut = jnp.minimum(cut_points[:, 0], cut_points[:, 1])[:, None]
    upper_cut = jnp.maximum(cut_points[:, 0], cut_points[:, 1])[:, None]
    row_index = jnp.arange(CAP, dtype=jnp.int32)[None, :]
    past_lower = row_index >= lower_cut
    past_upper = row_index >= upper_cut
    seg_ids = past_lower.astype(jnp.int32) + past_upper.astype(jnp.int32)
    seg_start = jnp.where(past_upper, upper_cut, jnp.where(past_lower, lower_cut, 0))
    place = row_index - seg_start
    return (live_counts, seg_ids.reshape(TOKENS).astype(jnp.int32), place.reshape(TOKENS).astype(jnp.int32))


def draw_counts(key, part):
    return packing(key)[0]


def draw_segments(key, part):
    return packing(key)[1]


def draw_positions(key, part):
    return packing(key)[2]


def levels(own_key, extent, cuts, smallest, largest):
    level, own = 1.0, jax.random.fold_in(own_key, 6)
    for dim, blocks in cuts:
        steps = jnp.exp(jax.random.uniform(jax.random.fold_in(own, dim), (blocks,), jnp.float32, smallest / len(cuts), largest / len(cuts)))
        level = level * jnp.repeat(steps, extent[dim] // blocks).reshape([-1 if axis == dim else 1 for axis in range(len(extent))])
    return level


def gaussian(own_key, shape, deviation, most, shards=(), kind=jnp.bfloat16):
    entries = deviation * jax.random.normal(own_key, shape, jnp.float32)
    if shards:
        entries = entries * levels(own_key, shape, shards, -0.22, 0.18)
    return jnp.clip(entries, -most, most).astype(kind)


def setup_inputs(seed: int = 0) -> dict:
    seeds = jax.random.split(jax.random.key(seed), 15)
    tokens = gaussian(seeds[0], (TOKENS, MODEL_WIDTH), 1.0, 6.0, ((0, 32),))
    cotangent = gaussian(seeds[1], (TOKENS, MODEL_WIDTH), 1.0, 6.0, ((0, 32),))
    segments = draw_segments(jax.random.fold_in(seeds[14], 71), 0)
    positions = draw_positions(jax.random.fold_in(seeds[14], 71), 0)
    counts = draw_counts(jax.random.fold_in(seeds[14], 71), 0)
    query_weight = gaussian(seeds[5], (MODEL_WIDTH, QUERY_HEADS * HEAD_SIZE), MODEL_WIDTH ** -0.5, 0.109375, ((0, 8), (1, 4)))
    key_projection_weight = gaussian(seeds[6], (MODEL_WIDTH, KEY_VALUE_HEADS * HEAD_SIZE), MODEL_WIDTH ** -0.5, 0.109375, ((0, 8), (1, 4)))
    value_projection_weight = gaussian(seeds[7], (MODEL_WIDTH, KEY_VALUE_HEADS * HEAD_SIZE), MODEL_WIDTH ** -0.5, 0.109375, ((0, 8), (1, 4)))
    out_weight = gaussian(seeds[8], (QUERY_HEADS * HEAD_SIZE, MODEL_WIDTH), (max(QUERY_HEADS * HEAD_SIZE * 4 // CAP, 1)) ** -0.5, 2.5, ((0, 4), (1, 8)))
    attn_gain = jnp.clip(1.0 + 0.18 * jax.random.normal(seeds[9], (MODEL_WIDTH,), jnp.float32), 0.099609375, 1.8984375).astype(jnp.bfloat16)
    gate_weight = gaussian(seeds[10], (MODEL_WIDTH, FF), MODEL_WIDTH ** -0.5, 0.109375, ((0, 8), (1, 4)))
    up_weight = gaussian(seeds[11], (MODEL_WIDTH, FF), MODEL_WIDTH ** -0.5, 0.109375, ((0, 8), (1, 4)))
    down_weight = gaussian(seeds[12], (FF, MODEL_WIDTH), FF ** -0.5, 0.0625, ((0, 4), (1, 8)))
    mlp_gain = jnp.clip(1.0 + 0.18 * jax.random.normal(seeds[13], (MODEL_WIDTH,), jnp.float32), 0.099609375, 1.8984375).astype(jnp.bfloat16)
    return dict(tokens=tokens, cotangent=cotangent, segments=segments, positions=positions, counts=counts, query_weight=query_weight, key_projection_weight=key_projection_weight, value_projection_weight=value_projection_weight, out_weight=out_weight, attn_gain=attn_gain, gate_weight=gate_weight, up_weight=up_weight, down_weight=down_weight, mlp_gain=mlp_gain)


EPSILON = 1e-05
ROPE_BASE = 500000.0
MASKED = -1e+30
EXACT_PRECISION = lax.Precision.HIGHEST

@jax.custom_vjp
def low(v):
    return lax.optimization_barrier(v.astype(jnp.bfloat16)).astype(jnp.float32)

@jax.custom_vjp
def low_back(v):
    return v

def low_keep(v):
    return (low(v), None)

def low_pass(kept, grad):
    return (grad,)

def back_keep(v):
    return (v, None)

def back_low(kept, grad):
    return (low(grad),)
low.defvjp(low_keep, low_pass)
low_back.defvjp(back_keep, back_low)

def rms_norm(source, gain):
    inverse = lax.rsqrt(lax.optimization_barrier(jnp.mean(source * source, axis=-1, keepdims=True)) + EPSILON)
    return source * inverse * gain

def rope_tables(place):
    half_size = HEAD_SIZE // 2
    freqs = ROPE_BASE ** (-(jnp.arange(half_size, dtype=jnp.float32) * 2.0) / HEAD_SIZE)
    angles = place.astype(jnp.float32)[:, None] * freqs[None, :]
    return (jnp.cos(angles)[:, None, :], jnp.sin(angles)[:, None, :])

def apply_rotary(vector, cosine_table, sine_table):
    half_size = vector.shape[-1] // 2
    first = vector[..., :half_size]
    second = vector[..., half_size:]
    return jnp.concatenate([first * cosine_table - second * sine_table, second * cosine_table + first * sine_table], axis=-1)

def attention(query_rows, key_rows, value_rows, seg_ids, place, live_rows):
    every_row_count = query_rows.shape[0]
    rows_per_block = 512 if every_row_count % 512 == 0 else every_row_count
    head_groups = QUERY_HEADS // KEY_VALUE_HEADS
    score_scale = HEAD_SIZE ** (-0.5)
    row_index = jnp.arange(every_row_count, dtype=jnp.int32)
    query_block_list = query_rows.reshape(every_row_count // rows_per_block, rows_per_block, KEY_VALUE_HEADS, head_groups, HEAD_SIZE)
    seg_blocks = seg_ids.reshape(-1, rows_per_block)
    place_blocks = place.reshape(-1, rows_per_block)
    index_blocks = row_index.reshape(-1, rows_per_block)

    @jax.checkpoint
    def one_block(items):
        query_blk, seg_blk, place_blk, index_blk = items
        scores = low_back(jnp.einsum('bkgd,nkd->kgbn', query_blk, key_rows, precision=EXACT_PRECISION) * score_scale)
        allowed = (seg_blk[:, None] == seg_ids[None, :]) & (place[None, :] <= place_blk[:, None])
        allowed = allowed & (live_rows[None, :] | (row_index[None, :] == index_blk[:, None]))
        scores = jnp.where(allowed[None, None], scores, MASKED)
        probs = low(jax.nn.softmax(scores, axis=-1))
        block_out = jnp.einsum('kgbn,nkd->bkgd', probs, value_rows, precision=EXACT_PRECISION)
        return block_out.reshape(rows_per_block, QUERY_HEADS * HEAD_SIZE)
    block_outs = lax.map(one_block, (query_block_list, seg_blocks, place_blocks, index_blocks))
    return block_outs.reshape(every_row_count, QUERY_HEADS * HEAD_SIZE)

def group_forward(source, query_weight, key_projection_weight, value_projection_weight, out_weight, attn_gain, gate_weight, up_weight, down_weight, mlp_gain, seg_ids, place, live_count):
    every_row_count = source.shape[0]
    live_rows = jnp.arange(every_row_count, dtype=jnp.int32) < live_count
    first_normalized = low(rms_norm(source, attn_gain))
    cosine_table, sine_table = rope_tables(place)
    query_rows = low(apply_rotary(low_back(jnp.dot(first_normalized, query_weight, precision=EXACT_PRECISION)).reshape(every_row_count, QUERY_HEADS, HEAD_SIZE), cosine_table, sine_table))
    key_rows = low(apply_rotary(low_back(jnp.dot(first_normalized, key_projection_weight, precision=EXACT_PRECISION)).reshape(every_row_count, KEY_VALUE_HEADS, HEAD_SIZE), cosine_table, sine_table))
    value_rows = low(low_back(jnp.dot(first_normalized, value_projection_weight, precision=EXACT_PRECISION))).reshape(every_row_count, KEY_VALUE_HEADS, HEAD_SIZE)
    attended = attention(query_rows, key_rows, value_rows, seg_ids, place, live_rows)
    attended = low(low_back(attended))
    hidden = source + low_back(jnp.dot(attended, out_weight, precision=EXACT_PRECISION))
    normed_two = low(rms_norm(hidden, mlp_gain))
    gate_proj = low_back(jnp.dot(normed_two, gate_weight, precision=EXACT_PRECISION))
    up_proj = low_back(jnp.dot(normed_two, up_weight, precision=EXACT_PRECISION))
    mixed_act = low(jax.nn.silu(gate_proj) * up_proj)
    result = hidden + low_back(jnp.dot(mixed_act, down_weight, precision=EXACT_PRECISION))
    return result * live_rows[:, None].astype(result.dtype)

def reference(tokens, cotangent, segments, positions, counts, query_weight, key_projection_weight, value_projection_weight, out_weight, attn_gain, gate_weight, up_weight, down_weight, mlp_gain):
    weights = tuple((item.astype(jnp.float32) for item in (query_weight, key_projection_weight, value_projection_weight, out_weight, attn_gain, gate_weight, up_weight, down_weight, mlp_gain)))
    sources = tokens.astype(jnp.float32).reshape(N_DP, CAP, MODEL_WIDTH)
    cot_rows = cotangent.astype(jnp.float32).reshape(N_DP, CAP, MODEL_WIDTH)
    seg_rows = segments.reshape(N_DP, CAP)
    place_rows = positions.reshape(N_DP, CAP)

    def one_group(totals, items):
        source, cot_group, seg_ids, place, live_count = items

        def forward(source_in, *weight_list):
            return group_forward(source_in, *weight_list, seg_ids, place, live_count)
        result, pullback = jax.vjp(forward, source, *weights)
        grads = pullback(cot_group)
        totals = tuple((left + right for left, right in zip(totals, grads[1:])))
        return (totals, (result.astype(jnp.bfloat16), grads[0]))
    initial = tuple((jnp.zeros_like(item) for item in weights))
    totals, (outputs, grad_sources) = lax.scan(one_group, initial, (sources, cot_rows, seg_rows, place_rows, counts))
    return (outputs.reshape(TOKENS, MODEL_WIDTH), grad_sources.reshape(TOKENS, MODEL_WIDTH), totals[0], totals[1], totals[2], totals[3], totals[4], totals[5], totals[6], totals[7], totals[8])
```

```python
import functools
import math

import jax
import jax.numpy as jnp
import numpy as np
from jax import lax
from jax.experimental import pallas as pl
from jax.experimental.pallas import tpu as pltpu
from jax.sharding import PartitionSpec as P

HEAD_SIZE = 128
EPSILON = 1e-05
ROPE_BASE = 500000.0
MASKED = -1e30
F32 = jnp.float32
BF16 = jnp.bfloat16
NT = (((1,), (1,)), ((), ()))
NN = (((1,), (0,)), ((), ()))
TN = (((0,), (0,)), ((), ()))


def dot(a, b, dims, out=F32):
    return lax.dot_general(a, b, dims, preferred_element_type=F32).astype(out)


def after(value, *others):
    return lax.optimization_barrier((value, *others))[0]


def arrival_order(n):
    return [
        [s for d in range(1, n) for s in (i - d, i + d) if 0 <= s < n]
        for i in range(n)
    ]


def pick(place, choices):
    distinct = []
    for value in choices:
        if not any(value is other for other in distinct):
            distinct.append(value)
    out = distinct[0]
    for value in distinct[1:]:
        here = functools.reduce(
            jnp.logical_or, [place == i for i, c in enumerate(choices) if c is value]
        )
        out = jnp.where(here, value, out)
    return out


def travel(items, work=lambda: ()):
    arrays = lax.optimization_barrier(tuple(array for array, _ in items))
    moved = [lax.ppermute(array, "tensor", pairs) for array, (_, pairs) in zip(arrays, items)]
    out = lax.optimization_barrier((*moved, *work()))
    return list(out[: len(moved)])


def line_gather(own, n, use, fill=lambda step: (), along=lambda step: ()):
    place = lax.axis_index("tensor")
    order = arrival_order(n)
    right = left = own
    from_left, from_right = [own], [own]
    slots, used, others = [own], [], []
    for d in range(1, n):

        def work():
            used.append(use(d - 1, slots[d - 1]))
            return (used[-1], *fill(d))

        right, left, *more = travel(
            [
                (right, [(i, i + 1) for i in range(d - 1, n - 1)]),
                (left, [(i + 1, i) for i in range(n - d)]),
                *along(d),
            ],
            work,
        )
        others += more
        from_left.append(right)
        from_right.append(left)
        slots.append(
            pick(
                place,
                [
                    from_left[i - order[i][d - 1]] if order[i][d - 1] < i else from_right[order[i][d - 1] - i]
                    for i in range(n)
                ],
            )
        )
    used.append(use(n - 1, slots[-1]))
    return slots, used, others


def line_reduce(part, n, fill=lambda step, parts: (), along=lambda step: ()):
    place = lax.axis_index("tensor")
    parts = [None] * n
    parts[n - 1] = lax.optimization_barrier(part(n - 1))
    order = [[i] + row for i, row in enumerate(arrival_order(n))]
    right = left = None
    others = []
    for k in range(1, n):
        to_right = pick(
            place,
            [parts[order[i].index(i + n - k)] if i < k else parts[n - k] for i in range(n)],
        )
        to_left = pick(
            place,
            [parts[order[i].index(i - n + k)] if i >= n - k else parts[n - k] for i in range(n)],
        )
        if right is not None:
            to_right = (to_right.astype(F32) + right.astype(F32)).astype(BF16)
            to_left = (to_left.astype(F32) + left.astype(F32)).astype(BF16)

        def work():
            if k == 1:
                for s in range(n - 2, -1, -1):
                    parts[s] = lax.optimization_barrier(part(s))
            return (*fill(k, parts), *(parts[: n - 1] if k == 1 else ()))

        right, left, *more = travel(
            [
                (to_right, [(i, i + 1) for i in range(k)]),
                (to_left, [(n - 1 - i, n - 2 - i) for i in range(k)]),
                *along(k),
            ],
            work,
        )
        others += more
    return parts[0].astype(F32) + (right.astype(F32) + left.astype(F32)), others


def pairs_of(n):
    return [(i, i ^ 1) for i in range(n)]


def attend_forward(n, heads, rows, c, place_ref, *refs):
    chunks = refs[:n]
    cos_ref, sin_ref, qseg_ref, kseg_ref, o_ref, rot_ref, lse_ref, vt, acc, stat = refs[n:]
    hd = HEAD_SIZE
    kc, vc = heads * hd, (heads + 1) * hd
    for s in range(n):
        at = pl.ds(pl.multiple_of(place_ref[s] * rows, rows), rows)
        cos, sin = cos_ref[at, :], sin_ref[at, :]
        for h in range(heads + 1):
            u = chunks[s][:, h * hd : (h + 1) * hd]
            rot_ref[at, h * hd : (h + 1) * hd] = (u * cos + pltpu.roll(u, hd // 2, 1) * sin).astype(BF16)
        v = chunks[s][:, vc : vc + hd]
        rot_ref[at, vc : vc + hd] = v.astype(BF16)
        vt[:, at] = v.T.astype(BF16)

    def block(i, j, diagonal):
        qi = pl.ds(pl.multiple_of(i * rows, rows), rows)
        kj = pl.ds(pl.multiple_of(j * rows, rows), rows)
        k = rot_ref[kj, kc : kc + hd]
        allowed = kseg_ref[kj, :] == qseg_ref[:, qi]
        if diagonal:
            kr = lax.broadcasted_iota(jnp.int32, (rows, rows), 0)
            qr = lax.broadcasted_iota(jnp.int32, (rows, rows), 1)
            allowed = (allowed & (kr < qr)) | (kr == qr)
        for h in range(heads):
            q = rot_ref[qi, h * hd : (h + 1) * hd]
            scores = jnp.where(allowed, dot(k, q, NT) * c, MASKED)
            m = stat[h : h + 1, :]
            top = jnp.maximum(m, jnp.max(scores, axis=0, keepdims=True))
            p = jnp.exp2(scores - top)
            alpha = jnp.exp2(m - top)
            stat[h : h + 1, :] = top
            total = alpha * stat[8 + h : 9 + h, :] + jnp.sum(p, axis=0, keepdims=True)
            stat[8 + h : 9 + h, :] = total
            new = alpha * acc[h] + dot(vt[:, kj], p.astype(BF16), NN)
            if diagonal:
                at = pl.ds(pl.multiple_of(place_ref[n + i] * rows, rows), rows)
                o_ref[at, h * hd : (h + 1) * hd] = (new / total).T.astype(BF16)
                lse_ref[0, h : h + 1, qi] = top + jnp.log2(total)
            else:
                acc[h] = new

    @pl.loop(0, n)
    def _(i):
        stat[0:8, :] = jnp.full((8, rows), MASKED, F32)
        stat[8:16, :] = jnp.zeros((8, rows), F32)
        acc[...] = jnp.zeros_like(acc)

        @pl.loop(0, i)
        def _(j):
            block(i, j, False)

        block(i, i, True)


def attend_backward(n, heads, rows, c, place_ref, *refs):
    gas = refs[:n]
    rot_ref, o_ref, lse_ref, cos_ref, sin_ref, qseg_ref, kseg_ref, d_ref, go, dqt, delta, dk, dv, kt = refs[n:]
    hd = HEAD_SIZE
    scale = hd**-0.5
    kc, vc = heads * hd, (heads + 1) * hd
    for s in range(n):
        at = pl.ds(pl.multiple_of(place_ref[s] * rows, rows), rows)
        for h in range(heads):
            g = gas[s][:, h * hd : (h + 1) * hd]
            o = o_ref[s * rows : (s + 1) * rows, h * hd : (h + 1) * hd]
            go[at, h * hd : (h + 1) * hd] = g
            both = (g.astype(F32) * o.astype(F32)).T
            delta[h : h + 1, at] = jnp.sum(both, axis=0, keepdims=True)
        kt[:, at] = rot_ref[at, kc : kc + hd].astype(F32).T.astype(BF16)
    dqt[...] = jnp.zeros_like(dqt)

    def block(i, j, diagonal):
        qi = pl.ds(pl.multiple_of(i * rows, rows), rows)
        kj = pl.ds(pl.multiple_of(j * rows, rows), rows)
        k = rot_ref[kj, kc : kc + hd]
        v = rot_ref[kj, vc : vc + hd]
        allowed = kseg_ref[kj, :] == qseg_ref[:, qi]
        if diagonal:
            kr = lax.broadcasted_iota(jnp.int32, (rows, rows), 0)
            qr = lax.broadcasted_iota(jnp.int32, (rows, rows), 1)
            allowed = (allowed & (kr < qr)) | (kr == qr)
        for h in range(heads):
            cols = slice(h * hd, (h + 1) * hd)
            q = rot_ref[qi, cols]
            g = go[qi, cols]
            scores = jnp.where(allowed, dot(k, q, NT) * c, MASKED)
            p = jnp.exp2(scores - lse_ref[0, h : h + 1, qi])
            gp = dot(v, g, NT)
            ds = (p * (gp - delta[h : h + 1, qi])).astype(BF16)
            new_v = dot(p.astype(BF16), g, NN)
            new_k = dot(ds, q, NN)
            if diagonal and h == 0:
                dv[...] = new_v
                dk[...] = new_k
            else:
                dv[...] += new_v
                dk[...] += new_k
            dqt[h * hd : (h + 1) * hd, qi] += dot(kt[:, kj], ds, NN)

    def unrotate(u, at):
        return u * cos_ref[at, :] - pltpu.roll(u, hd // 2, 1) * sin_ref[at, :]

    @pl.loop(0, n)
    def _(j):
        block(j, j, True)

        @pl.loop(j + 1, n)
        def _(i):
            block(i, j, False)

        kj = pl.ds(pl.multiple_of(j * rows, rows), rows)
        to = pl.ds(pl.multiple_of(place_ref[n + j] * rows, rows), rows)
        for h in range(heads):
            u = dqt[h * hd : (h + 1) * hd, kj].T * scale
            d_ref[to, h * hd : (h + 1) * hd] = unrotate(u, kj).astype(BF16)
        d_ref[to, kc : kc + hd] = unrotate(dk[...] * scale, kj).astype(BF16)
        d_ref[to, vc : vc + hd] = dv[...].astype(BF16)


def attention_calls(n, rows, heads_q, heads_kv):
    heads = heads_q // heads_kv
    every = n * rows
    wide = (heads + 2) * HEAD_SIZE
    c = HEAD_SIZE**-0.5 * math.log2(math.e)
    whole = lambda shape: pl.BlockSpec(shape, lambda g, place: (0, 0))
    by_head = lambda r, w: pl.BlockSpec((r, w), lambda g, place: (0, g))
    tables = [
        whole((every, HEAD_SIZE)),
        whole((every, HEAD_SIZE)),
        whole((1, every)),
        whole((every, 1)),
    ]
    lse_spec = pl.BlockSpec((1, 8, every), lambda g, place: (g, 0, 0))
    pairs = every * (every + rows) // 2 * heads_q
    params = pltpu.CompilerParams(vmem_limit_bytes=58 << 20)
    forward = pl.pallas_call(
        functools.partial(attend_forward, n, heads, rows, c),
        grid_spec=pltpu.PrefetchScalarGridSpec(
            num_scalar_prefetch=1,
            grid=(heads_kv,),
            in_specs=[by_head(rows, wide)] * n + tables,
            out_specs=[by_head(every, heads * HEAD_SIZE), by_head(every, wide), lse_spec],
            scratch_shapes=[
                pltpu.VMEM((HEAD_SIZE, every), BF16),
                pltpu.VMEM((heads, HEAD_SIZE, rows), F32),
                pltpu.VMEM((16, rows), F32),
            ],
        ),
        out_shape=[
            jax.ShapeDtypeStruct((every, heads_q * HEAD_SIZE), BF16),
            jax.ShapeDtypeStruct((every, heads_kv * wide), BF16),
            jax.ShapeDtypeStruct((heads_kv, 8, every), F32),
        ],
        compiler_params=params,
        cost_estimate=pl.CostEstimate(
            flops=pairs * 4 * HEAD_SIZE, transcendentals=pairs, bytes_accessed=every * heads_kv * wide * 8
        ),
    )
    backward = pl.pallas_call(
        functools.partial(attend_backward, n, heads, rows, c),
        grid_spec=pltpu.PrefetchScalarGridSpec(
            num_scalar_prefetch=1,
            grid=(heads_kv,),
            in_specs=[by_head(rows, heads * HEAD_SIZE)] * n
            + [by_head(every, wide), by_head(every, heads * HEAD_SIZE), lse_spec]
            + tables,
            out_specs=by_head(every, wide),
            scratch_shapes=[
                pltpu.VMEM((every, heads * HEAD_SIZE), BF16),
                pltpu.VMEM((heads * HEAD_SIZE, every), F32),
                pltpu.VMEM((8, every), F32),
                pltpu.VMEM((rows, HEAD_SIZE), F32),
                pltpu.VMEM((rows, HEAD_SIZE), F32),
                pltpu.VMEM((HEAD_SIZE, every), BF16),
            ],
        ),
        out_shape=jax.ShapeDtypeStruct((every, heads_kv * wide), BF16),
        compiler_params=params,
        cost_estimate=pl.CostEstimate(
            flops=pairs * 10 * HEAD_SIZE, transcendentals=pairs, bytes_accessed=every * heads_kv * wide * 10
        ),
    )
    return forward, backward


def gated_kernel(x_ref, gate_ref, up_ref, gm_ref, *refs):
    mixed_ref, dg_ref, du_ref = refs[-3:]
    x = x_ref[...]
    step = 256 if mixed_ref.shape[1] % 256 == 0 else mixed_ref.shape[1]
    for c in range(0, mixed_ref.shape[1], step):
        at = slice(c, c + step)
        gate = dot(x, gate_ref[:, at], NN)
        up = dot(x, up_ref[:, at], NN)
        gm = gm_ref[:, at]
        sig = 1.0 / (1.0 + jnp.exp(-gate))
        act = gate * sig
        mixed_ref[:, at] = (act * up).astype(BF16)
        du_ref[:, at] = (gm * act).astype(BF16)
        dg_ref[:, at] = (gm * up * sig * (1.0 + gate * (1.0 - sig))).astype(BF16)


def gated(x, w_gate, w_up, gm, part, before=None):
    rows, width = x.shape
    hidden = w_gate.shape[1]
    tile = 512 if hidden % 512 == 0 else hidden
    weight = pl.BlockSpec((width, tile), lambda j: (0, j))
    here = pl.BlockSpec((rows, tile), lambda j: (part, j))
    before = () if before is None else tuple(before)
    return pl.pallas_call(
        gated_kernel,
        grid=(hidden // tile,),
        in_specs=[pl.BlockSpec((rows, width), lambda j: (0, 0)), weight, weight, here]
        + [pl.BlockSpec(memory_space=pl.ANY)] * len(before),
        out_specs=[here] * 3,
        out_shape=[jax.ShapeDtypeStruct((2 * rows, hidden), BF16)] * 3,
        input_output_aliases={4 + i: i for i in range(len(before))},
        compiler_params=pltpu.CompilerParams(vmem_limit_bytes=50 << 20),
        cost_estimate=pl.CostEstimate(
            flops=4 * rows * width * hidden,
            transcendentals=rows * hidden,
            bytes_accessed=4 * width * hidden + 2 * rows * width + 10 * rows * hidden,
        ),
    )(x, w_gate, w_up, gm, *before)


def spread_kernel(count, *refs):
    total = None
    for a_ref, w_ref in zip(refs[:count], refs[count : 2 * count]):
        term = lax.dot_general(a_ref[...], w_ref[...], NT, preferred_element_type=F32)
        total = term if total is None else total + term
    refs[-1][...] = total.astype(refs[-1].dtype)


def spread(acts, weights, part, out):
    rows, hidden = acts[0].shape[0] // 2, acts[0].shape[1]
    width = weights[0].shape[0]
    tile = 256 if width % 256 == 0 else width
    count = len(acts)
    return pl.pallas_call(
        functools.partial(spread_kernel, count),
        grid=(width // tile,),
        in_specs=[pl.BlockSpec((rows, hidden), lambda j: (part, 0))] * count
        + [pl.BlockSpec((tile, hidden), lambda j: (j, 0))] * count,
        out_specs=pl.BlockSpec((rows, tile), lambda j: (0, j)),
        out_shape=jax.ShapeDtypeStruct((rows, width), out),
        compiler_params=pltpu.CompilerParams(vmem_limit_bytes=50 << 20),
        cost_estimate=pl.CostEstimate(
            flops=2 * count * rows * width * hidden,
            transcendentals=0,
            bytes_accessed=count * 2 * hidden * (rows + width) + 4 * rows * width,
        ),
    )(*acts, *weights)


def norm_inverse(source):
    return lax.rsqrt(jnp.mean(source * source, axis=-1, keepdims=True) + EPSILON)


def norm_back(grad_normed, source, inverse, gain):
    unit_rows = source * inverse
    gain_term = jnp.sum(grad_normed * unit_rows, axis=0)
    scaled = grad_normed * gain
    grad_source = inverse * (scaled - unit_rows * jnp.mean(scaled * unit_rows, axis=-1, keepdims=True))
    return (grad_source, gain_term)


def shards(
    tokens,
    cotangent,
    segments,
    positions,
    counts,
    query_weight,
    key_projection_weight,
    value_projection_weight,
    out_weight,
    attn_gain,
    gate_weight,
    up_weight,
    down_weight,
    mlp_gain,
):
    n = lax.axis_size("tensor")
    place = lax.axis_index("tensor")
    rows, width = tokens.shape
    every = rows * n
    heads_q = query_weight.shape[1] // HEAD_SIZE
    heads_kv = key_projection_weight.shape[1] // HEAD_SIZE
    heads = heads_q // heads_kv
    qw, hd = heads * HEAD_SIZE, HEAD_SIZE
    wide = qw + 2 * hd
    slices = n // 2

    def gather(shard):
        return lax.all_gather(shard, "dp", axis=0, tiled=True)

    own_qkv = jnp.concatenate(
        [
            part
            for g in range(heads_kv)
            for part in (
                query_weight[:, g * qw : (g + 1) * qw],
                key_projection_weight[:, g * hd : (g + 1) * hd],
                value_projection_weight[:, g * hd : (g + 1) * hd],
            )
        ],
        axis=1,
    )
    w_qkv = gather(own_qkv)
    w_out = gather(out_weight.T)
    gains = lax.all_gather(jnp.stack([attn_gain, mlp_gain]), "dp", axis=1, tiled=True).astype(F32)
    gain_one, gain_two = gains[0], gains[1]
    down_t = down_weight.T

    def to_others(shard):
        return [(shard, [((i + 2 * k) % n, i) for i in range(n)]) for k in range(1, slices)]

    def to_owners(sums):
        return [(one, [(i, (i + 2 * k) % n) for i in range(n)]) for k, one in enumerate(sums, 1)]

    w_down = [gather(down_t)]
    w_gate = [gather(gate_weight)]
    w_up = [gather(up_weight)]

    live_count = counts[0]
    own_index = place * rows + jnp.arange(rows, dtype=jnp.int32)
    live = (own_index < live_count).astype(F32)[:, None]
    labels = lax.all_gather(jnp.stack([segments, positions]), "tensor", axis=1, tiled=True)
    seg_all, place_all = labels[0], labels[1]
    index_all = jnp.arange(every, dtype=jnp.int32)
    key_seg = jnp.where(index_all < live_count, seg_all, -1)[:, None]
    query_seg = seg_all[None, :]
    freqs = ROPE_BASE ** (-(jnp.arange(hd // 2, dtype=F32) * 2.0) / hd)
    angles = place_all.astype(F32)[:, None] * freqs[None, :]
    cos, sin = jnp.cos(angles), jnp.sin(angles)
    cos = jnp.concatenate([cos, cos], axis=1)
    sin = jnp.concatenate([-sin, sin], axis=1)
    order = np.array([[i] + row for i, row in enumerate(arrival_order(n))], np.int32)
    where_is = np.argsort(order, axis=1).astype(np.int32)
    slot_table = jnp.asarray(np.concatenate([order, where_is], axis=1))[place]
    attend, attend_back = attention_calls(n, rows, heads_q, heads_kv)
    tables = (cos, sin, query_seg, key_seg)

    source = tokens.astype(F32)
    inv_one = norm_inverse(source)
    normed_one = (source * inv_one * gain_one).astype(BF16)
    grad_result = cotangent.astype(F32) * live
    grad_low = grad_result.astype(BF16)
    slots_one, projected, moved = line_gather(
        after(normed_one, labels),
        n,
        lambda s, shard: dot(shard, w_qkv, NN),
        lambda step: tables if step == 1 else (),
        lambda step: to_others(down_t) if step == n - 1 else (),
    )
    w_down += [gather(shard) for shard in moved]
    projected[n - 1] = after(projected[n - 1], w_out, w_down[0])
    kept = []

    def attention():
        kept.extend(attend(slot_table, *projected, *tables))
        return kept

    gates, lows = lax.optimization_barrier((gate_weight, grad_low, projected[n - 1]))[:2]
    *moved, grad_theirs = travel([*to_others(gates), (lows, pairs_of(n))], attention)
    attended, rotated, lse = kept
    w_gate += [gather(shard) for shard in moved]
    grad_two = jnp.concatenate([grad_low, grad_theirs], axis=0)
    grad_mixed = []

    def while_out(step, parts):
        if step == 1:
            grad_mixed.append(dot(grad_two, w_down[0], NN))
            return (w_gate[0], grad_mixed[0])
        if step == 2:
            grad_mixed.extend(dot(grad_two, w, NN) for w in w_down[1:])
            return (w_up[0], *grad_mixed[1:])
        return ()

    summed, moved = line_reduce(
        lambda s: dot(after(attended, *moved)[s * rows : (s + 1) * rows], w_out, NT, BF16),
        n,
        while_out,
        lambda step: to_others(up_weight) if step == 1 else (),
    )
    w_up += [gather(shard) for shard in moved]
    hidden = source + summed

    inv_two = norm_inverse(hidden)
    normed_two = (hidden * inv_two * gain_two).astype(BF16)
    mine = []

    def own_rows():
        mine.extend(gated(normed_two, g, u, gm, 0) for g, u, gm in zip(w_gate, w_up, grad_mixed))
        return [one[0] for one in mine]

    (two_theirs,) = travel([(normed_two, pairs_of(n))], own_rows)
    both = [
        gated(two_theirs, g, u, gm, 1, before) for g, u, gm, before in zip(w_gate, w_up, grad_mixed, mine)
    ]
    mixed, grad_gate, grad_up = zip(*both)
    two = jnp.concatenate([normed_two, two_theirs], axis=0)
    d_down = [None] * slices
    d_down[1:] = [dot(grad_two, m, TN, BF16) for m in mixed[1:]]
    grads, weights = list(grad_gate + grad_up), w_gate + w_up
    theirs = spread([after(grads[0], *d_down[1:])] + grads[1:], weights, 1, BF16)
    ours, d_up, d_gate = [], [None] * slices, [None] * slices

    def own_sums():
        ours.append(spread(grads, weights, 0, F32))
        d_up[1:] = [dot(two, g, TN, BF16) for g in grad_up[1:]]
        return (ours[0], *d_up[1:])

    (from_theirs,) = travel([(theirs, pairs_of(n))], own_sums)
    grad_normed_two = ours[0] + from_theirs.astype(F32)
    grad_hidden_norm, gain_two_term = norm_back(grad_normed_two, hidden, inv_two, gain_two)
    grad_hidden = grad_result + grad_hidden_norm

    def owner_sum(partial):
        return lax.psum_scatter(partial, "dp", scatter_dimension=0, tiled=True)

    results = []

    def while_gather(step):
        if step == 1:
            d_gate[1:] = [dot(two, g, TN, BF16) for g in grad_gate[1:]]
            d_down[0] = dot(grad_two, mixed[0], TN, BF16)
            return (*d_gate[1:], d_down[0])
        if step == 2:
            d_up[0] = dot(two, grad_up[0], TN, BF16)
            d_gate[0] = dot(two, grad_gate[0], TN, BF16)
            return (d_up[0], d_gate[0])
        results.extend((spread(mixed, w_down, 1, BF16), spread(mixed, w_down, 0, F32)))
        return results

    sums_down = [owner_sum(d) for d in d_down[1:]]
    slots_back, grad_attended, back_down = line_gather(
        grad_hidden.astype(BF16),
        n,
        lambda s, shard: dot(shard, w_out, NN, BF16),
        while_gather,
        lambda step: to_owners(sums_down) if step == n - 1 else (),
    )
    kept = []

    def attention_back():
        kept.append(attend_back(slot_table, *grad_attended, rotated, attended, lse, *tables))
        return kept

    (from_partner,) = travel([(after(results[0], grad_attended[n - 1]), pairs_of(n))], attention_back)
    grad_qkv = kept[0]
    result = hidden + (results[1] + from_partner.astype(F32))
    output = (result * live).astype(BF16)
    d_qkv = dot(jnp.concatenate(slots_one, axis=0), grad_qkv, TN, BF16)
    d_out = dot(jnp.concatenate(slots_back, axis=0), after(attended, grad_qkv), TN, BF16)
    gain_terms = []

    def while_reduce(step, parts):
        if step == 1:
            return (d_qkv, d_out)
        if step == 2:
            gain_one_term = sum(
                jnp.sum(one.astype(F32) * part.astype(F32), axis=0) for one, part in zip(slots_one, parts)
            )
            gain_terms.append(jnp.stack([gain_one_term / gain_one, gain_two_term]))
            return (gain_terms[0], output)
        return ()

    sums_up = [owner_sum(d) for d in d_up[1:]]
    sums_gate = [owner_sum(d) for d in d_gate[1:]]
    grad_normed_one, back_up = line_reduce(
        lambda s: dot(after(grad_qkv, from_partner)[s * rows : (s + 1) * rows], w_qkv, NT, BF16),
        n,
        while_reduce,
        lambda step: to_owners(sums_up) if step == 1 else (),
    )
    back_gate = travel(to_owners([after(one, grad_normed_one) for one in sums_gate]))

    def whole(first, back):
        return sum((one.astype(F32) for one in back), owner_sum(first).astype(F32))

    grad_down_w = whole(d_down[0], back_down).T
    grad_up_w = whole(d_up[0], back_up)
    grad_gate_w = whole(d_gate[0], back_gate)
    grad_out_w = owner_sum(d_out).astype(F32).T
    grad_qkv_w = owner_sum(d_qkv).astype(F32)
    grad_input_norm, _ = norm_back(grad_normed_one, source, inv_one, gain_one)
    grad_tokens = grad_hidden + grad_input_norm
    gain_sums = lax.psum(after(gain_terms[0], *back_gate), ("dp", "tensor"))
    owned = attn_gain.shape[0]
    gain_own = lax.dynamic_slice_in_dim(gain_sums, lax.axis_index("dp") * owned, owned, 1)

    def columns(offset, size):
        return jnp.concatenate(
            [grad_qkv_w[:, g * wide + offset : g * wide + offset + size] for g in range(heads_kv)], axis=1
        )

    return (
        output,
        grad_tokens,
        columns(0, qw),
        columns(qw, hd),
        columns(qw + hd, hd),
        grad_out_w,
        gain_own[0],
        grad_gate_w,
        grad_up_w,
        grad_down_w,
        gain_own[1],
    )


def solution(mesh):
    rows = P(("dp", "tensor"), None)
    row = P(("dp", "tensor"))
    down_cols = P("tensor", "dp")
    cols = P("dp", "tensor")
    return jax.shard_map(
        shards,
        mesh=mesh,
        in_specs=(rows, rows, row, row, P("dp"), cols, cols, cols, down_cols, P("dp"), cols, cols, down_cols, P("dp")),
        out_specs=(rows, rows, cols, cols, cols, down_cols, P("dp"), cols, cols, down_cols, P("dp")),
        check_vma=False,
    )
```

```python
import functools
import math

import jax
import jax.numpy as jnp
import numpy as np
from jax import lax
from jax.experimental import pallas as pl
from jax.experimental.pallas import tpu as pltpu
from jax.sharding import PartitionSpec as P

HEAD_SIZE = 128
EPSILON = 1e-05
ROPE_BASE = 500000.0
MASKED = -1e30
F32 = jnp.float32
BF16 = jnp.bfloat16
NT = (((1,), (1,)), ((), ()))
NN = (((1,), (0,)), ((), ()))
TN = (((0,), (0,)), ((), ()))
HIDES = pl.CostEstimate(flops=1, transcendentals=0, bytes_accessed=1)


def dot(a, b, dims, out=F32):
    return lax.dot_general(a, b, dims, preferred_element_type=F32).astype(out)


def after(value, *others):
    return lax.optimization_barrier((value, *others))[0]


def arrival_order(n):
    return [
        [s for d in range(1, n) for s in (i - d, i + d) if 0 <= s < n]
        for i in range(n)
    ]


def pick(place, choices):
    distinct = []
    for value in choices:
        if not any(value is other for other in distinct):
            distinct.append(value)
    out = distinct[0]
    for value in distinct[1:]:
        here = functools.reduce(
            jnp.logical_or, [place == i for i, c in enumerate(choices) if c is value]
        )
        out = jnp.where(here, value, out)
    return out


def travel(items, work=lambda gate: ()):
    arrays = lax.optimization_barrier(tuple(array for array, _ in items))
    moved = [lax.ppermute(array, "tensor", pairs) for array, (_, pairs) in zip(arrays, items)]
    out = lax.optimization_barrier((*moved, *work(arrays[0])))
    return list(out[: len(moved)]), list(out[len(moved) :])


def line_gather(own, n, use, fill=lambda step, gate: (), along=lambda step: (), took=lambda step, arrived, filled: None):
    place = lax.axis_index("tensor")
    order = arrival_order(n)
    right = left = own
    from_left, from_right = [own], [own]
    slots, used = [own], []
    for d in range(1, n):

        def work(gate):
            return (use(d - 1, slots[d - 1]), *fill(d, gate))

        (right, left, *more), (result, *filled) = travel(
            [
                (right, [(i, i + 1) for i in range(d - 1, n - 1)]),
                (left, [(i + 1, i) for i in range(n - d)]),
                *along(d),
            ],
            work,
        )
        used.append(result)
        took(d, more, filled)
        from_left.append(right)
        from_right.append(left)
        slots.append(
            pick(
                place,
                [
                    from_left[i - order[i][d - 1]] if order[i][d - 1] < i else from_right[order[i][d - 1] - i]
                    for i in range(n)
                ],
            )
        )
    used.append(use(n - 1, slots[-1]))
    return slots, used


def line_reduce(part, n, fill=lambda step, gate: (), along=lambda step: (), took=lambda step, arrived, filled: None):
    place = lax.axis_index("tensor")
    parts = [None] * n
    parts[n - 1] = lax.optimization_barrier(part(n - 1))
    order = [[i] + row for i, row in enumerate(arrival_order(n))]
    right = left = None

    def add(value, *sums):
        if right is None:
            return value
        return (value.astype(F32) + sum(one.astype(F32) for one in sums)).astype(BF16)

    for k in range(1, n):
        rightward = [parts[order[i].index(i + n - k)] if i < k else parts[n - k] for i in range(n)]
        leftward = [parts[order[i].index(i - n + k)] if i >= n - k else parts[n - k] for i in range(n)]
        if 2 * k <= n:
            choice = [r if i < k else l for i, (r, l) in enumerate(zip(rightward, leftward))]
            to_right = to_left = add(pick(place, choice), right, left)
        else:
            to_right, to_left = add(pick(place, rightward), right), add(pick(place, leftward), left)

        coming = list(range(n - 2, 0, -1)) if k == 1 else []
        if k == n - 1:
            coming.append(0)

        def work(gate):
            return (*(part(s) for s in coming), *fill(k, gate))

        (right, left, *more), worked = travel(
            [
                (to_right, [(i, i + 1) for i in range(k)]),
                (to_left, [(n - 1 - i, n - 2 - i) for i in range(k)]),
                *along(k),
            ],
            work,
        )
        for s, one in zip(coming, worked):
            parts[s] = one
        took(k, more, worked[len(coming) :])
    return parts[0].astype(F32) + (right.astype(F32) + left.astype(F32))


def halves(n, pairs):
    ends = [(a, b) for a, b in pairs if a < n // 4 or a >= n - n // 4]
    return ends, [pair for pair in pairs if pair not in ends]


def joined(first, second):
    return first + second


def attend_forward(n, heads, rows, c, place_ref, *refs):
    chunks = refs[:n]
    cos_ref, sin_ref, qseg_ref, kseg_ref, o_ref, rot_ref, lse_ref, vt, acc, stat = refs[n:]
    hd = HEAD_SIZE
    kc, vc = heads * hd, (heads + 1) * hd
    for s in range(n):
        at = pl.ds(pl.multiple_of(place_ref[s] * rows, rows), rows)
        cos, sin = cos_ref[at, :], sin_ref[at, :]
        for h in range(heads + 1):
            u = chunks[s][:, h * hd : (h + 1) * hd]
            rot_ref[at, h * hd : (h + 1) * hd] = (u * cos + pltpu.roll(u, hd // 2, 1) * sin).astype(BF16)
        v = chunks[s][:, vc : vc + hd]
        rot_ref[at, vc : vc + hd] = v.astype(BF16)
        vt[:, at] = v.T.astype(BF16)

    def block(i, j, diagonal):
        qi = pl.ds(pl.multiple_of(i * rows, rows), rows)
        kj = pl.ds(pl.multiple_of(j * rows, rows), rows)
        k = rot_ref[kj, kc : kc + hd]
        allowed = kseg_ref[kj, :] == qseg_ref[:, qi]
        if diagonal:
            kr = lax.broadcasted_iota(jnp.int32, (rows, rows), 0)
            qr = lax.broadcasted_iota(jnp.int32, (rows, rows), 1)
            allowed = (allowed & (kr < qr)) | (kr == qr)
        for h in range(heads):
            q = rot_ref[qi, h * hd : (h + 1) * hd]
            scores = jnp.where(allowed, dot(k, q, NT) * c, MASKED)
            m = stat[h : h + 1, :]
            top = jnp.maximum(m, jnp.max(scores, axis=0, keepdims=True))
            p = jnp.exp2(scores - top)
            alpha = jnp.exp2(m - top)
            stat[h : h + 1, :] = top
            total = alpha * stat[8 + h : 9 + h, :] + jnp.sum(p, axis=0, keepdims=True)
            stat[8 + h : 9 + h, :] = total
            new = alpha * acc[h] + dot(vt[:, kj], p.astype(BF16), NN)
            if diagonal:
                at = pl.ds(pl.multiple_of(place_ref[n + i] * rows, rows), rows)
                o_ref[at, h * hd : (h + 1) * hd] = (new / total).T.astype(BF16)
                lse_ref[0, h : h + 1, qi] = top + jnp.log2(total)
            else:
                acc[h] = new

    @pl.loop(0, n)
    def _(i):
        stat[0:8, :] = jnp.full((8, rows), MASKED, F32)
        stat[8:16, :] = jnp.zeros((8, rows), F32)
        acc[...] = jnp.zeros_like(acc)

        @pl.loop(0, i)
        def _(j):
            block(i, j, False)

        block(i, i, True)


def attend_backward(n, heads, rows, c, place_ref, *refs):
    gas = refs[:n]
    rot_ref, o_ref, lse_ref, cos_ref, sin_ref, qseg_ref, kseg_ref, d_ref, go, dqt, delta, dk, dv, kt = refs[n:]
    hd = HEAD_SIZE
    scale = hd**-0.5
    kc, vc = heads * hd, (heads + 1) * hd
    for s in range(n):
        at = pl.ds(pl.multiple_of(place_ref[s] * rows, rows), rows)
        for h in range(heads):
            g = gas[s][:, h * hd : (h + 1) * hd]
            o = o_ref[s * rows : (s + 1) * rows, h * hd : (h + 1) * hd]
            go[at, h * hd : (h + 1) * hd] = g
            both = (g.astype(F32) * o.astype(F32)).T
            delta[h : h + 1, at] = jnp.sum(both, axis=0, keepdims=True)
        kt[:, at] = rot_ref[at, kc : kc + hd].astype(F32).T.astype(BF16)
    dqt[...] = jnp.zeros_like(dqt)

    def block(i, j, diagonal):
        qi = pl.ds(pl.multiple_of(i * rows, rows), rows)
        kj = pl.ds(pl.multiple_of(j * rows, rows), rows)
        k = rot_ref[kj, kc : kc + hd]
        v = rot_ref[kj, vc : vc + hd]
        allowed = kseg_ref[kj, :] == qseg_ref[:, qi]
        if diagonal:
            kr = lax.broadcasted_iota(jnp.int32, (rows, rows), 0)
            qr = lax.broadcasted_iota(jnp.int32, (rows, rows), 1)
            allowed = (allowed & (kr < qr)) | (kr == qr)
        for h in range(heads):
            cols = slice(h * hd, (h + 1) * hd)
            q = rot_ref[qi, cols]
            g = go[qi, cols]
            scores = jnp.where(allowed, dot(k, q, NT) * c, MASKED)
            p = jnp.exp2(scores - lse_ref[0, h : h + 1, qi])
            gp = dot(v, g, NT)
            ds = (p * (gp - delta[h : h + 1, qi])).astype(BF16)
            new_v = dot(p.astype(BF16), g, NN)
            new_k = dot(ds, q, NN)
            if diagonal and h == 0:
                dv[...] = new_v
                dk[...] = new_k
            else:
                dv[...] += new_v
                dk[...] += new_k
            dqt[h * hd : (h + 1) * hd, qi] += dot(kt[:, kj], ds, NN)

    def unrotate(u, at):
        return u * cos_ref[at, :] - pltpu.roll(u, hd // 2, 1) * sin_ref[at, :]

    @pl.loop(0, n)
    def _(j):
        block(j, j, True)

        @pl.loop(j + 1, n)
        def _(i):
            block(i, j, False)

        kj = pl.ds(pl.multiple_of(j * rows, rows), rows)
        to = pl.ds(pl.multiple_of(place_ref[n + j] * rows, rows), rows)
        for h in range(heads):
            u = dqt[h * hd : (h + 1) * hd, kj].T * scale
            d_ref[to, h * hd : (h + 1) * hd] = unrotate(u, kj).astype(BF16)
        d_ref[to, kc : kc + hd] = unrotate(dk[...] * scale, kj).astype(BF16)
        d_ref[to, vc : vc + hd] = dv[...].astype(BF16)


def attention_calls(n, rows, heads_q, heads_kv):
    heads = heads_q // heads_kv
    every = n * rows
    wide = (heads + 2) * HEAD_SIZE
    c = HEAD_SIZE**-0.5 * math.log2(math.e)
    whole = lambda shape: pl.BlockSpec(shape, lambda g, place: (0, 0))
    by_head = lambda r, w: pl.BlockSpec((r, w), lambda g, place: (0, g))
    tables = [
        whole((every, HEAD_SIZE)),
        whole((every, HEAD_SIZE)),
        whole((1, every)),
        whole((every, 1)),
    ]
    lse_spec = pl.BlockSpec((1, 8, every), lambda g, place: (g, 0, 0))
    params = pltpu.CompilerParams(vmem_limit_bytes=58 << 20)
    forward = pl.pallas_call(
        functools.partial(attend_forward, n, heads, rows, c),
        grid_spec=pltpu.PrefetchScalarGridSpec(
            num_scalar_prefetch=1,
            grid=(heads_kv,),
            in_specs=[by_head(rows, wide)] * n + tables,
            out_specs=[by_head(every, heads * HEAD_SIZE), by_head(every, wide), lse_spec],
            scratch_shapes=[
                pltpu.VMEM((HEAD_SIZE, every), BF16),
                pltpu.VMEM((heads, HEAD_SIZE, rows), F32),
                pltpu.VMEM((16, rows), F32),
            ],
        ),
        out_shape=[
            jax.ShapeDtypeStruct((every, heads_q * HEAD_SIZE), BF16),
            jax.ShapeDtypeStruct((every, heads_kv * wide), BF16),
            jax.ShapeDtypeStruct((heads_kv, 8, every), F32),
        ],
        compiler_params=params,
        cost_estimate=HIDES,
    )
    backward = pl.pallas_call(
        functools.partial(attend_backward, n, heads, rows, c),
        grid_spec=pltpu.PrefetchScalarGridSpec(
            num_scalar_prefetch=1,
            grid=(heads_kv,),
            in_specs=[by_head(rows, heads * HEAD_SIZE)] * n
            + [by_head(every, wide), by_head(every, heads * HEAD_SIZE), lse_spec]
            + tables,
            out_specs=by_head(every, wide),
            scratch_shapes=[
                pltpu.VMEM((every, heads * HEAD_SIZE), BF16),
                pltpu.VMEM((heads * HEAD_SIZE, every), F32),
                pltpu.VMEM((8, every), F32),
                pltpu.VMEM((rows, HEAD_SIZE), F32),
                pltpu.VMEM((rows, HEAD_SIZE), F32),
                pltpu.VMEM((HEAD_SIZE, every), BF16),
            ],
        ),
        out_shape=jax.ShapeDtypeStruct((every, heads_kv * wide), BF16),
        compiler_params=params,
        cost_estimate=HIDES,
    )
    return forward, backward


def gated_kernel(x_ref, gate_ref, up_ref, gm_ref, *refs):
    mixed_ref, dg_ref, du_ref = refs[-3:]
    x = x_ref[...]
    step = 256 if mixed_ref.shape[1] % 256 == 0 else mixed_ref.shape[1]
    for c in range(0, mixed_ref.shape[1], step):
        at = slice(c, c + step)
        gate = dot(x, gate_ref[:, at], NN)
        up = dot(x, up_ref[:, at], NN)
        gm = gm_ref[:, at]
        sig = 1.0 / (1.0 + jnp.exp(-gate))
        act = gate * sig
        mixed_ref[:, at] = (act * up).astype(BF16)
        du_ref[:, at] = (gm * act).astype(BF16)
        dg_ref[:, at] = (gm * up * sig * (1.0 + gate * (1.0 - sig))).astype(BF16)


def gated(x, w_gate, w_up, gm, part, before=None):
    rows, width = x.shape
    hidden = w_gate.shape[1]
    tile = 512 if hidden % 512 == 0 else hidden
    weight = pl.BlockSpec((width, tile), lambda j: (0, j))
    here = pl.BlockSpec((rows, tile), lambda j: (part, j))
    before = () if before is None else tuple(before)
    return pl.pallas_call(
        gated_kernel,
        grid=(hidden // tile,),
        in_specs=[pl.BlockSpec((rows, width), lambda j: (0, 0)), weight, weight, here]
        + [pl.BlockSpec(memory_space=pl.ANY)] * len(before),
        out_specs=[here] * 3,
        out_shape=[jax.ShapeDtypeStruct((2 * rows, hidden), BF16)] * 3,
        input_output_aliases={4 + i: i for i in range(len(before))},
        compiler_params=pltpu.CompilerParams(vmem_limit_bytes=50 << 20),
        cost_estimate=HIDES,
    )(x, w_gate, w_up, gm, *before)


def spread_kernel(count, *refs):
    total = None
    for a_ref, w_ref in zip(refs[:count], refs[count : 2 * count]):
        term = lax.dot_general(a_ref[...], w_ref[...], NT, preferred_element_type=F32)
        total = term if total is None else total + term
    refs[-1][...] = total.astype(refs[-1].dtype)


def spread(acts, weights, part, out, cost=HIDES):
    rows, hidden = acts[0].shape[0] // 2, acts[0].shape[1]
    width = weights[0].shape[0]
    tile = 256 if width % 256 == 0 else width
    count = len(acts)
    return pl.pallas_call(
        functools.partial(spread_kernel, count),
        grid=(width // tile,),
        in_specs=[pl.BlockSpec((rows, hidden), lambda j: (part, 0))] * count
        + [pl.BlockSpec((tile, hidden), lambda j: (j, 0))] * count,
        out_specs=pl.BlockSpec((rows, tile), lambda j: (0, j)),
        out_shape=jax.ShapeDtypeStruct((rows, width), out),
        compiler_params=pltpu.CompilerParams(vmem_limit_bytes=50 << 20),
        cost_estimate=cost,
    )(*acts, *weights)


def norm_inverse(source):
    return lax.rsqrt(jnp.mean(source * source, axis=-1, keepdims=True) + EPSILON)


def norm_back(grad_normed, source, inverse, gain):
    unit_rows = source * inverse
    scaled = grad_normed * gain
    return inverse * (scaled - unit_rows * jnp.mean(scaled * unit_rows, axis=-1, keepdims=True))


def shards(
    tokens,
    cotangent,
    segments,
    positions,
    counts,
    query_weight,
    key_projection_weight,
    value_projection_weight,
    out_weight,
    attn_gain,
    gate_weight,
    up_weight,
    down_weight,
    mlp_gain,
):
    n = lax.axis_size("tensor")
    place = lax.axis_index("tensor")
    rows, width = tokens.shape
    every = rows * n
    heads_q = query_weight.shape[1] // HEAD_SIZE
    heads_kv = key_projection_weight.shape[1] // HEAD_SIZE
    heads = heads_q // heads_kv
    qw, hd = heads * HEAD_SIZE, HEAD_SIZE
    wide = qw + 2 * hd
    slices = n // 2

    def gather(shard):
        return lax.all_gather(shard, "dp", axis=0, tiled=True)

    own_qkv = jnp.concatenate(
        [
            part
            for g in range(heads_kv)
            for part in (
                query_weight[:, g * qw : (g + 1) * qw],
                key_projection_weight[:, g * hd : (g + 1) * hd],
                value_projection_weight[:, g * hd : (g + 1) * hd],
            )
        ],
        axis=1,
    )
    w_qkv = gather(own_qkv)
    w_out = gather(out_weight.T)
    gains = lax.all_gather(jnp.stack([attn_gain, mlp_gain]), "dp", axis=1, tiled=True).astype(F32)
    gain_one, gain_two = gains[0], gains[1]
    down_t = down_weight.T

    partners = halves(n, [(i, i ^ 1) for i in range(n)])
    outward = [halves(n, [((i + 2 * k) % n, i) for i in range(n)]) for k in range(1, slices)]
    homeward = [halves(n, [(i, (i + 2 * k) % n) for i in range(n)]) for k in range(1, slices)]

    def to_others(shard, half):
        return [(shard, pairs[half]) for pairs in outward]

    def to_owners(sums, half):
        return [(one, pairs[half]) for one, pairs in zip(sums, homeward)]

    w_down = [gather(down_t)]
    w_gate = [gather(gate_weight)]
    w_up = [gather(up_weight)]

    live_count = counts[0]
    own_index = place * rows + jnp.arange(rows, dtype=jnp.int32)
    live = (own_index < live_count).astype(F32)[:, None]
    labels = lax.all_gather(jnp.stack([segments, positions]), "tensor", axis=1, tiled=True)
    seg_all, place_all = labels[0], labels[1]
    index_all = jnp.arange(every, dtype=jnp.int32)
    key_seg = jnp.where(index_all < live_count, seg_all, -1)[:, None]
    query_seg = seg_all[None, :]
    freqs = ROPE_BASE ** (-(jnp.arange(hd // 2, dtype=F32) * 2.0) / hd)
    angles = place_all.astype(F32)[:, None] * freqs[None, :]
    cos, sin = jnp.cos(angles), jnp.sin(angles)
    cos = jnp.concatenate([cos, cos], axis=1)
    sin = jnp.concatenate([-sin, sin], axis=1)
    order = np.array([[i] + row for i, row in enumerate(arrival_order(n))], np.int32)
    where_is = np.argsort(order, axis=1).astype(np.int32)
    slot_table = jnp.asarray(np.concatenate([order, where_is], axis=1))[place]
    attend, attend_back = attention_calls(n, rows, heads_q, heads_kv)
    tables = (cos, sin, query_seg, key_seg)

    source = tokens.astype(F32)
    inv_one = norm_inverse(source)
    normed_one = (source * inv_one * gain_one).astype(BF16)
    grad_result = cotangent.astype(F32) * live
    grad_low = grad_result.astype(BF16)
    more = slices - 1
    early = []
    slots_one, projected = line_gather(
        after(normed_one, labels),
        n,
        lambda s, shard: dot(shard, w_qkv, NN),
        lambda step, gate: tables if step == 1 else (),
        lambda step: {
            n - 2: [(grad_low, partners[0])],
            n - 1: to_others(down_t, 0) + to_others(gate_weight, 0),
        }.get(step, ()),
        lambda step, arrived, filled: early.extend(arrived),
    )
    low_ends, down_ends, gate_ends = early[0], early[1 : 1 + more], early[1 + more :]
    projected[n - 1] = after(projected[n - 1], w_out, w_down[0])

    def attention(gate):
        return attend(slot_table, *projected, *tables)

    downs, ups = lax.optimization_barrier((down_t, up_weight, projected[n - 1]))[:2]
    moved, (attended, rotated, lse) = travel(to_others(downs, 1) + to_others(ups, 0), attention)
    w_down += [gather(joined(a, b)) for a, b in zip(down_ends, moved[:more])]
    up_ends = moved[more:]
    grad_mixed, lows = [], []

    def while_out(step, gate):
        if step == 1:
            return (w_gate[0],)
        if step == n - 1:
            theirs = joined(low_ends, lows[0])
            lows.append(theirs)
            return (w_up[0], *(dot(jnp.concatenate([grad_low, theirs], axis=0), w, NN) for w in w_down))
        return ()

    def along_out(step):
        if step == 1:
            return to_others(gate_weight, 1) + to_others(up_weight, 1)
        if step == 2:
            return [(grad_low, partners[1])]
        return ()

    def took_out(step, arrived, filled):
        if step == 1:
            w_gate.extend(gather(joined(a, b)) for a, b in zip(gate_ends, arrived[:more]))
            w_up.extend(gather(joined(a, b)) for a, b in zip(up_ends, arrived[more:]))
        elif step == n - 1:
            grad_mixed.extend(filled[1:])
        else:
            lows.extend(arrived)

    summed = line_reduce(
        lambda s: dot(attended[s * rows : (s + 1) * rows], w_out, NT, BF16), n, while_out, along_out, took_out
    )
    hidden = source + summed
    grad_two = jnp.concatenate([grad_low, lows[1]], axis=0)

    inv_two = norm_inverse(hidden)
    normed_two = (hidden * inv_two * gain_two).astype(BF16)

    def own_rows(gate):
        return [one for g, u, gm in zip(w_gate, w_up, grad_mixed) for one in gated(gate, g, u, gm, 0)]

    (two_theirs,), mine = travel([(normed_two, partners[0] + partners[1])], own_rows)
    two = jnp.concatenate([normed_two, two_theirs], axis=0)
    mixed, grad_gate, grad_up, d_down = [None] * slices, [None] * slices, [None] * slices, [None] * slices
    rows_in = two_theirs
    for k in range(slices - 1, -1, -1):
        mixed[k], grad_gate[k], grad_up[k] = gated(rows_in, w_gate[k], w_up[k], grad_mixed[k], 1, mine[3 * k : 3 * k + 3])
        if k > 0:
            d_down[k] = dot(grad_two, mixed[k], TN, BF16)
            rows_in = after(two_theirs, d_down[k])
    grads, weights = grad_gate + grad_up, w_gate + w_up
    theirs = spread(grads, weights, 1, BF16)
    d_up, d_gate = [None] * slices, [None] * slices

    def own_sums(gate):
        return (
            spread([after(grads[0], gate)] + grads[1:], weights, 0, F32),
            *(dot(two, after(g, gate), TN, BF16) for g in grad_up[1:]),
        )

    (from_theirs,), (ours, *d_up[1:]) = travel([(theirs, partners[0] + partners[1])], own_sums)
    grad_normed_two = ours + from_theirs.astype(F32)
    grad_hidden_norm = norm_back(grad_normed_two, hidden, inv_two, gain_two)
    grad_hidden = grad_result + grad_hidden_norm

    def owner_sum(partial):
        return lax.psum_scatter(partial, "dp", scatter_dimension=0, tiled=True)

    results, early = [], []

    def d_of(left, right, gate):
        return dot(left, after(right, gate), TN, BF16)

    def result_rows(part, out, gate, cost=HIDES):
        return spread([after(mixed[0], gate), *mixed[1:]], w_down, part, out, cost)

    def while_gather(step, gate):
        if step == 1:
            flops = 2 * rows * width * slices * gate_weight.shape[1]
            cost = pl.CostEstimate(flops=flops, transcendentals=0, bytes_accessed=flops // rows)
            return (result_rows(1, BF16, gate, cost), *(d_of(two, g, gate) for g in grad_gate[1:]))
        if step == 2:
            return (result_rows(0, F32, gate), d_of(grad_two, mixed[0], gate))
        if step == n - 1:
            return (d_of(two, grad_up[0], gate),)
        return ()

    def took_gather(step, arrived, filled):
        early.extend(arrived)
        if step == 1:
            results.append(filled[0])
            d_gate[1:] = filled[1:]
        elif step == 2:
            results.append(filled[0])
            d_down[0] = filled[1]
        elif step == n - 1:
            d_up[0] = filled[0]

    sums = [jnp.concatenate([owner_sum(a), owner_sum(b)], axis=1) for a, b in zip(d_down[1:], d_up[1:])]
    slots_back, grad_attended = line_gather(
        grad_hidden.astype(BF16),
        n,
        lambda s, shard: dot(shard, w_out, NN, BF16),
        while_gather,
        lambda step: {
            2: [(results[0], partners[0])] if results else (),
            n - 1: to_owners(sums, 0),
        }.get(step, ()),
        took_gather,
    )
    result_ends, sum_ends = early[0], early[1:]

    def attention_back(gate):
        return (
            attend_back(slot_table, *grad_attended, rotated, attended, lse, *tables),
            d_of(two, grad_gate[0], gate),
            sum_down,
        )

    sums_gate = [owner_sum(d) for d in d_gate[1:]]
    sum_down, sum_up = owner_sum(d_down[0]), owner_sum(d_up[0])
    leaving = [after(one, grad_attended[n - 1]) for one in sums_gate]
    moved, (grad_qkv, d_gate[0], _) = travel(to_owners(leaving, 0) + to_owners(leaving, 1), attention_back)
    back_gate = [joined(a, b) for a, b in zip(moved[:more], moved[more:])]
    back_down, back_up, outputs, d_own = [], [], [], []
    sum_gate = owner_sum(d_gate[0])

    def while_reduce(step, gate):
        if step == 1:
            return (d_of(jnp.concatenate(slots_one, axis=0), grad_qkv, gate), sum_up)
        if step == 2:
            return (d_of(jnp.concatenate(slots_back, axis=0), attended, gate), sum_gate)
        if step == n - 1:
            from_partner = joined(result_ends, outputs[0])
            result = hidden + (results[1] + after(from_partner, gate).astype(F32))
            return ((result * live).astype(BF16),)
        return ()

    def along_reduce(step):
        if step == 1:
            return to_owners(sums, 1)
        if step == 2:
            return [(results[0], partners[1])]
        return ()

    def took_reduce(step, arrived, filled):
        if step == 1:
            for a, b in zip(sum_ends, arrived):
                back = joined(a, b)
                back_down.append(back[:, : down_t.shape[1]])
                back_up.append(back[:, down_t.shape[1] :])
            d_own.append(filled[0])
        elif step == 2:
            outputs.extend(arrived)
            d_own.append(filled[0])
        elif step == n - 1:
            outputs.append(filled[0])

    grad_normed_one = line_reduce(
        lambda s: dot(grad_qkv[s * rows : (s + 1) * rows], w_qkv, NT, BF16),
        n,
        while_reduce,
        along_reduce,
        took_reduce,
    )
    output = outputs[1]

    def whole(first, back):
        return sum((one.astype(F32) for one in back), first.astype(F32))

    grad_down_w = whole(sum_down, back_down).T
    grad_up_w = whole(sum_up, back_up)
    grad_gate_w = whole(sum_gate, back_gate)
    sum_qkv = owner_sum(d_own[0])
    grad_qkv_w = sum_qkv.astype(F32)
    grad_out_w = owner_sum(after(d_own[1], sum_qkv)).astype(F32).T
    grad_input_norm = norm_back(grad_normed_one, source, inv_one, gain_one)
    grad_tokens = grad_hidden + grad_input_norm

    def along_row(weight, grad):
        return jnp.sum(weight.astype(F32) * grad, axis=1)

    gain_parts = jnp.stack(
        [
            along_row(own_qkv, grad_qkv_w),
            along_row(gate_weight, grad_gate_w) + along_row(up_weight, grad_up_w),
        ]
    )
    gain_own = lax.psum(gain_parts, "tensor") / jnp.stack([attn_gain, mlp_gain]).astype(F32)

    def columns(offset, size):
        return jnp.concatenate(
            [grad_qkv_w[:, g * wide + offset : g * wide + offset + size] for g in range(heads_kv)], axis=1
        )

    return (
        output,
        grad_tokens,
        columns(0, qw),
        columns(qw, hd),
        columns(qw + hd, hd),
        grad_out_w,
        gain_own[0],
        grad_gate_w,
        grad_up_w,
        grad_down_w,
        gain_own[1],
    )


def solution(mesh):
    rows = P(("dp", "tensor"), None)
    row = P(("dp", "tensor"))
    down_cols = P("tensor", "dp")
    cols = P("dp", "tensor")
    return jax.shard_map(
        shards,
        mesh=mesh,
        in_specs=(rows, rows, row, row, P("dp"), cols, cols, cols, down_cols, P("dp"), cols, cols, down_cols, P("dp")),
        out_specs=(rows, rows, cols, cols, cols, down_cols, P("dp"), cols, cols, down_cols, P("dp")),
        check_vma=False,
    )
```

```python
import functools
import math

import jax
import jax.numpy as jnp
import numpy as np
from jax import lax
from jax.experimental import pallas as pl
from jax.experimental.pallas import tpu as pltpu
from jax.sharding import PartitionSpec as P

HEAD_SIZE = 128
EPSILON = 1e-05
ROPE_BASE = 500000.0
MASKED = -1e30
F32 = jnp.float32
BF16 = jnp.bfloat16
NT = (((1,), (1,)), ((), ()))
NN = (((1,), (0,)), ((), ()))
TN = (((0,), (0,)), ((), ()))
HIDES = pl.CostEstimate(flops=1, transcendentals=0, bytes_accessed=1)


def dot(a, b, dims, out=F32):
    return lax.dot_general(a, b, dims, preferred_element_type=F32).astype(out)


def after(value, *others):
    return lax.optimization_barrier((value, *others))[0]


def arrival_order(n):
    return [
        [s for d in range(1, n) for s in (i - d, i + d) if 0 <= s < n]
        for i in range(n)
    ]


def pick(place, choices):
    distinct = []
    for value in choices:
        if not any(value is other for other in distinct):
            distinct.append(value)
    out = distinct[0]
    for value in distinct[1:]:
        here = functools.reduce(
            jnp.logical_or, [place == i for i, c in enumerate(choices) if c is value]
        )
        out = jnp.where(here, value, out)
    return out


def travel(items, work=lambda gate: ()):
    arrays = lax.optimization_barrier(tuple(array for array, _ in items))
    moved = [lax.ppermute(array, "tensor", pairs) for array, (_, pairs) in zip(arrays, items)]
    out = lax.optimization_barrier((*moved, *work(arrays[0])))
    return list(out[: len(moved)]), list(out[len(moved) :])


def line_gather(own, n, use, fill=lambda step, gate: (), along=lambda step: (), took=lambda step, arrived, filled: None):
    place = lax.axis_index("tensor")
    order = arrival_order(n)
    right = left = own
    from_left, from_right = [own], [own]
    slots, used = [own], []
    for d in range(1, n):

        def work(gate):
            return (use(d - 1, after(slots[d - 1], gate) if d > 1 else own), *fill(d, gate))

        (right, left, *more), (result, *filled) = travel(
            [
                (right, [(i, i + 1) for i in range(d - 1, n - 1)]),
                (left, [(i + 1, i) for i in range(n - d)]),
                *along(d),
            ],
            work,
        )
        used.append(result)
        took(d, more, filled)
        from_left.append(right)
        from_right.append(left)
        slots.append(
            pick(
                place,
                [
                    from_left[i - order[i][d - 1]] if order[i][d - 1] < i else from_right[order[i][d - 1] - i]
                    for i in range(n)
                ],
            )
        )
    used.append(use(n - 1, slots[-1]))
    return slots, used


def line_reduce(part, n, fill=lambda step, gate: (), along=lambda step: (), took=lambda step, arrived, filled: None):
    place = lax.axis_index("tensor")
    parts = [None] * n
    parts[n - 1] = lax.optimization_barrier(part(n - 1))
    order = [[i] + row for i, row in enumerate(arrival_order(n))]
    right = left = None

    def sent(k):
        ways = [order[i].index(i + n - k) for i in range(k)] + [order[i].index(i - n + k) for i in range(n - k, n)]
        return sorted(set(ways), reverse=True)

    def add(value, *sums):
        if right is None:
            return value
        return (value.astype(F32) + sum(one.astype(F32) for one in sums)).astype(BF16)

    for k in range(1, n):
        rightward = [parts[order[i].index(i + n - k)] if i < k else parts[n - k] for i in range(n)]
        leftward = [parts[order[i].index(i - n + k)] if i >= n - k else parts[n - k] for i in range(n)]
        if 2 * k <= n:
            choice = [r if i < k else l for i, (r, l) in enumerate(zip(rightward, leftward))]
            to_right = to_left = add(pick(place, choice), right, left)
        else:
            to_right, to_left = add(pick(place, rightward), right), add(pick(place, leftward), left)

        coming = [0] if k == n - 1 else [s for s in sent(k + 1) if parts[s] is None]

        def work(gate):
            return (*(part(s) for s in coming), *fill(k, gate))

        (right, left, *more), worked = travel(
            [
                (to_right, [(i, i + 1) for i in range(k)]),
                (to_left, [(n - 1 - i, n - 2 - i) for i in range(k)]),
                *along(k),
            ],
            work,
        )
        for s, one in zip(coming, worked):
            parts[s] = one
        took(k, more, worked[len(coming) :])
    return parts[0], right, left


def halves(n, pairs):
    ends = [(a, b) for a, b in pairs if a < n // 4 or a >= n - n // 4]
    return ends, [pair for pair in pairs if pair not in ends]


def joined(first, second):
    return first + second


def attend_forward(n, heads, rows, c, place_ref, *refs):
    chunks = refs[:n]
    cos_ref, sin_ref, qseg_ref, kseg_ref, o_ref, rot_ref, lse_ref, vt, acc, stat = refs[n:]
    hd = HEAD_SIZE
    kc, vc = heads * hd, (heads + 1) * hd
    for s in range(n):
        at = pl.ds(pl.multiple_of(place_ref[s] * rows, rows), rows)
        cos, sin = cos_ref[at, :], sin_ref[at, :]
        for h in range(heads + 1):
            u = chunks[s][:, h * hd : (h + 1) * hd]
            rot_ref[at, h * hd : (h + 1) * hd] = (u * cos + pltpu.roll(u, hd // 2, 1) * sin).astype(BF16)
        v = chunks[s][:, vc : vc + hd]
        rot_ref[at, vc : vc + hd] = v.astype(BF16)
        vt[:, at] = v.T.astype(BF16)

    def block(i, j, diagonal):
        qi = pl.ds(pl.multiple_of(i * rows, rows), rows)
        kj = pl.ds(pl.multiple_of(j * rows, rows), rows)
        k = rot_ref[kj, kc : kc + hd]
        allowed = kseg_ref[kj, :] == qseg_ref[:, qi]
        if diagonal:
            kr = lax.broadcasted_iota(jnp.int32, (rows, rows), 0)
            qr = lax.broadcasted_iota(jnp.int32, (rows, rows), 1)
            allowed = (allowed & (kr < qr)) | (kr == qr)
        for h in range(heads):
            q = rot_ref[qi, h * hd : (h + 1) * hd]
            scores = jnp.where(allowed, dot(k, q, NT) * c, MASKED)
            m = stat[h : h + 1, :]
            top = jnp.maximum(m, jnp.max(scores, axis=0, keepdims=True))
            p = jnp.exp2(scores - top)
            alpha = jnp.exp2(m - top)
            stat[h : h + 1, :] = top
            total = alpha * stat[8 + h : 9 + h, :] + jnp.sum(p, axis=0, keepdims=True)
            stat[8 + h : 9 + h, :] = total
            new = alpha * acc[h] + dot(vt[:, kj], p.astype(BF16), NN)
            if diagonal:
                at = pl.ds(pl.multiple_of(place_ref[n + i] * rows, rows), rows)
                o_ref[at, h * hd : (h + 1) * hd] = (new / total).T.astype(BF16)
                lse_ref[0, h : h + 1, qi] = top + jnp.log2(total)
            else:
                acc[h] = new

    @pl.loop(0, n)
    def _(i):
        stat[0:8, :] = jnp.full((8, rows), MASKED, F32)
        stat[8:16, :] = jnp.zeros((8, rows), F32)
        acc[...] = jnp.zeros_like(acc)

        @pl.loop(0, i)
        def _(j):
            block(i, j, False)

        block(i, i, True)


def attend_backward(n, heads, rows, c, place_ref, *refs):
    gas = refs[:n]
    rot_ref, o_ref, lse_ref, cos_ref, sin_ref, qseg_ref, kseg_ref, d_ref, go, dqt, delta, dk, dv, kt = refs[n:]
    hd = HEAD_SIZE
    scale = hd**-0.5
    kc, vc = heads * hd, (heads + 1) * hd
    for s in range(n):
        at = pl.ds(pl.multiple_of(place_ref[s] * rows, rows), rows)
        for h in range(heads):
            g = gas[s][:, h * hd : (h + 1) * hd]
            o = o_ref[s * rows : (s + 1) * rows, h * hd : (h + 1) * hd]
            go[at, h * hd : (h + 1) * hd] = g
            both = (g.astype(F32) * o.astype(F32)).T
            delta[h : h + 1, at] = jnp.sum(both, axis=0, keepdims=True)
        kt[:, at] = rot_ref[at, kc : kc + hd].astype(F32).T.astype(BF16)
    dqt[...] = jnp.zeros_like(dqt)

    def block(i, j, diagonal):
        qi = pl.ds(pl.multiple_of(i * rows, rows), rows)
        kj = pl.ds(pl.multiple_of(j * rows, rows), rows)
        k = rot_ref[kj, kc : kc + hd]
        v = rot_ref[kj, vc : vc + hd]
        allowed = kseg_ref[kj, :] == qseg_ref[:, qi]
        if diagonal:
            kr = lax.broadcasted_iota(jnp.int32, (rows, rows), 0)
            qr = lax.broadcasted_iota(jnp.int32, (rows, rows), 1)
            allowed = (allowed & (kr < qr)) | (kr == qr)
        for h in range(heads):
            cols = slice(h * hd, (h + 1) * hd)
            q = rot_ref[qi, cols]
            g = go[qi, cols]
            scores = jnp.where(allowed, dot(k, q, NT) * c, MASKED)
            p = jnp.exp2(scores - lse_ref[0, h : h + 1, qi])
            gp = dot(v, g, NT)
            ds = (p * (gp - delta[h : h + 1, qi])).astype(BF16)
            new_v = dot(p.astype(BF16), g, NN)
            new_k = dot(ds, q, NN)
            if diagonal and h == 0:
                dv[...] = new_v
                dk[...] = new_k
            else:
                dv[...] += new_v
                dk[...] += new_k
            dqt[h * hd : (h + 1) * hd, qi] += dot(kt[:, kj], ds, NN)

    def unrotate(u, at):
        return u * cos_ref[at, :] - pltpu.roll(u, hd // 2, 1) * sin_ref[at, :]

    @pl.loop(0, n)
    def _(j):
        block(j, j, True)

        @pl.loop(j + 1, n)
        def _(i):
            block(i, j, False)

        kj = pl.ds(pl.multiple_of(j * rows, rows), rows)
        to = pl.ds(pl.multiple_of(place_ref[n + j] * rows, rows), rows)
        for h in range(heads):
            u = dqt[h * hd : (h + 1) * hd, kj].T * scale
            d_ref[to, h * hd : (h + 1) * hd] = unrotate(u, kj).astype(BF16)
        d_ref[to, kc : kc + hd] = unrotate(dk[...] * scale, kj).astype(BF16)
        d_ref[to, vc : vc + hd] = dv[...].astype(BF16)


def attention_calls(n, rows, heads_q, heads_kv):
    heads = heads_q // heads_kv
    every = n * rows
    wide = (heads + 2) * HEAD_SIZE
    c = HEAD_SIZE**-0.5 * math.log2(math.e)
    whole = lambda shape: pl.BlockSpec(shape, lambda g, place: (0, 0))
    by_head = lambda r, w: pl.BlockSpec((r, w), lambda g, place: (0, g))
    tables = [
        whole((every, HEAD_SIZE)),
        whole((every, HEAD_SIZE)),
        whole((1, every)),
        whole((every, 1)),
    ]
    lse_spec = pl.BlockSpec((1, 8, every), lambda g, place: (g, 0, 0))
    pairs = every * every * heads_q
    params = pltpu.CompilerParams(vmem_limit_bytes=58 << 20)
    forward = pl.pallas_call(
        functools.partial(attend_forward, n, heads, rows, c),
        grid_spec=pltpu.PrefetchScalarGridSpec(
            num_scalar_prefetch=1,
            grid=(heads_kv,),
            in_specs=[by_head(rows, wide)] * n + tables,
            out_specs=[by_head(every, heads * HEAD_SIZE), by_head(every, wide), lse_spec],
            scratch_shapes=[
                pltpu.VMEM((HEAD_SIZE, every), BF16),
                pltpu.VMEM((heads, HEAD_SIZE, rows), F32),
                pltpu.VMEM((16, rows), F32),
            ],
        ),
        out_shape=[
            jax.ShapeDtypeStruct((every, heads_q * HEAD_SIZE), BF16),
            jax.ShapeDtypeStruct((every, heads_kv * wide), BF16),
            jax.ShapeDtypeStruct((heads_kv, 8, every), F32),
        ],
        compiler_params=params,
        cost_estimate=HIDES,
    )
    backward = pl.pallas_call(
        functools.partial(attend_backward, n, heads, rows, c),
        grid_spec=pltpu.PrefetchScalarGridSpec(
            num_scalar_prefetch=1,
            grid=(heads_kv,),
            in_specs=[by_head(rows, heads * HEAD_SIZE)] * n
            + [by_head(every, wide), by_head(every, heads * HEAD_SIZE), lse_spec]
            + tables,
            out_specs=by_head(every, wide),
            scratch_shapes=[
                pltpu.VMEM((every, heads * HEAD_SIZE), BF16),
                pltpu.VMEM((heads * HEAD_SIZE, every), F32),
                pltpu.VMEM((8, every), F32),
                pltpu.VMEM((rows, HEAD_SIZE), F32),
                pltpu.VMEM((rows, HEAD_SIZE), F32),
                pltpu.VMEM((HEAD_SIZE, every), BF16),
            ],
        ),
        out_shape=jax.ShapeDtypeStruct((every, heads_kv * wide), BF16),
        compiler_params=params,
        cost_estimate=pl.CostEstimate(flops=pairs * 10 * HEAD_SIZE, transcendentals=pairs, bytes_accessed=every * wide * 20),
    )
    return forward, backward


def gated_kernel(x_ref, gate_ref, up_ref, gm_ref, *refs):
    mixed_ref, dg_ref, du_ref = refs[-3:]
    x = x_ref[...]
    step = 256 if mixed_ref.shape[1] % 256 == 0 else mixed_ref.shape[1]
    for c in range(0, mixed_ref.shape[1], step):
        at = slice(c, c + step)
        gate = dot(x, gate_ref[:, at], NN)
        up = dot(x, up_ref[:, at], NN)
        gm = gm_ref[:, at]
        sig = 1.0 / (1.0 + jnp.exp(-gate))
        act = gate * sig
        mixed_ref[:, at] = (act * up).astype(BF16)
        du_ref[:, at] = (gm * act).astype(BF16)
        dg_ref[:, at] = (gm * up * sig * (1.0 + gate * (1.0 - sig))).astype(BF16)


def gated(x, w_both, gm, part, before=None):
    rows, width = x.shape
    hidden = w_both.shape[1] // 2
    tile = 512 if hidden % 512 == 0 else hidden
    tiles = hidden // tile
    weight = [pl.BlockSpec((width, tile), lambda j: (0, j)), pl.BlockSpec((width, tile), lambda j: (0, j + tiles))]
    here = pl.BlockSpec((rows, tile), lambda j: (part, j))
    before = () if before is None else tuple(before)
    return pl.pallas_call(
        gated_kernel,
        grid=(tiles,),
        in_specs=[pl.BlockSpec((rows, width), lambda j: (0, 0)), *weight, here]
        + [pl.BlockSpec(memory_space=pl.ANY)] * len(before),
        out_specs=[here] * 3,
        out_shape=[jax.ShapeDtypeStruct((2 * rows, hidden), BF16)] * 3,
        input_output_aliases={4 + i: i for i in range(len(before))},
        compiler_params=pltpu.CompilerParams(vmem_limit_bytes=50 << 20),
        cost_estimate=HIDES,
    )(x, w_both, w_both, gm, *before)


def spread_kernel(count, *refs):
    total = None
    for a_ref, w_ref in zip(refs[:count], refs[count : 2 * count]):
        term = lax.dot_general(a_ref[...], w_ref[...], NT, preferred_element_type=F32)
        total = term if total is None else total + term
    refs[-1][...] = total.astype(refs[-1].dtype)


def spread(acts, weights, part, out, cost=HIDES, piece=0, pieces=1):
    rows, hidden = acts[0].shape[0] // 2, acts[0].shape[1]
    width = weights[0][0].shape[0] // pieces
    tile = 256 if width % 256 == 0 else width
    tiles = width // tile
    count = len(acts)

    def column_block(which):
        return pl.BlockSpec((tile, hidden), lambda j: (j + piece * tiles, which))

    return pl.pallas_call(
        functools.partial(spread_kernel, count),
        grid=(tiles,),
        in_specs=[pl.BlockSpec((rows, hidden), lambda j: (part, 0))] * count
        + [column_block(which) for _, which in weights],
        out_specs=pl.BlockSpec((rows, tile), lambda j: (0, j)),
        out_shape=jax.ShapeDtypeStruct((rows, width), out),
        compiler_params=pltpu.CompilerParams(vmem_limit_bytes=50 << 20),
        cost_estimate=cost,
    )(*acts, *[array for array, _ in weights])


def norm_inverse(source):
    return lax.rsqrt(jnp.mean(source * source, axis=-1, keepdims=True) + EPSILON)


def norm_back_kernel(places, masked, gain_ref, source_ref, straight_ref, *refs):
    grads, refs = refs[: len(places)], refs[len(places) :]
    source = source_ref[...].astype(F32)
    width = source.shape[1]
    inverse = lax.rsqrt(jnp.mean(source * source, axis=-1, keepdims=True) + EPSILON)
    pieces = []
    for half in range(2):
        at = slice(half * width // 2, (half + 1) * width // 2)
        terms = [
            ref[:, at] if count == 2 else ref[...]
            for ref, (first, count) in zip(grads, places)
            if first <= half < first + count
        ]
        pieces.append(sum(term.astype(F32) for term in terms))
    scaled = jnp.concatenate(pieces, axis=1) * gain_ref[...]
    unit_rows = source * inverse
    grad = inverse * (scaled - unit_rows * jnp.mean(scaled * unit_rows, axis=-1, keepdims=True))
    straight = straight_ref[...].astype(F32)
    if masked:
        straight = straight * refs[0][...]
    total = straight + grad
    if masked:
        refs[1][...] = total
        refs[2][...] = total.astype(BF16)
    else:
        refs[0][...] = total


def norm_back(grads, source, gain, straight, mask, low):
    rows, width = source.shape
    tile = 64 if rows % 64 == 0 else rows
    block = lambda wide: pl.BlockSpec((tile, wide), lambda i: (i, 0))
    masked = mask is not None
    out_shape = [jax.ShapeDtypeStruct((rows, width), F32)] + [jax.ShapeDtypeStruct((rows, width), BF16)] * low
    return pl.pallas_call(
        functools.partial(norm_back_kernel, [place for _, *place in grads], masked),
        grid=(rows // tile,),
        in_specs=[pl.BlockSpec((1, width), lambda i: (0, 0)), block(width), block(width)]
        + [block(array.shape[1]) for array, _, _ in grads]
        + [block(1)] * masked,
        out_specs=[block(width)] * len(out_shape) if low else block(width),
        out_shape=out_shape if low else out_shape[0],
        compiler_params=pltpu.CompilerParams(vmem_limit_bytes=40 << 20),
        cost_estimate=HIDES,
    )(gain[None, :], source, straight, *[array for array, _, _ in grads], *([mask] if masked else []))


def turn_kernel(x_ref, o_ref):
    o_ref[...] = x_ref[...].astype(F32).T


def turned(array, first, size):
    rows = array.shape[0]
    return pl.pallas_call(
        turn_kernel,
        grid=(size // HEAD_SIZE,),
        in_specs=[pl.BlockSpec((rows, HEAD_SIZE), lambda j: (0, j + first // HEAD_SIZE))],
        out_specs=pl.BlockSpec((HEAD_SIZE, rows), lambda j: (j, 0)),
        out_shape=jax.ShapeDtypeStruct((size, rows), F32),
        cost_estimate=HIDES,
    )(array)


def shards(
    tokens,
    cotangent,
    segments,
    positions,
    counts,
    query_weight,
    key_projection_weight,
    value_projection_weight,
    out_weight,
    attn_gain,
    gate_weight,
    up_weight,
    down_weight,
    mlp_gain,
):
    n = lax.axis_size("tensor")
    place = lax.axis_index("tensor")
    rows, width = tokens.shape
    every = rows * n
    heads_q = query_weight.shape[1] // HEAD_SIZE
    heads_kv = key_projection_weight.shape[1] // HEAD_SIZE
    heads = heads_q // heads_kv
    qw, hd = heads * HEAD_SIZE, HEAD_SIZE
    wide = qw + 2 * hd
    slices = n // 2

    def gather(shard):
        return lax.all_gather(shard, "dp", axis=0, tiled=True)

    own_qkv = jnp.concatenate(
        [
            part
            for g in range(heads_kv)
            for part in (
                query_weight[:, g * qw : (g + 1) * qw],
                key_projection_weight[:, g * hd : (g + 1) * hd],
                value_projection_weight[:, g * hd : (g + 1) * hd],
            )
        ],
        axis=1,
    )
    w_qkv = gather(own_qkv)
    w_out = gather(out_weight.T)
    gains = lax.all_gather(jnp.stack([attn_gain, mlp_gain]), "dp", axis=1, tiled=True).astype(F32)
    gain_one, gain_two = gains[0], gains[1]
    down_t = down_weight.T

    partners = halves(n, [(i, i ^ 1) for i in range(n)])
    outward = [halves(n, [((i + 2 * k) % n, i) for i in range(n)]) for k in range(1, slices)]
    homeward = [halves(n, [(i, (i + 2 * k) % n) for i in range(n)]) for k in range(1, slices)]

    def to_others(shard, half):
        return [(shard, pairs[half]) for pairs in outward]

    def to_owners(sums, half):
        return [(one, pairs[half]) for one, pairs in zip(sums, homeward)]

    w_down = [gather(down_t)]
    both_weight = jnp.concatenate([gate_weight, up_weight], axis=1)
    w_both = [gather(both_weight)]

    live_count = counts[0]
    own_index = place * rows + jnp.arange(rows, dtype=jnp.int32)
    live = (own_index < live_count).astype(F32)[:, None]
    labels = lax.all_gather(jnp.stack([segments, positions]), "tensor", axis=1, tiled=True)
    seg_all, place_all = labels[0], labels[1]
    index_all = jnp.arange(every, dtype=jnp.int32)
    key_seg = jnp.where(index_all < live_count, seg_all, -1)[:, None]
    query_seg = seg_all[None, :]
    freqs = ROPE_BASE ** (-(jnp.arange(hd // 2, dtype=F32) * 2.0) / hd)
    angles = place_all.astype(F32)[:, None] * freqs[None, :]
    cos, sin = jnp.cos(angles), jnp.sin(angles)
    cos = jnp.concatenate([cos, cos], axis=1)
    sin = jnp.concatenate([-sin, sin], axis=1)
    order = np.array([[i] + row for i, row in enumerate(arrival_order(n))], np.int32)
    where_is = np.argsort(order, axis=1).astype(np.int32)
    slot_table = jnp.asarray(np.concatenate([order, where_is], axis=1))[place]
    attend, attend_back = attention_calls(n, rows, heads_q, heads_kv)
    tables = (cos, sin, query_seg, key_seg)

    source = tokens.astype(F32)
    inv_one = norm_inverse(source)
    normed_one = (source * inv_one * gain_one).astype(BF16)
    grad_result = cotangent.astype(F32) * live
    grad_low = grad_result.astype(BF16)
    more = slices - 1
    early = []
    slots_one, projected = line_gather(
        after(normed_one, labels),
        n,
        lambda s, shard: dot(shard, w_qkv, NN),
        lambda step, gate: tables if step == 1 else (),
        lambda step: {
            n - 2: [(grad_low, partners[0])],
            n - 1: to_others(both_weight, 0),
        }.get(step, ()),
        lambda step, arrived, filled: early.extend(arrived),
    )
    low_ends, both_ends = early[0], early[1:]
    projected[n - 1] = after(projected[n - 1], w_out, w_down[0])

    def attention(gate):
        return attend(slot_table, *projected, *tables)

    downs = after(down_t, projected[n - 1])
    moved, (attended, rotated, lse) = travel([(downs, a + b) for a, b in outward], attention)
    w_down += [gather(shard) for shard in moved]
    grad_mixed, lows = [], []

    def while_out(step, gate):
        if step == 1:
            return (w_both[0],)
        if step == n - 1:
            theirs = joined(low_ends, lows[0])
            lows.append(theirs)
            return tuple(dot(jnp.concatenate([grad_low, theirs], axis=0), w, NN) for w in w_down)
        return ()

    def along_out(step):
        if step == 1:
            return to_others(both_weight, 1)
        if step == 2:
            return [(grad_low, partners[1])]
        return ()

    def took_out(step, arrived, filled):
        if step == 1:
            w_both.extend(gather(joined(a, b)) for a, b in zip(both_ends, arrived))
        elif step == n - 1:
            grad_mixed.extend(filled)
        else:
            lows.extend(arrived)

    summed = line_reduce(
        lambda s: dot(attended[s * rows : (s + 1) * rows], w_out, NT, BF16), n, while_out, along_out, took_out
    )
    hidden = source + sum(term.astype(F32) for term in summed)
    grad_two = jnp.concatenate([grad_low, lows[1]], axis=0)

    inv_two = norm_inverse(hidden)
    normed_two = (hidden * inv_two * gain_two).astype(BF16)

    def own_rows(gate):
        made = [one for w, gm in zip(w_both, grad_mixed) for one in gated(gate, w, gm, 0)]
        return [spread(made[1::3] + made[2::3], weights, 0, F32), *made]

    swap = partners[0] + partners[1]
    weights = [(w, 0) for w in w_both] + [(w, 1) for w in w_both]
    (two_theirs,), (ours, *mine) = travel([(normed_two, swap)], own_rows)
    two = jnp.concatenate([normed_two, two_theirs], axis=0)
    mixed, grad_gate, grad_up, d_down = [None] * slices, [None] * slices, [None] * slices, [None] * slices
    rows_in = two_theirs
    for k in range(slices - 1, -1, -1):
        mixed[k], grad_gate[k], grad_up[k] = gated(rows_in, w_both[k], grad_mixed[k], 1, mine[3 * k : 3 * k + 3])
        if k > 0:
            d_down[k] = dot(grad_two, mixed[k], TN, BF16)
            rows_in = after(two_theirs, d_down[k])
    grads = grad_gate + grad_up
    d_up, d_gate = [None] * slices, [None] * slices

    def second_half(gate):
        return (
            spread([after(grads[0], gate)] + grads[1:], weights, 1, BF16, HIDES, 1, 2),
            *(dot(two, after(g, gate), TN, BF16) for g in grad_up[1:]),
        )

    def gate_weights(gate):
        return tuple(dot(two, after(g, gate), TN, BF16) for g in grad_gate[1:])

    theirs = spread(grads, weights, 1, BF16, HIDES, 0, 2)
    (from_first,), (theirs, *d_up[1:]) = travel([(theirs, swap)], second_half)
    (from_second,), d_gate[1:] = travel([(theirs, swap)], gate_weights)
    grad_hidden, grad_hidden_low = norm_back(
        [(ours, 0, 2), (from_first, 0, 1), (from_second, 1, 1)], hidden, gain_two, cotangent, live, True
    )

    def owner_sum(partial):
        return lax.psum_scatter(partial, "dp", scatter_dimension=0, tiled=True)

    results, early = [], []

    def d_of(left, right, gate):
        return dot(left, after(right, gate), TN, BF16)

    def result_rows(part, out, gate, cost=HIDES):
        return spread([after(mixed[0], gate), *mixed[1:]], [(w, 0) for w in w_down], part, out, cost)

    def while_gather(step, gate):
        if step == 1:
            flops = 2 * rows * width * slices * gate_weight.shape[1]
            cost = pl.CostEstimate(flops=flops, transcendentals=0, bytes_accessed=flops // rows)
            return (result_rows(1, BF16, gate, cost), d_of(grad_two, mixed[0], gate))
        if step == 2:
            return (result_rows(0, F32, gate), d_of(two, grad_up[0], gate), *joined_sums())
        if step == n - 1:
            return (d_of(two, grad_gate[0], gate),)
        return ()

    def took_gather(step, arrived, filled):
        early.extend(arrived)
        if step == 1:
            results.append(filled[0])
            d_down[0] = filled[1]
        elif step == 2:
            results.append(filled[0])
            d_up[0] = filled[1]
            sums.extend(filled[2:])
        elif step == n - 1:
            d_gate[0] = filled[0]

    sums = []

    def joined_sums():
        return [jnp.concatenate([owner_sum(a), owner_sum(b)], axis=1) for a, b in zip(d_down[1:], d_up[1:])]

    slots_back, grad_attended = line_gather(
        grad_hidden_low,
        n,
        lambda s, shard: dot(shard, w_out, NN, BF16),
        while_gather,
        lambda step: {
            2: [(results[0], partners[0])] if results else (),
            n - 1: to_owners(sums, 0),
        }.get(step, ()),
        took_gather,
    )
    result_ends, sum_ends = early[0], early[1:]

    def attention_back(gate):
        return (
            attend_back(after(slot_table, gate), *grad_attended, rotated, attended, lse, *tables),
            d_of(jnp.concatenate(slots_back, axis=0), attended, gate),
            sum_down,
        )

    sums_gate = [owner_sum(d) for d in d_gate[1:]]
    sum_down, sum_up, sum_gate = owner_sum(d_down[0]), owner_sum(d_up[0]), owner_sum(d_gate[0])
    leaving = [after(one, grad_attended[n - 1]) for one in sums_gate]
    back_gate, (grad_qkv, d_out, _) = travel(
        [(one, a + b) for one, (a, b) in zip(leaving, homeward)], attention_back
    )
    back_down, back_up, outputs, d_attention = [], [], [], []

    def while_reduce(step, gate):
        if step == 1:
            d_qkv = d_of(jnp.concatenate(slots_one, axis=0), grad_qkv, gate)
            return (jnp.concatenate([d_qkv, d_out], axis=1), sum_up)
        if step == 2:
            return (sum_gate,)
        if step == n - 1:
            from_partner = joined(result_ends, outputs[0])
            result = hidden + (results[1] + after(from_partner, gate).astype(F32))
            return ((result * live).astype(BF16),)
        return ()

    def along_reduce(step):
        if step == 1:
            return to_owners(sums, 1)
        if step == 2:
            return [(results[0], partners[1])]
        return ()

    def took_reduce(step, arrived, filled):
        if step == 1:
            for a, b in zip(sum_ends, arrived):
                back = joined(a, b)
                back_down.append(back[:, : down_t.shape[1]])
                back_up.append(back[:, down_t.shape[1] :])
            d_attention.append(filled[0])
        elif step == 2:
            outputs.extend(arrived)
        elif step == n - 1:
            outputs.append(filled[0])

    grad_normed_one = line_reduce(
        lambda s: dot(grad_qkv[s * rows : (s + 1) * rows], w_qkv, NT, BF16),
        n,
        while_reduce,
        along_reduce,
        took_reduce,
    )
    output = outputs[1]

    def whole(first, back):
        return sum((one.astype(F32) for one in back), first.astype(F32))

    all_heads = own_qkv.shape[1]
    grad_down_w = whole(sum_down, back_down).T
    grad_gate_w = whole(sum_gate, back_gate)
    grad_up_w = whole(sum_up, back_up)
    sum_attention = owner_sum(d_attention[0])
    grad_qkv_w = sum_attention[:, :all_heads].astype(F32)
    grad_out_w = turned(sum_attention, all_heads, out_weight.shape[0])
    grad_tokens = norm_back([(term, 0, 2) for term in grad_normed_one], tokens, gain_one, grad_hidden, None, False)

    def along_row(weight, grad):
        return jnp.sum(weight.astype(F32) * grad, axis=1)

    gain_parts = jnp.stack(
        [
            along_row(own_qkv, grad_qkv_w),
            along_row(gate_weight, grad_gate_w) + along_row(up_weight, grad_up_w),
        ]
    )
    gain_own = lax.psum(gain_parts, "tensor") / jnp.stack([attn_gain, mlp_gain]).astype(F32)

    def columns(offset, size):
        return jnp.concatenate(
            [grad_qkv_w[:, g * wide + offset : g * wide + offset + size] for g in range(heads_kv)], axis=1
        )

    return (
        output,
        grad_tokens,
        columns(0, qw),
        columns(qw, hd),
        columns(qw + hd, hd),
        grad_out_w,
        gain_own[0],
        grad_gate_w,
        grad_up_w,
        grad_down_w,
        gain_own[1],
    )


def solution(mesh):
    rows = P(("dp", "tensor"), None)
    row = P(("dp", "tensor"))
    down_cols = P("tensor", "dp")
    cols = P("dp", "tensor")
    return jax.shard_map(
        shards,
        mesh=mesh,
        in_specs=(rows, rows, row, row, P("dp"), cols, cols, cols, down_cols, P("dp"), cols, cols, down_cols, P("dp")),
        out_specs=(rows, rows, cols, cols, cols, down_cols, P("dp"), cols, cols, down_cols, P("dp")),
        check_vma=False,
    )
```

```python
import functools
import math

import jax
import jax.numpy as jnp
import numpy as np
from jax import lax
from jax.experimental import pallas as pl
from jax.experimental.pallas import tpu as pltpu
from jax.sharding import PartitionSpec as P

HEAD_SIZE = 128
EPSILON = 1e-05
ROPE_BASE = 500000.0
MASKED = -1e30
F32 = jnp.float32
BF16 = jnp.bfloat16
NT = (((1,), (1,)), ((), ()))
NN = (((1,), (0,)), ((), ()))
TN = (((0,), (0,)), ((), ()))
HIDES = pl.CostEstimate(flops=1, transcendentals=0, bytes_accessed=1)


def dot(a, b, dims, out=F32):
    return lax.dot_general(a, b, dims, preferred_element_type=F32).astype(out)


def after(value, *others):
    return lax.optimization_barrier((value, *others))[0]


def arrival_order(n):
    return [
        [s for d in range(1, n) for s in (i - d, i + d) if 0 <= s < n]
        for i in range(n)
    ]


def pick(place, choices):
    distinct = []
    for value in choices:
        if not any(value is other for other in distinct):
            distinct.append(value)
    out = distinct[0]
    for value in distinct[1:]:
        here = functools.reduce(
            jnp.logical_or, [place == i for i, c in enumerate(choices) if c is value]
        )
        out = jnp.where(here, value, out)
    return out


def travel(items, work=lambda gate: ()):
    arrays = lax.optimization_barrier(tuple(array for array, _ in items))
    moved = [lax.ppermute(array, "tensor", pairs) for array, (_, pairs) in zip(arrays, items)]
    out = lax.optimization_barrier((*moved, *work(arrays[0])))
    return list(out[: len(moved)]), list(out[len(moved) :])


def line_gather(own, n, use, arrive=lambda shard, gate: shard, fill=lambda step, gate: (), along=lambda step: (), took=lambda step, arrived, filled: None):
    place = lax.axis_index("tensor")
    order = arrival_order(n)
    right = left = own
    from_left, from_right = [own], [own]
    slots, used = [own], []
    for d in range(1, n):

        def work(gate):
            slots[d - 1] = arrive(after(slots[d - 1], gate), gate)
            return (use(d - 1, slots[d - 1]), *fill(d, gate))

        (right, left, *more), (result, *filled) = travel(
            [
                (right, [(i, i + 1) for i in range(d - 1, n - 1)]),
                (left, [(i + 1, i) for i in range(n - d)]),
                *along(d),
            ],
            work,
        )
        used.append(result)
        took(d, more, filled)
        from_left.append(right)
        from_right.append(left)
        slots.append(
            pick(
                place,
                [
                    from_left[i - order[i][d - 1]] if order[i][d - 1] < i else from_right[order[i][d - 1] - i]
                    for i in range(n)
                ],
            )
        )
    slots[-1] = arrive(slots[-1], slots[-1])
    used.append(use(n - 1, slots[-1]))
    return slots, used


def line_reduce(part, n, fill=lambda step, gate: (), along=lambda step: (), took=lambda step, arrived, filled: None):
    place = lax.axis_index("tensor")
    parts = [None] * n
    parts[n - 1] = lax.optimization_barrier(part(n - 1))
    order = [[i] + row for i, row in enumerate(arrival_order(n))]
    right = left = None

    def sent(k):
        ways = [order[i].index(i + n - k) for i in range(k)] + [order[i].index(i - n + k) for i in range(n - k, n)]
        return sorted(set(ways), reverse=True)

    def add(value, *sums):
        if right is None:
            return value
        return (value.astype(F32) + sum(one.astype(F32) for one in sums)).astype(BF16)

    for k in range(1, n):
        rightward = [parts[order[i].index(i + n - k)] if i < k else parts[n - k] for i in range(n)]
        leftward = [parts[order[i].index(i - n + k)] if i >= n - k else parts[n - k] for i in range(n)]
        if 2 * k <= n:
            choice = [r if i < k else l for i, (r, l) in enumerate(zip(rightward, leftward))]
            to_right = to_left = add(pick(place, choice), right, left)
        else:
            to_right, to_left = add(pick(place, rightward), right), add(pick(place, leftward), left)

        coming = [0] if k == n - 1 else [s for s in sent(k + 1) if parts[s] is None]

        def work(gate):
            return (*(part(s) for s in coming), *fill(k, gate))

        (right, left, *more), worked = travel(
            [
                (to_right, [(i, i + 1) for i in range(k)]),
                (to_left, [(n - 1 - i, n - 2 - i) for i in range(k)]),
                *along(k),
            ],
            work,
        )
        for s, one in zip(coming, worked):
            parts[s] = one
        took(k, more, worked[len(coming) :])
    return parts[0], right, left


def halves(n, pairs):
    ends = [(a, b) for a, b in pairs if a < n // 4 or a >= n - n // 4]
    return ends, [pair for pair in pairs if pair not in ends]


def joined(first, second):
    return first + second


def attend_forward(n, heads, rows, c, place_ref, *refs):
    chunks = refs[:n]
    cos_ref, sin_ref, qseg_ref, kseg_ref, o_ref, rot_ref, lse_ref, vt, acc, stat = refs[n:]
    hd = HEAD_SIZE
    kc, vc = heads * hd, (heads + 1) * hd
    for s in range(n):
        at = pl.ds(pl.multiple_of(place_ref[s] * rows, rows), rows)
        cos, sin = cos_ref[at, :], sin_ref[at, :]
        for h in range(heads + 1):
            u = chunks[s][:, h * hd : (h + 1) * hd]
            rot_ref[at, h * hd : (h + 1) * hd] = (u * cos + pltpu.roll(u, hd // 2, 1) * sin).astype(BF16)
        v = chunks[s][:, vc : vc + hd]
        rot_ref[at, vc : vc + hd] = v.astype(BF16)
        vt[:, at] = v.T.astype(BF16)

    def block(i, j, diagonal):
        qi = pl.ds(pl.multiple_of(i * rows, rows), rows)
        kj = pl.ds(pl.multiple_of(j * rows, rows), rows)
        k = rot_ref[kj, kc : kc + hd]
        allowed = kseg_ref[kj, :] == qseg_ref[:, qi]
        if diagonal:
            kr = lax.broadcasted_iota(jnp.int32, (rows, rows), 0)
            qr = lax.broadcasted_iota(jnp.int32, (rows, rows), 1)
            allowed = (allowed & (kr < qr)) | (kr == qr)
        for h in range(heads):
            q = rot_ref[qi, h * hd : (h + 1) * hd]
            scores = jnp.where(allowed, dot(k, q, NT) * c, MASKED)
            m = stat[h : h + 1, :]
            top = jnp.maximum(m, jnp.max(scores, axis=0, keepdims=True))
            p = jnp.exp2(scores - top)
            alpha = jnp.exp2(m - top)
            stat[h : h + 1, :] = top
            total = alpha * stat[8 + h : 9 + h, :] + jnp.sum(p, axis=0, keepdims=True)
            stat[8 + h : 9 + h, :] = total
            new = alpha * acc[h] + dot(vt[:, kj], p.astype(BF16), NN)
            if diagonal:
                at = pl.ds(pl.multiple_of(place_ref[n + i] * rows, rows), rows)
                o_ref[at, h * hd : (h + 1) * hd] = (new / total).T.astype(BF16)
                lse_ref[0, h : h + 1, qi] = top + jnp.log2(total)
            else:
                acc[h] = new

    @pl.loop(0, n)
    def _(i):
        stat[0:8, :] = jnp.full((8, rows), MASKED, F32)
        stat[8:16, :] = jnp.zeros((8, rows), F32)
        acc[...] = jnp.zeros_like(acc)

        @pl.loop(0, i)
        def _(j):
            block(i, j, False)

        block(i, i, True)


def attend_backward(n, heads, rows, c, place_ref, *refs):
    gas = refs[:n]
    rot_ref, o_ref, lse_ref, cos_ref, sin_ref, qseg_ref, kseg_ref, d_ref, go, dqt, delta, dk, dv, kt = refs[n:]
    hd = HEAD_SIZE
    scale = hd**-0.5
    kc, vc = heads * hd, (heads + 1) * hd
    for s in range(n):
        at = pl.ds(pl.multiple_of(place_ref[s] * rows, rows), rows)
        for h in range(heads):
            g = gas[s][:, h * hd : (h + 1) * hd]
            o = o_ref[s * rows : (s + 1) * rows, h * hd : (h + 1) * hd]
            go[at, h * hd : (h + 1) * hd] = g
            both = (g.astype(F32) * o.astype(F32)).T
            delta[h : h + 1, at] = jnp.sum(both, axis=0, keepdims=True)
        kt[:, at] = rot_ref[at, kc : kc + hd].astype(F32).T.astype(BF16)
    dqt[...] = jnp.zeros_like(dqt)

    def block(i, j, diagonal):
        qi = pl.ds(pl.multiple_of(i * rows, rows), rows)
        kj = pl.ds(pl.multiple_of(j * rows, rows), rows)
        k = rot_ref[kj, kc : kc + hd]
        v = rot_ref[kj, vc : vc + hd]
        allowed = kseg_ref[kj, :] == qseg_ref[:, qi]
        if diagonal:
            kr = lax.broadcasted_iota(jnp.int32, (rows, rows), 0)
            qr = lax.broadcasted_iota(jnp.int32, (rows, rows), 1)
            allowed = (allowed & (kr < qr)) | (kr == qr)
        for h in range(heads):
            cols = slice(h * hd, (h + 1) * hd)
            q = rot_ref[qi, cols]
            g = go[qi, cols]
            scores = jnp.where(allowed, dot(k, q, NT) * c, MASKED)
            p = jnp.exp2(scores - lse_ref[0, h : h + 1, qi])
            gp = dot(v, g, NT)
            ds = (p * (gp - delta[h : h + 1, qi])).astype(BF16)
            new_v = dot(p.astype(BF16), g, NN)
            new_k = dot(ds, q, NN)
            if diagonal and h == 0:
                dv[...] = new_v
                dk[...] = new_k
            else:
                dv[...] += new_v
                dk[...] += new_k
            dqt[h * hd : (h + 1) * hd, qi] += dot(kt[:, kj], ds, NN)

    def unrotate(u, at):
        return u * cos_ref[at, :] - pltpu.roll(u, hd // 2, 1) * sin_ref[at, :]

    @pl.loop(0, n)
    def _(j):
        block(j, j, True)

        @pl.loop(j + 1, n)
        def _(i):
            block(i, j, False)

        kj = pl.ds(pl.multiple_of(j * rows, rows), rows)
        to = pl.ds(pl.multiple_of(place_ref[n + j] * rows, rows), rows)
        for h in range(heads):
            u = dqt[h * hd : (h + 1) * hd, kj].T * scale
            d_ref[to, h * hd : (h + 1) * hd] = unrotate(u, kj).astype(BF16)
        d_ref[to, kc : kc + hd] = unrotate(dk[...] * scale, kj).astype(BF16)
        d_ref[to, vc : vc + hd] = dv[...].astype(BF16)


def attention_calls(n, rows, heads_q, heads_kv):
    heads = heads_q // heads_kv
    every = n * rows
    wide = (heads + 2) * HEAD_SIZE
    c = HEAD_SIZE**-0.5 * math.log2(math.e)
    whole = lambda shape: pl.BlockSpec(shape, lambda g, place: (0, 0))
    by_head = lambda r, w: pl.BlockSpec((r, w), lambda g, place: (0, g))
    tables = [
        whole((every, HEAD_SIZE)),
        whole((every, HEAD_SIZE)),
        whole((1, every)),
        whole((every, 1)),
    ]
    lse_spec = pl.BlockSpec((1, 8, every), lambda g, place: (g, 0, 0))
    pairs = every * every * heads_q
    params = pltpu.CompilerParams(vmem_limit_bytes=58 << 20)
    forward = pl.pallas_call(
        functools.partial(attend_forward, n, heads, rows, c),
        grid_spec=pltpu.PrefetchScalarGridSpec(
            num_scalar_prefetch=1,
            grid=(heads_kv,),
            in_specs=[by_head(rows, wide)] * n + tables,
            out_specs=[by_head(every, heads * HEAD_SIZE), by_head(every, wide), lse_spec],
            scratch_shapes=[
                pltpu.VMEM((HEAD_SIZE, every), BF16),
                pltpu.VMEM((heads, HEAD_SIZE, rows), F32),
                pltpu.VMEM((16, rows), F32),
            ],
        ),
        out_shape=[
            jax.ShapeDtypeStruct((every, heads_q * HEAD_SIZE), BF16),
            jax.ShapeDtypeStruct((every, heads_kv * wide), BF16),
            jax.ShapeDtypeStruct((heads_kv, 8, every), F32),
        ],
        compiler_params=params,
        cost_estimate=HIDES,
    )
    backward = pl.pallas_call(
        functools.partial(attend_backward, n, heads, rows, c),
        grid_spec=pltpu.PrefetchScalarGridSpec(
            num_scalar_prefetch=1,
            grid=(heads_kv,),
            in_specs=[by_head(rows, heads * HEAD_SIZE)] * n
            + [by_head(every, wide), by_head(every, heads * HEAD_SIZE), lse_spec]
            + tables,
            out_specs=by_head(every, wide),
            scratch_shapes=[
                pltpu.VMEM((every, heads * HEAD_SIZE), BF16),
                pltpu.VMEM((heads * HEAD_SIZE, every), F32),
                pltpu.VMEM((8, every), F32),
                pltpu.VMEM((rows, HEAD_SIZE), F32),
                pltpu.VMEM((rows, HEAD_SIZE), F32),
                pltpu.VMEM((HEAD_SIZE, every), BF16),
            ],
        ),
        out_shape=jax.ShapeDtypeStruct((every, heads_kv * wide), BF16),
        compiler_params=params,
        cost_estimate=pl.CostEstimate(flops=pairs * 10 * HEAD_SIZE, transcendentals=pairs, bytes_accessed=every * wide * 20),
    )
    return forward, backward


def gated_kernel(x_ref, gate_ref, up_ref, gm_ref, *refs):
    mixed_ref, dg_ref, du_ref = refs[-3:]
    x = x_ref[...]
    step = 256 if mixed_ref.shape[1] % 256 == 0 else mixed_ref.shape[1]
    for c in range(0, mixed_ref.shape[1], step):
        at = slice(c, c + step)
        gate = dot(x, gate_ref[:, at], NN)
        up = dot(x, up_ref[:, at], NN)
        gm = gm_ref[:, at]
        sig = 1.0 / (1.0 + jnp.exp(-gate))
        act = gate * sig
        mixed_ref[:, at] = (act * up).astype(BF16)
        du_ref[:, at] = (gm * act).astype(BF16)
        dg_ref[:, at] = (gm * up * sig * (1.0 + gate * (1.0 - sig))).astype(BF16)


def gated(x, w_both, gm, part, before=None):
    rows, width = x.shape
    hidden = w_both.shape[1] // 2
    tile = 512 if hidden % 512 == 0 else hidden
    tiles = hidden // tile
    weight = [pl.BlockSpec((width, tile), lambda j: (0, j)), pl.BlockSpec((width, tile), lambda j: (0, j + tiles))]
    here = pl.BlockSpec((rows, tile), lambda j: (part, j))
    before = () if before is None else tuple(before)
    return pl.pallas_call(
        gated_kernel,
        grid=(tiles,),
        in_specs=[pl.BlockSpec((rows, width), lambda j: (0, 0)), *weight, here]
        + [pl.BlockSpec(memory_space=pl.ANY)] * len(before),
        out_specs=[here] * 3,
        out_shape=[jax.ShapeDtypeStruct((2 * rows, hidden), BF16)] * 3,
        input_output_aliases={4 + i: i for i in range(len(before))},
        compiler_params=pltpu.CompilerParams(vmem_limit_bytes=50 << 20),
        cost_estimate=HIDES,
    )(x, w_both, w_both, gm, *before)


def spread_kernel(count, *refs):
    total = None
    for a_ref, w_ref in zip(refs[:count], refs[count : 2 * count]):
        term = lax.dot_general(a_ref[...], w_ref[...], NT, preferred_element_type=F32)
        total = term if total is None else total + term
    refs[-1][...] = total.astype(refs[-1].dtype)


def spread(acts, weights, part, out, cost=HIDES, piece=0, pieces=1):
    rows, hidden = acts[0].shape[0] // 2, acts[0].shape[1]
    width = weights[0][0].shape[0] // pieces
    tile = 256 if width % 256 == 0 else width
    tiles = width // tile
    count = len(acts)

    def column_block(which):
        return pl.BlockSpec((tile, hidden), lambda j: (j + piece * tiles, which))

    return pl.pallas_call(
        functools.partial(spread_kernel, count),
        grid=(tiles,),
        in_specs=[pl.BlockSpec((rows, hidden), lambda j: (part, 0))] * count
        + [column_block(which) for _, which in weights],
        out_specs=pl.BlockSpec((rows, tile), lambda j: (0, j)),
        out_shape=jax.ShapeDtypeStruct((rows, width), out),
        compiler_params=pltpu.CompilerParams(vmem_limit_bytes=50 << 20),
        cost_estimate=cost,
    )(*acts, *[array for array, _ in weights])


def norm_inverse(source):
    return lax.rsqrt(jnp.mean(source * source, axis=-1, keepdims=True) + EPSILON)


def norm_back_kernel(places, masked, gain_ref, source_ref, straight_ref, *refs):
    grads, refs = refs[: len(places)], refs[len(places) :]
    source = source_ref[...].astype(F32)
    width = source.shape[1]
    inverse = lax.rsqrt(jnp.mean(source * source, axis=-1, keepdims=True) + EPSILON)
    pieces = []
    for half in range(2):
        at = slice(half * width // 2, (half + 1) * width // 2)
        terms = [
            ref[:, at] if count == 2 else ref[...]
            for ref, (first, count) in zip(grads, places)
            if first <= half < first + count
        ]
        pieces.append(sum(term.astype(F32) for term in terms))
    scaled = jnp.concatenate(pieces, axis=1) * gain_ref[...]
    unit_rows = source * inverse
    grad = inverse * (scaled - unit_rows * jnp.mean(scaled * unit_rows, axis=-1, keepdims=True))
    straight = straight_ref[...].astype(F32)
    if masked:
        straight = straight * refs[0][...]
    total = straight + grad
    if masked:
        refs[1][...] = total
        refs[2][...] = total.astype(BF16)
    else:
        refs[0][...] = total


def norm_back(grads, source, gain, straight, mask, low):
    rows, width = source.shape
    tile = 64 if rows % 64 == 0 else rows
    block = lambda wide: pl.BlockSpec((tile, wide), lambda i: (i, 0))
    masked = mask is not None
    out_shape = [jax.ShapeDtypeStruct((rows, width), F32)] + [jax.ShapeDtypeStruct((rows, width), BF16)] * low
    return pl.pallas_call(
        functools.partial(norm_back_kernel, [place for _, *place in grads], masked),
        grid=(rows // tile,),
        in_specs=[pl.BlockSpec((1, width), lambda i: (0, 0)), block(width), block(width)]
        + [block(array.shape[1]) for array, _, _ in grads]
        + [block(1)] * masked,
        out_specs=[block(width)] * len(out_shape) if low else block(width),
        out_shape=out_shape if low else out_shape[0],
        compiler_params=pltpu.CompilerParams(vmem_limit_bytes=40 << 20),
        cost_estimate=HIDES,
    )(gain[None, :], source, straight, *[array for array, _, _ in grads], *([mask] if masked else []))


def turn_kernel(x_ref, o_ref):
    o_ref[...] = x_ref[...].astype(F32).T


def turned(array, first, size):
    rows = array.shape[0]
    return pl.pallas_call(
        turn_kernel,
        grid=(size // HEAD_SIZE,),
        in_specs=[pl.BlockSpec((rows, HEAD_SIZE), lambda j: (0, j + first // HEAD_SIZE))],
        out_specs=pl.BlockSpec((HEAD_SIZE, rows), lambda j: (j, 0)),
        out_shape=jax.ShapeDtypeStruct((size, rows), F32),
        cost_estimate=HIDES,
    )(array)


def shards(
    tokens,
    cotangent,
    segments,
    positions,
    counts,
    query_weight,
    key_projection_weight,
    value_projection_weight,
    out_weight,
    attn_gain,
    gate_weight,
    up_weight,
    down_weight,
    mlp_gain,
):
    n = lax.axis_size("tensor")
    place = lax.axis_index("tensor")
    rows, width = tokens.shape
    every = rows * n
    heads_q = query_weight.shape[1] // HEAD_SIZE
    heads_kv = key_projection_weight.shape[1] // HEAD_SIZE
    heads = heads_q // heads_kv
    qw, hd = heads * HEAD_SIZE, HEAD_SIZE
    wide = qw + 2 * hd
    slices = n // 2

    def gather(shard):
        return lax.all_gather(shard, "dp", axis=0, tiled=True)

    own_qkv = jnp.concatenate(
        [
            part
            for g in range(heads_kv)
            for part in (
                query_weight[:, g * qw : (g + 1) * qw],
                key_projection_weight[:, g * hd : (g + 1) * hd],
                value_projection_weight[:, g * hd : (g + 1) * hd],
            )
        ],
        axis=1,
    )
    w_qkv = gather(own_qkv)
    w_out = gather(out_weight.T)
    gains = []
    down_t = down_weight.T

    partners = halves(n, [(i, i ^ 1) for i in range(n)])
    outward = [halves(n, [((i + 2 * k) % n, i) for i in range(n)]) for k in range(1, slices)]
    homeward = [halves(n, [(i, (i + 2 * k) % n) for i in range(n)]) for k in range(1, slices)]

    def to_others(shard, half):
        return [(shard, pairs[half]) for pairs in outward]

    def to_owners(sums, half):
        return [(one, pairs[half]) for one, pairs in zip(sums, homeward)]

    w_down = [gather(down_t)]
    both_weight = jnp.concatenate([gate_weight, up_weight], axis=1)
    w_both = [gather(both_weight)]

    live_count = counts[0]
    own_index = place * rows + jnp.arange(rows, dtype=jnp.int32)
    live = (own_index < live_count).astype(F32)[:, None]
    labels = lax.all_gather(jnp.stack([segments, positions]), "tensor", axis=1, tiled=True)
    seg_all, place_all = labels[0], labels[1]
    index_all = jnp.arange(every, dtype=jnp.int32)
    key_seg = jnp.where(index_all < live_count, seg_all, -1)[:, None]
    query_seg = seg_all[None, :]
    freqs = ROPE_BASE ** (-(jnp.arange(hd // 2, dtype=F32) * 2.0) / hd)
    angles = place_all.astype(F32)[:, None] * freqs[None, :]
    cos, sin = jnp.cos(angles), jnp.sin(angles)
    cos = jnp.concatenate([cos, cos], axis=1)
    sin = jnp.concatenate([-sin, sin], axis=1)
    order = np.array([[i] + row for i, row in enumerate(arrival_order(n))], np.int32)
    where_is = np.argsort(order, axis=1).astype(np.int32)
    slot_table = jnp.asarray(np.concatenate([order, where_is], axis=1))[place]
    attend, attend_back = attention_calls(n, rows, heads_q, heads_kv)
    tables = (cos, sin, query_seg, key_seg)

    source = tokens.astype(F32)
    unit_one = (source * norm_inverse(source)).astype(BF16)

    def gained(shard, gate):
        if not gains:
            both = lax.all_gather(after(jnp.stack([attn_gain, mlp_gain]), gate), "dp", axis=1, tiled=True)
            gains.extend(both.astype(F32))
        return (shard.astype(F32) * gains[0]).astype(BF16)

    grad_result = cotangent.astype(F32) * live
    grad_low = grad_result.astype(BF16)
    more = slices - 1
    early = []
    slots_one, projected = line_gather(
        after(unit_one, labels),
        n,
        lambda s, shard: dot(shard, w_qkv, NN),
        gained,
        lambda step, gate: tables if step == 1 else (),
        lambda step: {
            n - 2: [(grad_low, partners[0])],
            n - 1: to_others(both_weight, 0),
        }.get(step, ()),
        lambda step, arrived, filled: early.extend(arrived),
    )
    low_ends, both_ends = early[0], early[1:]
    gain_one, gain_two = gains
    projected[n - 1] = after(projected[n - 1], w_out, w_down[0])

    def attention(gate):
        return attend(slot_table, *projected, *tables)

    downs = after(down_t, projected[n - 1])
    moved, (attended, rotated, lse) = travel([(downs, a + b) for a, b in outward], attention)
    w_down += [gather(shard) for shard in moved]
    grad_mixed, lows, both_rest = [], [], []

    def while_out(step, gate):
        if step == 1:
            return (w_both[0],)
        if step == 2:
            return tuple(joined(a, after(b, gate)) for a, b in zip(both_ends, both_rest))
        if step == n - 1:
            theirs = joined(low_ends, lows[0])
            lows.append(theirs)
            return tuple(dot(jnp.concatenate([grad_low, theirs], axis=0), w, NN) for w in w_down)
        return ()

    def along_out(step):
        if step == 1:
            return to_others(both_weight, 1)
        if step == 2:
            return [(grad_low, partners[1])]
        return ()

    def took_out(step, arrived, filled):
        if step == 1:
            both_rest.extend(arrived)
        elif step == n - 1:
            grad_mixed.extend(filled)
        elif step == 2:
            lows.extend(arrived)
            w_both.extend(gather(shard) for shard in filled)

    summed = line_reduce(
        lambda s: dot(attended[s * rows : (s + 1) * rows], w_out, NT, BF16), n, while_out, along_out, took_out
    )
    hidden = source + sum(term.astype(F32) for term in summed)
    grad_two = jnp.concatenate([grad_low, lows[1]], axis=0)

    inv_two = norm_inverse(hidden)
    normed_two = (hidden * inv_two * gain_two).astype(BF16)

    def own_rows(gate):
        made = [one for w, gm in zip(w_both, grad_mixed) for one in gated(gate, w, gm, 0)]
        return [spread(made[1::3] + made[2::3], weights, 0, F32), *made]

    swap = partners[0] + partners[1]
    weights = [(w, 0) for w in w_both] + [(w, 1) for w in w_both]
    (two_theirs,), (ours, *mine) = travel([(normed_two, swap)], own_rows)
    two = jnp.concatenate([normed_two, two_theirs], axis=0)
    mixed, grad_gate, grad_up, d_down = [None] * slices, [None] * slices, [None] * slices, [None] * slices
    rows_in = two_theirs
    for k in range(slices - 1, -1, -1):
        mixed[k], grad_gate[k], grad_up[k] = gated(rows_in, w_both[k], grad_mixed[k], 1, mine[3 * k : 3 * k + 3])
        if k > 0:
            d_down[k] = dot(grad_two, mixed[k], TN, BF16)
            rows_in = after(two_theirs, d_down[k])
    grads = grad_gate + grad_up
    d_up, d_gate = [None] * slices, [None] * slices

    def second_half(gate):
        return (
            spread([after(grads[0], gate)] + grads[1:], weights, 1, BF16, HIDES, 1, 2),
            *(dot(two, after(g, gate), TN, BF16) for g in grad_up[1:]),
        )

    def gate_weights(gate):
        return tuple(dot(two, after(g, gate), TN, BF16) for g in grad_gate[1:])

    theirs = spread(grads, weights, 1, BF16, HIDES, 0, 2)
    (from_first,), (theirs, *d_up[1:]) = travel([(theirs, swap)], second_half)
    (from_second,), d_gate[1:] = travel([(theirs, swap)], gate_weights)
    grad_hidden, grad_hidden_low = norm_back(
        [(ours, 0, 2), (from_first, 0, 1), (from_second, 1, 1)], hidden, gain_two, cotangent, live, True
    )

    def owner_sum(partial):
        return lax.psum_scatter(partial, "dp", scatter_dimension=0, tiled=True)

    results, early = [], []

    def d_of(left, right, gate):
        return dot(left, after(right, gate), TN, BF16)

    def result_rows(part, out, gate, cost=HIDES):
        return spread([after(mixed[0], gate), *mixed[1:]], [(w, 0) for w in w_down], part, out, cost)

    def while_gather(step, gate):
        if step == 1:
            flops = 2 * rows * width * slices * gate_weight.shape[1]
            cost = pl.CostEstimate(flops=flops, transcendentals=0, bytes_accessed=flops // rows)
            return (result_rows(1, BF16, gate, cost), d_of(grad_two, mixed[0], gate))
        if step == 2:
            return (result_rows(0, F32, gate), d_of(two, grad_up[0], gate), *joined_sums())
        if step == n - 1:
            return (d_of(two, grad_gate[0], gate),)
        return ()

    def took_gather(step, arrived, filled):
        early.extend(arrived)
        if step == 1:
            results.append(filled[0])
            d_down[0] = filled[1]
        elif step == 2:
            results.append(filled[0])
            d_up[0] = filled[1]
            sums.extend(filled[2:])
        elif step == n - 1:
            d_gate[0] = filled[0]

    sums = []

    def joined_sums():
        return [jnp.concatenate([owner_sum(a), owner_sum(b)], axis=1) for a, b in zip(d_down[1:], d_up[1:])]

    slots_back, grad_attended = line_gather(
        grad_hidden_low,
        n,
        lambda s, shard: dot(shard, w_out, NN, BF16),
        lambda shard, gate: shard,
        while_gather,
        lambda step: {
            2: [(results[0], partners[0])] if results else (),
            n - 1: to_owners(sums, 0),
        }.get(step, ()),
        took_gather,
    )
    result_ends, sum_ends = early[0], early[1:]

    def attention_back(gate):
        return (
            attend_back(after(slot_table, gate), *grad_attended, rotated, attended, lse, *tables),
            sum_down,
        )

    sums_gate = [owner_sum(d) for d in d_gate[1:]]
    sum_down, sum_up, sum_gate = owner_sum(d_down[0]), owner_sum(d_up[0]), owner_sum(d_gate[0])
    leaving = [after(one, grad_attended[n - 1]) for one in sums_gate]
    back_gate, (grad_qkv, _) = travel(
        [(one, a + b) for one, (a, b) in zip(leaving, homeward)], attention_back
    )
    back_down, back_up, outputs, d_attention = [], [], [], []

    def while_reduce(step, gate):
        if step == 1:
            d_qkv = d_of(jnp.concatenate(slots_one, axis=0), grad_qkv, gate)
            d_out = d_of(jnp.concatenate(slots_back, axis=0), attended, gate)
            return (jnp.concatenate([d_qkv, d_out], axis=1), sum_up)
        if step == 2:
            return (sum_gate,)
        if step == n - 1:
            from_partner = joined(result_ends, outputs[0])
            result = hidden + (results[1] + after(from_partner, gate).astype(F32))
            return ((result * live).astype(BF16),)
        return ()

    def along_reduce(step):
        if step == 1:
            return to_owners(sums, 1)
        if step == 2:
            return [(results[0], partners[1])]
        return ()

    def took_reduce(step, arrived, filled):
        if step == 1:
            for a, b in zip(sum_ends, arrived):
                back = joined(a, b)
                back_down.append(back[:, : down_t.shape[1]])
                back_up.append(back[:, down_t.shape[1] :])
            d_attention.append(filled[0])
        elif step == 2:
            outputs.extend(arrived)
        elif step == n - 1:
            outputs.append(filled[0])

    grad_normed_one = line_reduce(
        lambda s: dot(grad_qkv[s * rows : (s + 1) * rows], w_qkv, NT, BF16),
        n,
        while_reduce,
        along_reduce,
        took_reduce,
    )
    output = outputs[1]

    def whole(first, back):
        return sum((one.astype(F32) for one in back), first.astype(F32))

    all_heads = own_qkv.shape[1]
    grad_down_w = whole(sum_down, back_down).T
    grad_gate_w = whole(sum_gate, back_gate)
    grad_up_w = whole(sum_up, back_up)
    sum_attention = owner_sum(d_attention[0])
    grad_qkv_w = sum_attention[:, :all_heads].astype(F32)
    grad_out_w = turned(sum_attention, all_heads, out_weight.shape[0])
    grad_tokens = norm_back([(term, 0, 2) for term in grad_normed_one], tokens, gain_one, grad_hidden, None, False)

    def along_row(weight, grad):
        return jnp.sum(weight.astype(F32) * grad, axis=1)

    gain_parts = jnp.stack(
        [
            along_row(own_qkv, grad_qkv_w),
            along_row(gate_weight, grad_gate_w) + along_row(up_weight, grad_up_w),
        ]
    )
    gain_own = lax.psum(gain_parts, "tensor") / jnp.stack([attn_gain, mlp_gain]).astype(F32)

    def columns(offset, size):
        return jnp.concatenate(
            [grad_qkv_w[:, g * wide + offset : g * wide + offset + size] for g in range(heads_kv)], axis=1
        )

    return (
        output,
        grad_tokens,
        columns(0, qw),
        columns(qw, hd),
        columns(qw + hd, hd),
        grad_out_w,
        gain_own[0],
        grad_gate_w,
        grad_up_w,
        grad_down_w,
        gain_own[1],
    )


def solution(mesh):
    rows = P(("dp", "tensor"), None)
    row = P(("dp", "tensor"))
    down_cols = P("tensor", "dp")
    cols = P("dp", "tensor")
    return jax.shard_map(
        shards,
        mesh=mesh,
        in_specs=(rows, rows, row, row, P("dp"), cols, cols, cols, down_cols, P("dp"), cols, cols, down_cols, P("dp")),
        out_specs=(rows, rows, cols, cols, cols, down_cols, P("dp"), cols, cols, down_cols, P("dp")),
        check_vma=False,
    )
```

```python
import functools
import math

import jax
import jax.numpy as jnp
import numpy as np
from jax import lax
from jax.experimental import pallas as pl
from jax.experimental.pallas import tpu as pltpu
from jax.sharding import PartitionSpec as P

HEAD_SIZE = 128
EPSILON = 1e-05
ROPE_BASE = 500000.0
MASKED = -1e30
F32 = jnp.float32
BF16 = jnp.bfloat16
NT = (((1,), (1,)), ((), ()))
NN = (((1,), (0,)), ((), ()))
TN = (((0,), (0,)), ((), ()))
HIDES = pl.CostEstimate(flops=1, transcendentals=0, bytes_accessed=1)


def dot(a, b, dims, out=F32):
    return lax.dot_general(a, b, dims, preferred_element_type=F32).astype(out)


def after(value, *others):
    return lax.optimization_barrier((value, *others))[0]


def arrival_order(n):
    return [
        [s for d in range(1, n) for s in (i - d, i + d) if 0 <= s < n]
        for i in range(n)
    ]


def pick(place, choices):
    distinct = []
    for value in choices:
        if not any(value is other for other in distinct):
            distinct.append(value)
    out = distinct[0]
    for value in distinct[1:]:
        here = functools.reduce(
            jnp.logical_or, [place == i for i, c in enumerate(choices) if c is value]
        )
        out = jnp.where(here, value, out)
    return out


def travel(items, work=lambda gate: ()):
    arrays = lax.optimization_barrier(tuple(array for array, _ in items))
    moved = [lax.ppermute(array, "tensor", pairs) for array, (_, pairs) in zip(arrays, items)]
    out = lax.optimization_barrier((*moved, *work(arrays[0])))
    return list(out[: len(moved)]), list(out[len(moved) :])


def line_gather(own, n, use, fill=lambda step, gate: (), along=lambda step: (), took=lambda step, arrived, filled: None):
    place = lax.axis_index("tensor")
    order = arrival_order(n)
    right = left = own
    from_left, from_right = [own], [own]
    slots, used = [own], []
    for d in range(1, n):

        def work(gate):
            return (use(d - 1, after(slots[d - 1], gate) if d > 1 else own), *fill(d, gate))

        (right, left, *more), (result, *filled) = travel(
            [
                (right, [(i, i + 1) for i in range(d - 1, n - 1)]),
                (left, [(i + 1, i) for i in range(n - d)]),
                *along(d),
            ],
            work,
        )
        used.append(result)
        took(d, more, filled)
        from_left.append(right)
        from_right.append(left)
        slots.append(
            pick(
                place,
                [
                    from_left[i - order[i][d - 1]] if order[i][d - 1] < i else from_right[order[i][d - 1] - i]
                    for i in range(n)
                ],
            )
        )
    used.append(use(n - 1, slots[-1]))
    return slots, used


def line_reduce(part, n, fill=lambda step, gate: (), along=lambda step: (), took=lambda step, arrived, filled: None):
    place = lax.axis_index("tensor")
    parts = [None] * n
    parts[n - 1] = lax.optimization_barrier(part(n - 1))
    order = [[i] + row for i, row in enumerate(arrival_order(n))]
    right = left = None

    def sent(k):
        ways = [order[i].index(i + n - k) for i in range(k)] + [order[i].index(i - n + k) for i in range(n - k, n)]
        return sorted(set(ways), reverse=True)

    def add(value, *sums):
        if right is None:
            return value
        return (value.astype(F32) + sum(one.astype(F32) for one in sums)).astype(BF16)

    for k in range(1, n):
        rightward = [parts[order[i].index(i + n - k)] if i < k else parts[n - k] for i in range(n)]
        leftward = [parts[order[i].index(i - n + k)] if i >= n - k else parts[n - k] for i in range(n)]
        if 2 * k <= n:
            choice = [r if i < k else l for i, (r, l) in enumerate(zip(rightward, leftward))]
            to_right = to_left = add(pick(place, choice), right, left)
        else:
            to_right, to_left = add(pick(place, rightward), right), add(pick(place, leftward), left)

        coming = [0] if k == n - 1 else [s for s in sent(k + 1) if parts[s] is None]

        def work(gate):
            return (*(part(s) for s in coming), *fill(k, gate))

        (right, left, *more), worked = travel(
            [
                (to_right, [(i, i + 1) for i in range(k)]),
                (to_left, [(n - 1 - i, n - 2 - i) for i in range(k)]),
                *along(k),
            ],
            work,
        )
        for s, one in zip(coming, worked):
            parts[s] = one
        took(k, more, worked[len(coming) :])
    return parts[0], right, left


def halves(n, pairs):
    ends = [(a, b) for a, b in pairs if a < n // 4 or a >= n - n // 4]
    return ends, [pair for pair in pairs if pair not in ends]


def joined(first, second):
    return first + second


def attend_forward(n, heads, rows, c, place_ref, *refs):
    chunks = refs[:n]
    cos_ref, sin_ref, qseg_ref, kseg_ref, o_ref, rot_ref, lse_ref, vt, acc, stat = refs[n:]
    hd = HEAD_SIZE
    kc, vc = heads * hd, (heads + 1) * hd
    for s in range(n):
        at = pl.ds(pl.multiple_of(place_ref[s] * rows, rows), rows)
        cos, sin = cos_ref[at, :], sin_ref[at, :]
        for h in range(heads + 1):
            u = chunks[s][:, h * hd : (h + 1) * hd]
            rot_ref[at, h * hd : (h + 1) * hd] = (u * cos + pltpu.roll(u, hd // 2, 1) * sin).astype(BF16)
        v = chunks[s][:, vc : vc + hd]
        rot_ref[at, vc : vc + hd] = v.astype(BF16)
        vt[:, at] = v.T.astype(BF16)

    def block(i, j, diagonal):
        qi = pl.ds(pl.multiple_of(i * rows, rows), rows)
        kj = pl.ds(pl.multiple_of(j * rows, rows), rows)
        k = rot_ref[kj, kc : kc + hd]
        allowed = kseg_ref[kj, :] == qseg_ref[:, qi]
        if diagonal:
            kr = lax.broadcasted_iota(jnp.int32, (rows, rows), 0)
            qr = lax.broadcasted_iota(jnp.int32, (rows, rows), 1)
            allowed = (allowed & (kr < qr)) | (kr == qr)
        for h in range(heads):
            q = rot_ref[qi, h * hd : (h + 1) * hd]
            scores = jnp.where(allowed, dot(k, q, NT) * c, MASKED)
            m = stat[h : h + 1, :]
            top = jnp.maximum(m, jnp.max(scores, axis=0, keepdims=True))
            p = jnp.exp2(scores - top)
            alpha = jnp.exp2(m - top)
            stat[h : h + 1, :] = top
            total = alpha * stat[8 + h : 9 + h, :] + jnp.sum(p, axis=0, keepdims=True)
            stat[8 + h : 9 + h, :] = total
            new = alpha * acc[h] + dot(vt[:, kj], p.astype(BF16), NN)
            if diagonal:
                at = pl.ds(pl.multiple_of(place_ref[n + i] * rows, rows), rows)
                o_ref[at, h * hd : (h + 1) * hd] = (new / total).T.astype(BF16)
                lse_ref[0, h : h + 1, qi] = top + jnp.log2(total)
            else:
                acc[h] = new

    @pl.loop(0, n)
    def _(i):
        stat[0:8, :] = jnp.full((8, rows), MASKED, F32)
        stat[8:16, :] = jnp.zeros((8, rows), F32)
        acc[...] = jnp.zeros_like(acc)

        @pl.loop(0, i)
        def _(j):
            block(i, j, False)

        block(i, i, True)


def attend_backward(n, heads, rows, c, place_ref, *refs):
    gas = refs[:n]
    rot_ref, o_ref, lse_ref, cos_ref, sin_ref, qseg_ref, kseg_ref, d_ref, go, dqt, delta, dk, dv, kt = refs[n:]
    hd = HEAD_SIZE
    scale = hd**-0.5
    kc, vc = heads * hd, (heads + 1) * hd
    for s in range(n):
        at = pl.ds(pl.multiple_of(place_ref[s] * rows, rows), rows)
        for h in range(heads):
            g = gas[s][:, h * hd : (h + 1) * hd]
            o = o_ref[s * rows : (s + 1) * rows, h * hd : (h + 1) * hd]
            go[at, h * hd : (h + 1) * hd] = g
            both = (g.astype(F32) * o.astype(F32)).T
            delta[h : h + 1, at] = jnp.sum(both, axis=0, keepdims=True)
        kt[:, at] = rot_ref[at, kc : kc + hd].astype(F32).T.astype(BF16)
    dqt[...] = jnp.zeros_like(dqt)

    def block(i, j, diagonal):
        qi = pl.ds(pl.multiple_of(i * rows, rows), rows)
        kj = pl.ds(pl.multiple_of(j * rows, rows), rows)
        k = rot_ref[kj, kc : kc + hd]
        v = rot_ref[kj, vc : vc + hd]
        allowed = kseg_ref[kj, :] == qseg_ref[:, qi]
        if diagonal:
            kr = lax.broadcasted_iota(jnp.int32, (rows, rows), 0)
            qr = lax.broadcasted_iota(jnp.int32, (rows, rows), 1)
            allowed = (allowed & (kr < qr)) | (kr == qr)
        for h in range(heads):
            cols = slice(h * hd, (h + 1) * hd)
            q = rot_ref[qi, cols]
            g = go[qi, cols]
            scores = jnp.where(allowed, dot(k, q, NT) * c, MASKED)
            p = jnp.exp2(scores - lse_ref[0, h : h + 1, qi])
            gp = dot(v, g, NT)
            ds = (p * (gp - delta[h : h + 1, qi])).astype(BF16)
            new_v = dot(p.astype(BF16), g, NN)
            new_k = dot(ds, q, NN)
            if diagonal and h == 0:
                dv[...] = new_v
                dk[...] = new_k
            else:
                dv[...] += new_v
                dk[...] += new_k
            dqt[h * hd : (h + 1) * hd, qi] += dot(kt[:, kj], ds, NN)

    def unrotate(u, at):
        return u * cos_ref[at, :] - pltpu.roll(u, hd // 2, 1) * sin_ref[at, :]

    @pl.loop(0, n)
    def _(j):
        block(j, j, True)

        @pl.loop(j + 1, n)
        def _(i):
            block(i, j, False)

        kj = pl.ds(pl.multiple_of(j * rows, rows), rows)
        to = pl.ds(pl.multiple_of(place_ref[n + j] * rows, rows), rows)
        for h in range(heads):
            u = dqt[h * hd : (h + 1) * hd, kj].T * scale
            d_ref[to, h * hd : (h + 1) * hd] = unrotate(u, kj).astype(BF16)
        d_ref[to, kc : kc + hd] = unrotate(dk[...] * scale, kj).astype(BF16)
        d_ref[to, vc : vc + hd] = dv[...].astype(BF16)


def attention_calls(n, rows, heads_q, heads_kv):
    heads = heads_q // heads_kv
    every = n * rows
    wide = (heads + 2) * HEAD_SIZE
    c = HEAD_SIZE**-0.5 * math.log2(math.e)
    whole = lambda shape: pl.BlockSpec(shape, lambda g, place: (0, 0))
    by_head = lambda r, w: pl.BlockSpec((r, w), lambda g, place: (0, g))
    tables = [
        whole((every, HEAD_SIZE)),
        whole((every, HEAD_SIZE)),
        whole((1, every)),
        whole((every, 1)),
    ]
    lse_spec = pl.BlockSpec((1, 8, every), lambda g, place: (g, 0, 0))
    pairs = every * every * heads_q
    params = pltpu.CompilerParams(vmem_limit_bytes=58 << 20)
    forward = pl.pallas_call(
        functools.partial(attend_forward, n, heads, rows, c),
        grid_spec=pltpu.PrefetchScalarGridSpec(
            num_scalar_prefetch=1,
            grid=(heads_kv,),
            in_specs=[by_head(rows, wide)] * n + tables,
            out_specs=[by_head(every, heads * HEAD_SIZE), by_head(every, wide), lse_spec],
            scratch_shapes=[
                pltpu.VMEM((HEAD_SIZE, every), BF16),
                pltpu.VMEM((heads, HEAD_SIZE, rows), F32),
                pltpu.VMEM((16, rows), F32),
            ],
        ),
        out_shape=[
            jax.ShapeDtypeStruct((every, heads_q * HEAD_SIZE), BF16),
            jax.ShapeDtypeStruct((every, heads_kv * wide), BF16),
            jax.ShapeDtypeStruct((heads_kv, 8, every), F32),
        ],
        compiler_params=params,
        cost_estimate=HIDES,
    )
    backward = pl.pallas_call(
        functools.partial(attend_backward, n, heads, rows, c),
        grid_spec=pltpu.PrefetchScalarGridSpec(
            num_scalar_prefetch=1,
            grid=(heads_kv,),
            in_specs=[by_head(rows, heads * HEAD_SIZE)] * n
            + [by_head(every, wide), by_head(every, heads * HEAD_SIZE), lse_spec]
            + tables,
            out_specs=by_head(every, wide),
            scratch_shapes=[
                pltpu.VMEM((every, heads * HEAD_SIZE), BF16),
                pltpu.VMEM((heads * HEAD_SIZE, every), F32),
                pltpu.VMEM((8, every), F32),
                pltpu.VMEM((rows, HEAD_SIZE), F32),
                pltpu.VMEM((rows, HEAD_SIZE), F32),
                pltpu.VMEM((HEAD_SIZE, every), BF16),
            ],
        ),
        out_shape=jax.ShapeDtypeStruct((every, heads_kv * wide), BF16),
        compiler_params=params,
        cost_estimate=pl.CostEstimate(flops=pairs * 10 * HEAD_SIZE, transcendentals=pairs, bytes_accessed=every * wide * 20),
    )
    return forward, backward


def gated_kernel(x_ref, gate_ref, up_ref, gm_ref, *refs):
    mixed_ref, dg_ref, du_ref = refs[-3:]
    x = x_ref[...]
    step = 256 if mixed_ref.shape[1] % 256 == 0 else mixed_ref.shape[1]
    for c in range(0, mixed_ref.shape[1], step):
        at = slice(c, c + step)
        gate = dot(x, gate_ref[:, at], NN)
        up = dot(x, up_ref[:, at], NN)
        gm = gm_ref[:, at]
        sig = 1.0 / (1.0 + jnp.exp(-gate))
        act = gate * sig
        mixed_ref[:, at] = (act * up).astype(BF16)
        du_ref[:, at] = (gm * act).astype(BF16)
        dg_ref[:, at] = (gm * up * sig * (1.0 + gate * (1.0 - sig))).astype(BF16)


def gated(x, w_both, gm, part, before=None):
    rows, width = x.shape
    hidden = w_both.shape[1] // 2
    tile = 512 if hidden % 512 == 0 else hidden
    tiles = hidden // tile
    weight = [pl.BlockSpec((width, tile), lambda j: (0, j)), pl.BlockSpec((width, tile), lambda j: (0, j + tiles))]
    here = pl.BlockSpec((rows, tile), lambda j: (part, j))
    before = () if before is None else tuple(before)
    return pl.pallas_call(
        gated_kernel,
        grid=(tiles,),
        in_specs=[pl.BlockSpec((rows, width), lambda j: (0, 0)), *weight, here]
        + [pl.BlockSpec(memory_space=pl.ANY)] * len(before),
        out_specs=[here] * 3,
        out_shape=[jax.ShapeDtypeStruct((2 * rows, hidden), BF16)] * 3,
        input_output_aliases={4 + i: i for i in range(len(before))},
        compiler_params=pltpu.CompilerParams(vmem_limit_bytes=50 << 20),
        cost_estimate=HIDES,
    )(x, w_both, w_both, gm, *before)


def spread_kernel(count, *refs):
    total = None
    for a_ref, w_ref in zip(refs[:count], refs[count : 2 * count]):
        term = lax.dot_general(a_ref[...], w_ref[...], NT, preferred_element_type=F32)
        total = term if total is None else total + term
    refs[-1][...] = total.astype(refs[-1].dtype)


def spread(acts, weights, part, out, cost=HIDES, piece=0, pieces=1):
    rows, hidden = acts[0].shape[0] // 2, acts[0].shape[1]
    width = weights[0][0].shape[0] // pieces
    tile = 256 if width % 256 == 0 else width
    tiles = width // tile
    count = len(acts)

    def column_block(which):
        return pl.BlockSpec((tile, hidden), lambda j: (j + piece * tiles, which))

    return pl.pallas_call(
        functools.partial(spread_kernel, count),
        grid=(tiles,),
        in_specs=[pl.BlockSpec((rows, hidden), lambda j: (part, 0))] * count
        + [column_block(which) for _, which in weights],
        out_specs=pl.BlockSpec((rows, tile), lambda j: (0, j)),
        out_shape=jax.ShapeDtypeStruct((rows, width), out),
        compiler_params=pltpu.CompilerParams(vmem_limit_bytes=50 << 20),
        cost_estimate=cost,
    )(*acts, *[array for array, _ in weights])


def norm_inverse(source):
    return lax.rsqrt(jnp.mean(source * source, axis=-1, keepdims=True) + EPSILON)


def norm_back_kernel(places, masked, gain_ref, source_ref, straight_ref, *refs):
    grads, refs = refs[: len(places)], refs[len(places) :]
    source = source_ref[...].astype(F32)
    width = source.shape[1]
    inverse = lax.rsqrt(jnp.mean(source * source, axis=-1, keepdims=True) + EPSILON)
    pieces = []
    for half in range(2):
        at = slice(half * width // 2, (half + 1) * width // 2)
        terms = [
            ref[:, at] if count == 2 else ref[...]
            for ref, (first, count) in zip(grads, places)
            if first <= half < first + count
        ]
        pieces.append(sum(term.astype(F32) for term in terms))
    scaled = jnp.concatenate(pieces, axis=1) * gain_ref[...]
    unit_rows = source * inverse
    grad = inverse * (scaled - unit_rows * jnp.mean(scaled * unit_rows, axis=-1, keepdims=True))
    straight = straight_ref[...].astype(F32)
    if masked:
        straight = straight * refs[0][...]
    total = straight + grad
    if masked:
        refs[1][...] = total
        refs[2][...] = total.astype(BF16)
    else:
        refs[0][...] = total


def norm_back(grads, source, gain, straight, mask, low):
    rows, width = source.shape
    tile = 64 if rows % 64 == 0 else rows
    block = lambda wide: pl.BlockSpec((tile, wide), lambda i: (i, 0))
    masked = mask is not None
    out_shape = [jax.ShapeDtypeStruct((rows, width), F32)] + [jax.ShapeDtypeStruct((rows, width), BF16)] * low
    return pl.pallas_call(
        functools.partial(norm_back_kernel, [place for _, *place in grads], masked),
        grid=(rows // tile,),
        in_specs=[pl.BlockSpec((1, width), lambda i: (0, 0)), block(width), block(width)]
        + [block(array.shape[1]) for array, _, _ in grads]
        + [block(1)] * masked,
        out_specs=[block(width)] * len(out_shape) if low else block(width),
        out_shape=out_shape if low else out_shape[0],
        compiler_params=pltpu.CompilerParams(vmem_limit_bytes=40 << 20),
        cost_estimate=HIDES,
    )(gain[None, :], source, straight, *[array for array, _, _ in grads], *([mask] if masked else []))


def turn_kernel(x_ref, o_ref):
    o_ref[...] = x_ref[...].astype(F32).T


def turned(array, first, size):
    rows = array.shape[0]
    return pl.pallas_call(
        turn_kernel,
        grid=(size // HEAD_SIZE,),
        in_specs=[pl.BlockSpec((rows, HEAD_SIZE), lambda j: (0, j + first // HEAD_SIZE))],
        out_specs=pl.BlockSpec((HEAD_SIZE, rows), lambda j: (j, 0)),
        out_shape=jax.ShapeDtypeStruct((size, rows), F32),
        cost_estimate=HIDES,
    )(array)


def shards(
    tokens,
    cotangent,
    segments,
    positions,
    counts,
    query_weight,
    key_projection_weight,
    value_projection_weight,
    out_weight,
    attn_gain,
    gate_weight,
    up_weight,
    down_weight,
    mlp_gain,
):
    n = lax.axis_size("tensor")
    place = lax.axis_index("tensor")
    rows, width = tokens.shape
    every = rows * n
    heads_q = query_weight.shape[1] // HEAD_SIZE
    heads_kv = key_projection_weight.shape[1] // HEAD_SIZE
    heads = heads_q // heads_kv
    qw, hd = heads * HEAD_SIZE, HEAD_SIZE
    wide = qw + 2 * hd
    slices = n // 2

    def gather(shard):
        return lax.all_gather(shard, "dp", axis=0, tiled=True)

    partners = halves(n, [(i, i ^ 1) for i in range(n)])
    outward = [halves(n, [((i + 2 * k) % n, i) for i in range(n)]) for k in range(1, slices)]
    homeward = [halves(n, [(i, (i + 2 * k) % n) for i in range(n)]) for k in range(1, slices)]

    def to_others(shard, half):
        return [(shard, pairs[half]) for pairs in outward]

    def to_owners(sums, half):
        return [(one, pairs[half]) for one, pairs in zip(sums, homeward)]

    live_count = counts[0]
    own_index = place * rows + jnp.arange(rows, dtype=jnp.int32)
    live = (own_index < live_count).astype(F32)[:, None]
    labels = lax.all_gather(jnp.stack([segments, positions]), "tensor", axis=1, tiled=True)
    seg_all, place_all = labels[0], labels[1]
    index_all = jnp.arange(every, dtype=jnp.int32)
    key_seg = jnp.where(index_all < live_count, seg_all, -1)[:, None]
    query_seg = seg_all[None, :]
    freqs = ROPE_BASE ** (-(jnp.arange(hd // 2, dtype=F32) * 2.0) / hd)
    angles = place_all.astype(F32)[:, None] * freqs[None, :]
    cos, sin = jnp.cos(angles), jnp.sin(angles)
    cos = jnp.concatenate([cos, cos], axis=1)
    sin = jnp.concatenate([-sin, sin], axis=1)
    order = np.array([[i] + row for i, row in enumerate(arrival_order(n))], np.int32)
    where_is = np.argsort(order, axis=1).astype(np.int32)
    slot_table = jnp.asarray(np.concatenate([order, where_is], axis=1))[place]
    attend, attend_back = attention_calls(n, rows, heads_q, heads_kv)
    tables = (cos, sin, query_seg, key_seg)

    gains = lax.all_gather(jnp.stack([attn_gain, mlp_gain]), "dp", axis=1, tiled=True).astype(F32)
    gain_one, gain_two = gains[0], gains[1]

    source = tokens.astype(F32)
    inv_one = norm_inverse(source)
    normed_one = (source * inv_one * gain_one).astype(BF16)

    def attention_weights(gate):
        query, key, value = lax.optimization_barrier((query_weight, key_projection_weight, value_projection_weight, gate))[:3]
        return jnp.concatenate(
            [
                part
                for g in range(heads_kv)
                for part in (
                    query[:, g * qw : (g + 1) * qw],
                    key[:, g * hd : (g + 1) * hd],
                    value[:, g * hd : (g + 1) * hd],
                )
            ],
            axis=1,
        )

    own_qkv = attention_weights(normed_one)
    w_qkv = gather(own_qkv)
    shards_here, early = [], []

    def shard_layouts(step, gate):
        if step != 1:
            return ()
        both = jnp.concatenate([after(gate_weight, gate), up_weight], axis=1)
        masked = (after(cotangent, gate).astype(F32) * live).astype(BF16)
        return (after(out_weight, gate).T, after(down_weight, gate).T, both, masked, *tables)

    def took_rows(step, arrived, filled):
        early.extend(arrived)
        if step == 1:
            shards_here.extend(filled[:4])

    more = slices - 1
    slots_one, projected = line_gather(
        after(normed_one, labels),
        n,
        lambda s, shard: dot(shard, w_qkv, NN),
        shard_layouts,
        lambda step: {
            n - 2: [(shards_here[3], partners[0])] if shards_here else (),
            n - 1: to_others(shards_here[2], 0) if shards_here else (),
        }.get(step, ()),
        took_rows,
    )
    low_ends, both_ends = early[0], early[1:]
    out_t, down_t, both_weight, grad_low = shards_here
    w_out, w_down, w_both = gather(out_t), [gather(down_t)], [gather(both_weight)]
    projected[n - 1] = after(projected[n - 1], w_out, w_down[0])

    def attention(gate):
        return attend(slot_table, *projected, *tables)

    downs = after(down_t, projected[n - 1])
    moved, (attended, rotated, lse) = travel([(downs, a + b) for a, b in outward], attention)
    w_down += [gather(shard) for shard in moved]
    grad_mixed, lows = [], []

    def while_out(step, gate):
        if step == 1:
            return (w_both[0],)
        if step == n - 1:
            theirs = joined(low_ends, lows[0])
            lows.append(theirs)
            return tuple(dot(jnp.concatenate([grad_low, theirs], axis=0), w, NN) for w in w_down)
        return ()

    def along_out(step):
        if step == 1:
            return to_others(both_weight, 1)
        if step == 2:
            return [(grad_low, partners[1])]
        return ()

    def took_out(step, arrived, filled):
        if step == 1:
            w_both.extend(gather(joined(a, b)) for a, b in zip(both_ends, arrived))
        elif step == n - 1:
            grad_mixed.extend(filled)
        else:
            lows.extend(arrived)

    summed = line_reduce(
        lambda s: dot(attended[s * rows : (s + 1) * rows], w_out, NT, BF16), n, while_out, along_out, took_out
    )
    hidden = source + sum(term.astype(F32) for term in summed)
    grad_two = jnp.concatenate([grad_low, lows[1]], axis=0)

    inv_two = norm_inverse(hidden)
    normed_two = (hidden * inv_two * gain_two).astype(BF16)

    def own_rows(gate):
        made = [one for w, gm in zip(w_both, grad_mixed) for one in gated(gate, w, gm, 0)]
        return [spread(made[1::3] + made[2::3], weights, 0, F32, HIDES, 0, 2), *made]

    swap = partners[0] + partners[1]
    weights = [(w, 0) for w in w_both] + [(w, 1) for w in w_both]
    (two_theirs,), (ours_first, *mine) = travel([(normed_two, swap)], own_rows)
    two = jnp.concatenate([normed_two, two_theirs], axis=0)
    mixed, grad_gate, grad_up, d_down = [None] * slices, [None] * slices, [None] * slices, [None] * slices
    rows_in = two_theirs
    for k in range(slices - 1, -1, -1):
        mixed[k], grad_gate[k], grad_up[k] = gated(rows_in, w_both[k], grad_mixed[k], 1, mine[3 * k : 3 * k + 3])
        if k > 0:
            d_down[k] = dot(grad_two, mixed[k], TN, BF16)
            rows_in = after(two_theirs, d_down[k])
    grads = grad_gate + grad_up
    d_up, d_gate = [None] * slices, [None] * slices

    def second_half(gate):
        return (
            spread([after(grads[0], gate)] + grads[1:], weights, 1, BF16, HIDES, 1, 2),
            *(dot(two, after(g, gate), TN, BF16) for g in grad_up[1:]),
        )

    def gate_weights(gate):
        return (
            spread([after(grads[0], gate)] + grads[1:], weights, 0, F32, HIDES, 1, 2),
            *(dot(two, after(g, gate), TN, BF16) for g in grad_gate[1:]),
        )

    theirs = spread(grads, weights, 1, BF16, HIDES, 0, 2)
    (from_first,), (theirs, *d_up[1:]) = travel([(theirs, swap)], second_half)
    (from_second,), (ours_second, *d_gate[1:]) = travel([(theirs, swap)], gate_weights)
    grad_hidden, grad_hidden_low = norm_back(
        [(ours_first, 0, 1), (ours_second, 1, 1), (from_first, 0, 1), (from_second, 1, 1)], hidden, gain_two, cotangent, live, True
    )

    def owner_sum(partial):
        return lax.psum_scatter(partial, "dp", scatter_dimension=0, tiled=True)

    results, early = [], []

    def d_of(left, right, gate):
        return dot(left, after(right, gate), TN, BF16)

    def result_rows(part, out, gate, cost=HIDES):
        return spread([after(mixed[0], gate), *mixed[1:]], [(w, 0) for w in w_down], part, out, cost)

    def while_gather(step, gate):
        if step == 1:
            flops = 2 * rows * width * slices * gate_weight.shape[1]
            cost = pl.CostEstimate(flops=flops, transcendentals=0, bytes_accessed=flops // rows)
            return (result_rows(1, BF16, gate, cost), d_of(grad_two, mixed[0], gate))
        if step == 2:
            return (result_rows(0, F32, gate), d_of(two, grad_up[0], gate), *joined_sums())
        if step == n - 1:
            return (d_of(two, grad_gate[0], gate),)
        return ()

    def took_gather(step, arrived, filled):
        early.extend(arrived)
        if step == 1:
            results.append(filled[0])
            d_down[0] = filled[1]
        elif step == 2:
            results.append(filled[0])
            d_up[0] = filled[1]
            sums.extend(filled[2:])
        elif step == n - 1:
            d_gate[0] = filled[0]

    sums = []

    def joined_sums():
        return [jnp.concatenate([owner_sum(a), owner_sum(b)], axis=1) for a, b in zip(d_down[1:], d_up[1:])]

    slots_back, grad_attended = line_gather(
        grad_hidden_low,
        n,
        lambda s, shard: dot(shard, w_out, NN, BF16),
        while_gather,
        lambda step: {
            2: [(results[0], partners[0])] if results else (),
            n - 1: to_owners(sums, 0),
        }.get(step, ()),
        took_gather,
    )
    result_ends, sum_ends = early[0], early[1:]

    def attention_back(gate):
        return (
            attend_back(after(slot_table, gate), *grad_attended, rotated, attended, lse, *tables),
            d_of(jnp.concatenate(slots_back, axis=0), attended, gate),
            sum_down,
        )

    sums_gate = [owner_sum(d) for d in d_gate[1:]]
    sum_down, sum_up, sum_gate = owner_sum(d_down[0]), owner_sum(d_up[0]), owner_sum(d_gate[0])
    leaving = [after(one, grad_attended[n - 1]) for one in sums_gate]
    back_gate, (grad_qkv, d_out, _) = travel(
        [(one, a + b) for one, (a, b) in zip(leaving, homeward)], attention_back
    )
    back_down, back_up, outputs, d_attention = [], [], [], []
    all_heads = own_qkv.shape[1]

    def columns(array, offset, size):
        return jnp.concatenate(
            [array[:, g * wide + offset : g * wide + offset + size] for g in range(heads_kv)], axis=1
        ).astype(F32)


    def while_reduce(step, gate):
        if step == 1:
            d_qkv = d_of(jnp.concatenate(slots_one, axis=0), grad_qkv, gate)
            return (jnp.concatenate([d_qkv, d_out], axis=1), sum_up)
        if step == 2:
            return (sum_gate,)
        if step == n - 1:
            from_partner = joined(result_ends, outputs[0])
            result = hidden + (results[1] + after(from_partner, gate).astype(F32))
            sum_attention = owner_sum(d_attention[0])
            return (
                (result * live).astype(BF16),
                turned(sum_attention, all_heads, out_weight.shape[0]),
                *(columns(sum_attention, *place) for place in ((0, qw), (qw, hd), (qw + hd, hd))),
                sum_attention,
            )
        return ()

    def along_reduce(step):
        if step == 1:
            return to_owners(sums, 1)
        if step == 2:
            return [(results[0], partners[1])]
        return ()

    def took_reduce(step, arrived, filled):
        if step == 1:
            for a, b in zip(sum_ends, arrived):
                back = joined(a, b)
                back_down.append(back[:, : down_t.shape[1]])
                back_up.append(back[:, down_t.shape[1] :])
            d_attention.append(filled[0])
        elif step == 2:
            outputs.extend(arrived)
        elif step == n - 1:
            outputs.extend(filled)

    grad_normed_one = line_reduce(
        lambda s: dot(grad_qkv[s * rows : (s + 1) * rows], w_qkv, NT, BF16),
        n,
        while_reduce,
        along_reduce,
        took_reduce,
    )
    _, output, grad_out_w, grad_query_w, grad_key_w, grad_value_w, sum_attention = outputs

    def whole(first, back):
        return sum((one.astype(F32) for one in back), first.astype(F32))

    grad_down_w = whole(sum_down, back_down).T
    grad_gate_w = whole(sum_gate, back_gate)
    grad_up_w = whole(sum_up, back_up)
    grad_qkv_w = sum_attention[:, :all_heads].astype(F32)
    def along_row(weight, grad):
        return jnp.sum(weight.astype(F32) * grad, axis=1)

    gain_parts = jnp.stack(
        [
            along_row(own_qkv, grad_qkv_w),
            along_row(gate_weight, grad_gate_w) + along_row(up_weight, grad_up_w),
        ]
    )
    gain_own = lax.psum(gain_parts, "tensor") / jnp.stack([attn_gain, mlp_gain]).astype(F32)

    grad_tokens = norm_back([(term, 0, 2) for term in grad_normed_one], tokens, gain_one, grad_hidden, None, False)

    return (
        output,
        grad_tokens,
        grad_query_w,
        grad_key_w,
        grad_value_w,
        grad_out_w,
        gain_own[0],
        grad_gate_w,
        grad_up_w,
        grad_down_w,
        gain_own[1],
    )


def solution(mesh):
    rows = P(("dp", "tensor"), None)
    row = P(("dp", "tensor"))
    down_cols = P("tensor", "dp")
    cols = P("dp", "tensor")
    return jax.shard_map(
        shards,
        mesh=mesh,
        in_specs=(rows, rows, row, row, P("dp"), cols, cols, cols, down_cols, P("dp"), cols, cols, down_cols, P("dp")),
        out_specs=(rows, rows, cols, cols, cols, down_cols, P("dp"), cols, cols, down_cols, P("dp")),
        check_vma=False,
    )
```

```python
import functools
import math

import jax
import jax.numpy as jnp
import numpy as np
from jax import lax
from jax.experimental import pallas as pl
from jax.experimental.pallas import tpu as pltpu
from jax.sharding import PartitionSpec as P

HEAD_SIZE = 128
EPSILON = 1e-05
ROPE_BASE = 500000.0
MASKED = -1e30
F32 = jnp.float32
BF16 = jnp.bfloat16
NT = (((1,), (1,)), ((), ()))
NN = (((1,), (0,)), ((), ()))
TN = (((0,), (0,)), ((), ()))
HIDES = pl.CostEstimate(flops=1, transcendentals=0, bytes_accessed=1)


def dot(a, b, dims, out=F32):
    return lax.dot_general(a, b, dims, preferred_element_type=F32).astype(out)


def after(value, *others):
    return lax.optimization_barrier((value, *others))[0]


def arrival_order(n):
    return [
        [s for d in range(1, n) for s in (i - d, i + d) if 0 <= s < n]
        for i in range(n)
    ]


def pick(place, choices):
    distinct = []
    for value in choices:
        if not any(value is other for other in distinct):
            distinct.append(value)
    out = distinct[0]
    for value in distinct[1:]:
        here = functools.reduce(
            jnp.logical_or, [place == i for i, c in enumerate(choices) if c is value]
        )
        out = jnp.where(here, value, out)
    return out


def travel(items, work=lambda gate: ()):
    arrays = lax.optimization_barrier(tuple(array for array, _ in items))
    moved = [lax.ppermute(array, "tensor", pairs) for array, (_, pairs) in zip(arrays, items)]
    out = lax.optimization_barrier((*moved, *work(arrays[0])))
    return list(out[: len(moved)]), list(out[len(moved) :])


def line_gather(own, n, use, fill=lambda step, gate: (), along=lambda step: (), took=lambda step, arrived, filled: None):
    place = lax.axis_index("tensor")
    order = arrival_order(n)
    right = left = own
    from_left, from_right = [own], [own]
    slots, used = [own], []
    for d in range(1, n):

        def work(gate):
            return (use(d - 1, after(slots[d - 1], gate) if d > 1 else own), *fill(d, gate))

        (right, left, *more), (result, *filled) = travel(
            [
                (right, [(i, i + 1) for i in range(d - 1, n - 1)]),
                (left, [(i + 1, i) for i in range(n - d)]),
                *along(d),
            ],
            work,
        )
        used.append(result)
        took(d, more, filled)
        from_left.append(right)
        from_right.append(left)
        slots.append(
            pick(
                place,
                [
                    from_left[i - order[i][d - 1]] if order[i][d - 1] < i else from_right[order[i][d - 1] - i]
                    for i in range(n)
                ],
            )
        )
    used.append(use(n - 1, slots[-1]))
    return slots, used


def choose_kernel(count, which_ref, *refs):
    value = refs[0][...]
    for c in range(1, count):
        value = jnp.where(which_ref[0] == c, refs[c][...], value)
    total = value.astype(F32)
    for ref in refs[count:-1]:
        total = total + ref[...].astype(F32)
    refs[-1][...] = total.astype(BF16)


def chosen_sum(place, choices, sums):
    distinct = []
    for value in choices:
        if not any(value is other for other in distinct):
            distinct.append(value)
    table = [next(d for d, other in enumerate(distinct) if value is other) for value in choices]
    which = jnp.asarray(table, jnp.int32)[place][None]
    rows, width = choices[0].shape
    tile = 64 if rows % 64 == 0 else rows

    def candidate(c):
        return pl.BlockSpec((tile, width), lambda i, which: (jnp.where(which[0] == c, i, 0), 0))

    plain = pl.BlockSpec((tile, width), lambda i, which: (i, 0))
    return pl.pallas_call(
        functools.partial(choose_kernel, len(distinct)),
        grid_spec=pltpu.PrefetchScalarGridSpec(
            num_scalar_prefetch=1,
            grid=(rows // tile,),
            in_specs=[candidate(c) for c in range(len(distinct))] + [plain] * len(sums),
            out_specs=plain,
        ),
        out_shape=jax.ShapeDtypeStruct((rows, width), BF16),
        compiler_params=pltpu.CompilerParams(vmem_limit_bytes=30 << 20),
        cost_estimate=HIDES,
    )(which, *distinct, *sums)


def line_reduce(part, n, fill=lambda step, gate: (), along=lambda step: (), took=lambda step, arrived, filled: None):
    place = lax.axis_index("tensor")
    parts = [None] * n
    parts[n - 1] = lax.optimization_barrier(part(n - 1))
    order = [[i] + row for i, row in enumerate(arrival_order(n))]
    right = left = None

    def sent(k):
        ways = [order[i].index(i + n - k) for i in range(k)] + [order[i].index(i - n + k) for i in range(n - k, n)]
        return sorted(set(ways), reverse=True)

    def add(value, *sums):
        if right is None:
            return value
        return (value.astype(F32) + sum(one.astype(F32) for one in sums)).astype(BF16)

    for k in range(1, n):
        rightward = [parts[order[i].index(i + n - k)] if i < k else parts[n - k] for i in range(n)]
        leftward = [parts[order[i].index(i - n + k)] if i >= n - k else parts[n - k] for i in range(n)]
        if 2 * k <= n:
            choice = [r if i < k else l for i, (r, l) in enumerate(zip(rightward, leftward))]
            to_right = to_left = pick(place, choice) if right is None else chosen_sum(place, choice, (right, left))
        else:
            to_right, to_left = add(pick(place, rightward), right), add(pick(place, leftward), left)

        coming = [0] if k == n - 1 else [s for s in sent(k + 1) if parts[s] is None]

        def work(gate):
            return (*(part(s) for s in coming), *fill(k, gate))

        (right, left, *more), worked = travel(
            [
                (to_right, [(i, i + 1) for i in range(k)]),
                (to_left, [(n - 1 - i, n - 2 - i) for i in range(k)]),
                *along(k),
            ],
            work,
        )
        for s, one in zip(coming, worked):
            parts[s] = one
        took(k, more, worked[len(coming) :])
    return parts[0], right, left


def halves(n, pairs):
    ends = [(a, b) for a, b in pairs if a < n // 4 or a >= n - n // 4]
    return ends, [pair for pair in pairs if pair not in ends]


def joined(first, second):
    return first + second


def attend_forward(n, heads, rows, c, place_ref, *refs):
    chunks = refs[:n]
    cos_ref, sin_ref, qseg_ref, kseg_ref, o_ref, rot_ref, lse_ref, vt, acc, stat = refs[n:]
    hd = HEAD_SIZE
    kc, vc = heads * hd, (heads + 1) * hd
    for s in range(n):
        at = pl.ds(pl.multiple_of(place_ref[s] * rows, rows), rows)
        cos, sin = cos_ref[at, :], sin_ref[at, :]
        for h in range(heads + 1):
            u = chunks[s][:, h * hd : (h + 1) * hd]
            rot_ref[at, h * hd : (h + 1) * hd] = (u * cos + pltpu.roll(u, hd // 2, 1) * sin).astype(BF16)
        v = chunks[s][:, vc : vc + hd]
        rot_ref[at, vc : vc + hd] = v.astype(BF16)
        vt[:, at] = v.T.astype(BF16)

    def block(i, j, diagonal):
        qi = pl.ds(pl.multiple_of(i * rows, rows), rows)
        kj = pl.ds(pl.multiple_of(j * rows, rows), rows)
        k = rot_ref[kj, kc : kc + hd]
        allowed = kseg_ref[kj, :] == qseg_ref[:, qi]
        if diagonal:
            kr = lax.broadcasted_iota(jnp.int32, (rows, rows), 0)
            qr = lax.broadcasted_iota(jnp.int32, (rows, rows), 1)
            allowed = (allowed & (kr < qr)) | (kr == qr)
        for h in range(heads):
            q = rot_ref[qi, h * hd : (h + 1) * hd]
            scores = jnp.where(allowed, dot(k, q, NT) * c, MASKED)
            m = stat[h : h + 1, :]
            top = jnp.maximum(m, jnp.max(scores, axis=0, keepdims=True))
            p = jnp.exp2(scores - top)
            alpha = jnp.exp2(m - top)
            stat[h : h + 1, :] = top
            total = alpha * stat[8 + h : 9 + h, :] + jnp.sum(p, axis=0, keepdims=True)
            stat[8 + h : 9 + h, :] = total
            new = alpha * acc[h] + dot(vt[:, kj], p.astype(BF16), NN)
            if diagonal:
                at = pl.ds(pl.multiple_of(place_ref[n + i] * rows, rows), rows)
                o_ref[at, h * hd : (h + 1) * hd] = (new / total).T.astype(BF16)
                lse_ref[0, h : h + 1, qi] = top + jnp.log2(total)
            else:
                acc[h] = new

    @pl.loop(0, n)
    def _(i):
        stat[0:8, :] = jnp.full((8, rows), MASKED, F32)
        stat[8:16, :] = jnp.zeros((8, rows), F32)
        acc[...] = jnp.zeros_like(acc)

        @pl.loop(0, i)
        def _(j):
            block(i, j, False)

        block(i, i, True)


def attend_backward(n, heads, rows, c, place_ref, *refs):
    gas = refs[:n]
    rot_ref, o_ref, lse_ref, cos_ref, sin_ref, qseg_ref, kseg_ref, d_ref, go, dqt, delta, dk, dv, kt = refs[n:]
    hd = HEAD_SIZE
    scale = hd**-0.5
    kc, vc = heads * hd, (heads + 1) * hd
    for s in range(n):
        at = pl.ds(pl.multiple_of(place_ref[s] * rows, rows), rows)
        for h in range(heads):
            g = gas[s][:, h * hd : (h + 1) * hd]
            o = o_ref[s * rows : (s + 1) * rows, h * hd : (h + 1) * hd]
            go[at, h * hd : (h + 1) * hd] = g
            both = (g.astype(F32) * o.astype(F32)).T
            delta[h : h + 1, at] = jnp.sum(both, axis=0, keepdims=True)
        kt[:, at] = rot_ref[at, kc : kc + hd].astype(F32).T.astype(BF16)
    dqt[...] = jnp.zeros_like(dqt)

    def block(i, j, diagonal):
        qi = pl.ds(pl.multiple_of(i * rows, rows), rows)
        kj = pl.ds(pl.multiple_of(j * rows, rows), rows)
        k = rot_ref[kj, kc : kc + hd]
        v = rot_ref[kj, vc : vc + hd]
        allowed = kseg_ref[kj, :] == qseg_ref[:, qi]
        if diagonal:
            kr = lax.broadcasted_iota(jnp.int32, (rows, rows), 0)
            qr = lax.broadcasted_iota(jnp.int32, (rows, rows), 1)
            allowed = (allowed & (kr < qr)) | (kr == qr)
        for h in range(heads):
            cols = slice(h * hd, (h + 1) * hd)
            q = rot_ref[qi, cols]
            g = go[qi, cols]
            scores = jnp.where(allowed, dot(k, q, NT) * c, MASKED)
            p = jnp.exp2(scores - lse_ref[0, h : h + 1, qi])
            gp = dot(v, g, NT)
            ds = (p * (gp - delta[h : h + 1, qi])).astype(BF16)
            new_v = dot(p.astype(BF16), g, NN)
            new_k = dot(ds, q, NN)
            if diagonal and h == 0:
                dv[...] = new_v
                dk[...] = new_k
            else:
                dv[...] += new_v
                dk[...] += new_k
            dqt[h * hd : (h + 1) * hd, qi] += dot(kt[:, kj], ds, NN)

    def unrotate(u, at):
        return u * cos_ref[at, :] - pltpu.roll(u, hd // 2, 1) * sin_ref[at, :]

    @pl.loop(0, n)
    def _(j):
        block(j, j, True)

        @pl.loop(j + 1, n)
        def _(i):
            block(i, j, False)

        kj = pl.ds(pl.multiple_of(j * rows, rows), rows)
        to = pl.ds(pl.multiple_of(place_ref[n + j] * rows, rows), rows)
        for h in range(heads):
            u = dqt[h * hd : (h + 1) * hd, kj].T * scale
            d_ref[to, h * hd : (h + 1) * hd] = unrotate(u, kj).astype(BF16)
        d_ref[to, kc : kc + hd] = unrotate(dk[...] * scale, kj).astype(BF16)
        d_ref[to, vc : vc + hd] = dv[...].astype(BF16)


def attention_calls(n, rows, heads_q, heads_kv):
    heads = heads_q // heads_kv
    every = n * rows
    wide = (heads + 2) * HEAD_SIZE
    c = HEAD_SIZE**-0.5 * math.log2(math.e)
    whole = lambda shape: pl.BlockSpec(shape, lambda g, place: (0, 0))
    by_head = lambda r, w: pl.BlockSpec((r, w), lambda g, place: (0, g))
    tables = [
        whole((every, HEAD_SIZE)),
        whole((every, HEAD_SIZE)),
        whole((1, every)),
        whole((every, 1)),
    ]
    lse_spec = pl.BlockSpec((1, 8, every), lambda g, place: (g, 0, 0))
    pairs = every * every * heads_q
    params = pltpu.CompilerParams(vmem_limit_bytes=58 << 20)
    forward = pl.pallas_call(
        functools.partial(attend_forward, n, heads, rows, c),
        grid_spec=pltpu.PrefetchScalarGridSpec(
            num_scalar_prefetch=1,
            grid=(heads_kv,),
            in_specs=[by_head(rows, wide)] * n + tables,
            out_specs=[by_head(every, heads * HEAD_SIZE), by_head(every, wide), lse_spec],
            scratch_shapes=[
                pltpu.VMEM((HEAD_SIZE, every), BF16),
                pltpu.VMEM((heads, HEAD_SIZE, rows), F32),
                pltpu.VMEM((16, rows), F32),
            ],
        ),
        out_shape=[
            jax.ShapeDtypeStruct((every, heads_q * HEAD_SIZE), BF16),
            jax.ShapeDtypeStruct((every, heads_kv * wide), BF16),
            jax.ShapeDtypeStruct((heads_kv, 8, every), F32),
        ],
        compiler_params=params,
        cost_estimate=HIDES,
    )
    backward = pl.pallas_call(
        functools.partial(attend_backward, n, heads, rows, c),
        grid_spec=pltpu.PrefetchScalarGridSpec(
            num_scalar_prefetch=1,
            grid=(heads_kv,),
            in_specs=[by_head(rows, heads * HEAD_SIZE)] * n
            + [by_head(every, wide), by_head(every, heads * HEAD_SIZE), lse_spec]
            + tables,
            out_specs=by_head(every, wide),
            scratch_shapes=[
                pltpu.VMEM((every, heads * HEAD_SIZE), BF16),
                pltpu.VMEM((heads * HEAD_SIZE, every), F32),
                pltpu.VMEM((8, every), F32),
                pltpu.VMEM((rows, HEAD_SIZE), F32),
                pltpu.VMEM((rows, HEAD_SIZE), F32),
                pltpu.VMEM((HEAD_SIZE, every), BF16),
            ],
        ),
        out_shape=jax.ShapeDtypeStruct((every, heads_kv * wide), BF16),
        compiler_params=params,
        cost_estimate=pl.CostEstimate(flops=pairs * 10 * HEAD_SIZE, transcendentals=pairs, bytes_accessed=every * wide * 20),
    )
    return forward, backward


def gated_kernel(x_ref, gate_ref, up_ref, gm_ref, *refs):
    mixed_ref, dg_ref, du_ref = refs[-3:]
    x = x_ref[...]
    step = 256 if mixed_ref.shape[1] % 256 == 0 else mixed_ref.shape[1]
    for c in range(0, mixed_ref.shape[1], step):
        at = slice(c, c + step)
        gate = dot(x, gate_ref[:, at], NN)
        up = dot(x, up_ref[:, at], NN)
        gm = gm_ref[:, at]
        sig = 1.0 / (1.0 + jnp.exp(-gate))
        act = gate * sig
        mixed_ref[:, at] = (act * up).astype(BF16)
        du_ref[:, at] = (gm * act).astype(BF16)
        dg_ref[:, at] = (gm * up * sig * (1.0 + gate * (1.0 - sig))).astype(BF16)


def gated(x, w_both, gm, part, before=None):
    rows, width = x.shape
    hidden = w_both.shape[1] // 2
    tile = 512 if hidden % 512 == 0 else hidden
    tiles = hidden // tile
    weight = [pl.BlockSpec((width, tile), lambda j: (0, j)), pl.BlockSpec((width, tile), lambda j: (0, j + tiles))]
    here = pl.BlockSpec((rows, tile), lambda j: (part, j))
    before = () if before is None else tuple(before)
    return pl.pallas_call(
        gated_kernel,
        grid=(tiles,),
        in_specs=[pl.BlockSpec((rows, width), lambda j: (0, 0)), *weight, here]
        + [pl.BlockSpec(memory_space=pl.ANY)] * len(before),
        out_specs=[here] * 3,
        out_shape=[jax.ShapeDtypeStruct((2 * rows, hidden), BF16)] * 3,
        input_output_aliases={4 + i: i for i in range(len(before))},
        compiler_params=pltpu.CompilerParams(vmem_limit_bytes=50 << 20),
        cost_estimate=HIDES,
    )(x, w_both, w_both, gm, *before)


def spread_kernel(count, *refs):
    total = None
    for a_ref, w_ref in zip(refs[:count], refs[count : 2 * count]):
        term = lax.dot_general(a_ref[...], w_ref[...], NT, preferred_element_type=F32)
        total = term if total is None else total + term
    refs[-1][...] = total.astype(refs[-1].dtype)


def spread(acts, weights, part, out, cost=HIDES, piece=0, pieces=1, parts=2):
    rows, hidden = acts[0].shape[0] // parts, acts[0].shape[1]
    width = weights[0][0].shape[0] // pieces
    tile = 256 if width % 256 == 0 else width
    tiles = width // tile
    count = len(acts)

    def column_block(which):
        return pl.BlockSpec((tile, hidden), lambda j: (j + piece * tiles, which))

    return pl.pallas_call(
        functools.partial(spread_kernel, count),
        grid=(tiles,),
        in_specs=[pl.BlockSpec((rows, hidden), lambda j: (part, 0))] * count
        + [column_block(which) for _, which in weights],
        out_specs=pl.BlockSpec((rows, tile), lambda j: (0, j)),
        out_shape=jax.ShapeDtypeStruct((rows, width), out),
        compiler_params=pltpu.CompilerParams(vmem_limit_bytes=50 << 20),
        cost_estimate=cost,
    )(*acts, *[array for array, _ in weights])


def norm_inverse(source):
    return lax.rsqrt(jnp.mean(source * source, axis=-1, keepdims=True) + EPSILON)


def norm_back_kernel(places, masked, gain_ref, source_ref, straight_ref, *refs):
    grads, refs = refs[: len(places)], refs[len(places) :]
    source = source_ref[...].astype(F32)
    width = source.shape[1]
    inverse = lax.rsqrt(jnp.mean(source * source, axis=-1, keepdims=True) + EPSILON)
    pieces = []
    for half in range(2):
        at = slice(half * width // 2, (half + 1) * width // 2)
        terms = [
            ref[:, at] if count == 2 else ref[...]
            for ref, (first, count) in zip(grads, places)
            if first <= half < first + count
        ]
        pieces.append(sum(term.astype(F32) for term in terms))
    scaled = jnp.concatenate(pieces, axis=1) * gain_ref[...]
    unit_rows = source * inverse
    grad = inverse * (scaled - unit_rows * jnp.mean(scaled * unit_rows, axis=-1, keepdims=True))
    straight = straight_ref[...].astype(F32)
    if masked:
        straight = straight * refs[0][...]
    total = straight + grad
    if masked:
        refs[1][...] = total
        refs[2][...] = total.astype(BF16)
    else:
        refs[0][...] = total


def norm_back(grads, source, gain, straight, mask, low):
    rows, width = source.shape
    tile = 64 if rows % 64 == 0 else rows
    block = lambda wide: pl.BlockSpec((tile, wide), lambda i: (i, 0))
    masked = mask is not None
    out_shape = [jax.ShapeDtypeStruct((rows, width), F32)] + [jax.ShapeDtypeStruct((rows, width), BF16)] * low
    return pl.pallas_call(
        functools.partial(norm_back_kernel, [place for _, *place in grads], masked),
        grid=(rows // tile,),
        in_specs=[pl.BlockSpec((1, width), lambda i: (0, 0)), block(width), block(width)]
        + [block(array.shape[1]) for array, _, _ in grads]
        + [block(1)] * masked,
        out_specs=[block(width)] * len(out_shape) if low else block(width),
        out_shape=out_shape if low else out_shape[0],
        compiler_params=pltpu.CompilerParams(vmem_limit_bytes=40 << 20),
        cost_estimate=HIDES,
    )(gain[None, :], source, straight, *[array for array, _, _ in grads], *([mask] if masked else []))


def turn_kernel(x_ref, o_ref):
    o_ref[...] = x_ref[...].astype(F32).T


def turned(array, first, size):
    rows = array.shape[0]
    return pl.pallas_call(
        turn_kernel,
        grid=(size // HEAD_SIZE,),
        in_specs=[pl.BlockSpec((rows, HEAD_SIZE), lambda j: (0, j + first // HEAD_SIZE))],
        out_specs=pl.BlockSpec((HEAD_SIZE, rows), lambda j: (j, 0)),
        out_shape=jax.ShapeDtypeStruct((size, rows), F32),
        cost_estimate=HIDES,
    )(array)


def shards(
    tokens,
    cotangent,
    segments,
    positions,
    counts,
    query_weight,
    key_projection_weight,
    value_projection_weight,
    out_weight,
    attn_gain,
    gate_weight,
    up_weight,
    down_weight,
    mlp_gain,
):
    n = lax.axis_size("tensor")
    place = lax.axis_index("tensor")
    rows, width = tokens.shape
    every = rows * n
    heads_q = query_weight.shape[1] // HEAD_SIZE
    heads_kv = key_projection_weight.shape[1] // HEAD_SIZE
    heads = heads_q // heads_kv
    qw, hd = heads * HEAD_SIZE, HEAD_SIZE
    wide = qw + 2 * hd
    slices = n // 2

    def gather(shard):
        return lax.all_gather(shard, "dp", axis=0, tiled=True)

    partners = halves(n, [(i, i ^ 1) for i in range(n)])
    outward = [halves(n, [((i + 2 * k) % n, i) for i in range(n)]) for k in range(1, slices)]
    homeward = [halves(n, [(i, (i + 2 * k) % n) for i in range(n)]) for k in range(1, slices)]

    def to_others(shard, half):
        return [(shard, pairs[half]) for pairs in outward]

    def to_owners(sums, half):
        return [(one, pairs[half]) for one, pairs in zip(sums, homeward)]

    live_count = counts[0]
    own_index = place * rows + jnp.arange(rows, dtype=jnp.int32)
    live = (own_index < live_count).astype(F32)[:, None]
    labels = lax.all_gather(jnp.stack([segments, positions]), "tensor", axis=1, tiled=True)
    seg_all, place_all = labels[0], labels[1]
    index_all = jnp.arange(every, dtype=jnp.int32)
    key_seg = jnp.where(index_all < live_count, seg_all, -1)[:, None]
    query_seg = seg_all[None, :]
    freqs = ROPE_BASE ** (-(jnp.arange(hd // 2, dtype=F32) * 2.0) / hd)
    angles = place_all.astype(F32)[:, None] * freqs[None, :]
    cos, sin = jnp.cos(angles), jnp.sin(angles)
    cos = jnp.concatenate([cos, cos], axis=1)
    sin = jnp.concatenate([-sin, sin], axis=1)
    order = np.array([[i] + row for i, row in enumerate(arrival_order(n))], np.int32)
    where_is = np.argsort(order, axis=1).astype(np.int32)
    slot_table = jnp.asarray(np.concatenate([order, where_is], axis=1))[place]
    attend, attend_back = attention_calls(n, rows, heads_q, heads_kv)
    tables = (cos, sin, query_seg, key_seg)

    gains = lax.all_gather(jnp.stack([attn_gain, mlp_gain]), "dp", axis=1, tiled=True).astype(F32)
    gain_one, gain_two = gains[0], gains[1]

    source = tokens.astype(F32)
    inv_one = norm_inverse(source)
    normed_one = (source * inv_one * gain_one).astype(BF16)

    def attention_weights(gate):
        query, key, value = lax.optimization_barrier((query_weight, key_projection_weight, value_projection_weight, gate))[:3]
        return jnp.concatenate(
            [
                part
                for g in range(heads_kv)
                for part in (
                    query[:, g * qw : (g + 1) * qw],
                    key[:, g * hd : (g + 1) * hd],
                    value[:, g * hd : (g + 1) * hd],
                )
            ],
            axis=1,
        )

    own_qkv = attention_weights(normed_one)
    w_qkv = gather(own_qkv)
    shards_here, early = [], []

    def shard_layouts(step, gate):
        if step != 1:
            return ()
        both = jnp.concatenate([after(gate_weight, gate), up_weight], axis=1)
        masked = (after(cotangent, gate).astype(F32) * live).astype(BF16)
        return (after(out_weight, gate).T, after(down_weight, gate).T, both, masked, *tables)

    def took_rows(step, arrived, filled):
        early.extend(arrived)
        if step == 1:
            shards_here.extend(filled[:4])

    more = slices - 1
    slots_one, projected = line_gather(
        after(normed_one, labels),
        n,
        lambda s, shard: dot(shard, w_qkv, NN),
        shard_layouts,
        lambda step: {
            n - 2: [(shards_here[3], partners[0])] if shards_here else (),
            n - 1: to_others(shards_here[2], 0) if shards_here else (),
        }.get(step, ()),
        took_rows,
    )
    low_ends, both_ends = early[0], early[1:]
    out_t, down_t, both_weight, grad_low = shards_here
    w_out, w_down, w_both = gather(out_t), [gather(down_t)], [gather(both_weight)]
    projected[n - 1] = after(projected[n - 1], w_out, w_down[0])

    def attention(gate):
        return attend(slot_table, *projected, *tables)

    downs = after(down_t, projected[n - 1])
    moved, (attended, rotated, lse) = travel([(downs, a + b) for a, b in outward], attention)
    w_down += [gather(shard) for shard in moved]
    grad_mixed, lows = [], []

    def while_out(step, gate):
        if step == 1:
            return (w_both[0],)
        if step == n - 1:
            theirs = joined(low_ends, lows[0])
            lows.append(theirs)
            return tuple(dot(jnp.concatenate([grad_low, theirs], axis=0), w, NN) for w in w_down)
        return ()

    def along_out(step):
        if step == 1:
            return to_others(both_weight, 1)
        if step == 2:
            return [(grad_low, partners[1])]
        return ()

    def took_out(step, arrived, filled):
        if step == 1:
            w_both.extend(gather(joined(a, b)) for a, b in zip(both_ends, arrived))
        elif step == n - 1:
            grad_mixed.extend(filled)
        else:
            lows.extend(arrived)

    summed = line_reduce(
        lambda s: dot(attended[s * rows : (s + 1) * rows], w_out, NT, BF16), n, while_out, along_out, took_out
    )
    hidden = source + sum(term.astype(F32) for term in summed)
    grad_two = jnp.concatenate([grad_low, lows[1]], axis=0)

    inv_two = norm_inverse(hidden)
    normed_two = (hidden * inv_two * gain_two).astype(BF16)

    def own_rows(gate):
        made = [one for w, gm in zip(w_both, grad_mixed) for one in gated(gate, w, gm, 0)]
        return [spread(made[1::3] + made[2::3], weights, 0, F32, HIDES, 0, 2), *made]

    swap = partners[0] + partners[1]
    weights = [(w, 0) for w in w_both] + [(w, 1) for w in w_both]
    (two_theirs,), (ours_first, *mine) = travel([(normed_two, swap)], own_rows)
    two = jnp.concatenate([normed_two, two_theirs], axis=0)
    mixed, grad_gate, grad_up, d_down = [None] * slices, [None] * slices, [None] * slices, [None] * slices
    rows_in = two_theirs
    for k in range(slices - 1, -1, -1):
        mixed[k], grad_gate[k], grad_up[k] = gated(rows_in, w_both[k], grad_mixed[k], 1, mine[3 * k : 3 * k + 3])
        if k > 0:
            d_down[k] = dot(grad_two, mixed[k], TN, BF16)
            rows_in = after(two_theirs, d_down[k])
    grads = grad_gate + grad_up
    d_up, d_gate = [None] * slices, [None] * slices

    def second_half(gate):
        return (
            spread([after(grads[0], gate)] + grads[1:], weights, 1, BF16, HIDES, 1, 2),
            *(dot(two, after(g, gate), TN, BF16) for g in grad_up[1:]),
        )

    def own_half(gate):
        return (spread([after(grads[0], gate)] + grads[1:], weights, 0, F32, HIDES, 1, 2),)

    theirs = spread(grads, weights, 1, BF16, HIDES, 0, 2)
    (from_first,), (theirs, *d_up[1:]) = travel([(theirs, swap)], second_half)
    (from_second,), (ours_second,) = travel([(theirs, swap)], own_half)
    grad_hidden, grad_hidden_low = norm_back(
        [(ours_first, 0, 1), (ours_second, 1, 1), (from_first, 0, 1), (from_second, 1, 1)], hidden, gain_two, cotangent, live, True
    )

    def owner_sum(partial):
        return lax.psum_scatter(partial, "dp", scatter_dimension=0, tiled=True)

    results, early = [], []

    def d_of(left, right, gate):
        return dot(left, after(right, gate), TN, BF16)

    def result_rows(part, out, gate, cost=HIDES):
        return spread([after(mixed[0], gate), *mixed[1:]], [(w, 0) for w in w_down], part, out, cost)

    def while_gather(step, gate):
        if step == 1:
            flops = 2 * rows * width * slices * gate_weight.shape[1]
            cost = pl.CostEstimate(flops=flops, transcendentals=0, bytes_accessed=flops // rows)
            return (result_rows(1, BF16, gate, cost), *(d_of(two, g, gate) for g in grad_gate[1:]))
        if step == 2:
            return (result_rows(0, F32, gate), d_of(two, grad_up[0], gate), *joined_sums())
        if step == n - 1:
            return (d_of(grad_two, mixed[0], gate), d_of(two, grad_gate[0], gate))
        return ()

    def took_gather(step, arrived, filled):
        early.extend(arrived)
        if step == 1:
            results.append(filled[0])
            d_gate[1:] = filled[1:]
        elif step == 2:
            results.append(filled[0])
            d_up[0] = filled[1]
            sums.extend(filled[2:])
        elif step == n - 1:
            d_down[0], d_gate[0] = filled

    sums = []

    def joined_sums():
        return [jnp.concatenate([owner_sum(a), owner_sum(b)], axis=1) for a, b in zip(d_down[1:], d_up[1:])]

    slots_back, grad_attended = line_gather(
        grad_hidden_low,
        n,
        lambda s, shard: dot(shard, w_out, NN, BF16),
        while_gather,
        lambda step: {
            2: [(results[0], partners[0])] if results else (),
            n - 1: to_owners(sums, 0),
        }.get(step, ()),
        took_gather,
    )
    result_ends, sum_ends = early[0], early[1:]

    def attention_back(gate):
        return (
            attend_back(after(slot_table, gate), *grad_attended, rotated, attended, lse, *tables),
            d_of(jnp.concatenate(slots_back, axis=0), attended, gate),
            sum_up,
        )

    sums_gate = [owner_sum(d) for d in d_gate[1:]]
    sum_down, sum_up, sum_gate = owner_sum(d_down[0]), owner_sum(d_up[0]), owner_sum(d_gate[0])
    leaving = [after(one, grad_attended[n - 1]) for one in sums_gate]
    back_gate, (grad_qkv, d_out, _) = travel(
        [(one, a + b) for one, (a, b) in zip(leaving, homeward)], attention_back
    )
    back_down, back_up, outputs, d_attention = [], [], [], []
    all_heads = own_qkv.shape[1]

    def columns(array, offset, size):
        return jnp.concatenate(
            [array[:, g * wide + offset : g * wide + offset + size] for g in range(heads_kv)], axis=1
        ).astype(F32)


    def while_reduce(step, gate):
        if step == 1:
            d_qkv = d_of(jnp.concatenate(slots_one, axis=0), grad_qkv, gate)
            return (jnp.concatenate([d_qkv, d_out], axis=1), sum_down)
        if step == 2:
            return (sum_gate,)
        if step == n - 1:
            from_partner = joined(result_ends, outputs[0])
            result = hidden + (results[1] + after(from_partner, gate).astype(F32))
            sum_attention = owner_sum(d_attention[0])
            return (
                (result * live).astype(BF16),
                turned(sum_attention, all_heads, out_weight.shape[0]),
                *(columns(sum_attention, *place) for place in ((0, qw), (qw, hd), (qw + hd, hd))),
                sum_attention,
            )
        return ()

    def along_reduce(step):
        if step == 1:
            return to_owners(sums, 1)
        if step == 2:
            return [(results[0], partners[1])]
        return ()

    def took_reduce(step, arrived, filled):
        if step == 1:
            for a, b in zip(sum_ends, arrived):
                back = joined(a, b)
                back_down.append(back[:, : down_t.shape[1]])
                back_up.append(back[:, down_t.shape[1] :])
            d_attention.append(filled[0])
        elif step == 2:
            outputs.extend(arrived)
        elif step == n - 1:
            outputs.extend(filled)

    def rows_part(s):
        if s == n - 1:
            return spread([grad_qkv], [(w_qkv, 0)], s, BF16, parts=n)
        return dot(grad_qkv[s * rows : (s + 1) * rows], w_qkv, NT, BF16)

    grad_normed_one = line_reduce(
        rows_part,
        n,
        while_reduce,
        along_reduce,
        took_reduce,
    )
    _, output, grad_out_w, grad_query_w, grad_key_w, grad_value_w, sum_attention = outputs

    def whole(first, back):
        return sum((one.astype(F32) for one in back), first.astype(F32))

    grad_down_w = whole(sum_down, back_down).T
    grad_gate_w = whole(sum_gate, back_gate)
    grad_up_w = whole(sum_up, back_up)
    grad_qkv_w = sum_attention[:, :all_heads].astype(F32)
    def along_row(weight, grad):
        return jnp.sum(weight.astype(F32) * grad, axis=1)

    gain_parts = jnp.stack(
        [
            along_row(own_qkv, grad_qkv_w),
            along_row(gate_weight, grad_gate_w) + along_row(up_weight, grad_up_w),
        ]
    )
    gain_own = lax.psum(gain_parts, "tensor") / jnp.stack([attn_gain, mlp_gain]).astype(F32)

    grad_tokens = norm_back([(term, 0, 2) for term in grad_normed_one], tokens, gain_one, grad_hidden, None, False)

    return (
        output,
        grad_tokens,
        grad_query_w,
        grad_key_w,
        grad_value_w,
        grad_out_w,
        gain_own[0],
        grad_gate_w,
        grad_up_w,
        grad_down_w,
        gain_own[1],
    )


def solution(mesh):
    rows = P(("dp", "tensor"), None)
    row = P(("dp", "tensor"))
    down_cols = P("tensor", "dp")
    cols = P("dp", "tensor")
    return jax.shard_map(
        shards,
        mesh=mesh,
        in_specs=(rows, rows, row, row, P("dp"), cols, cols, cols, down_cols, P("dp"), cols, cols, down_cols, P("dp")),
        out_specs=(rows, rows, cols, cols, cols, down_cols, P("dp"), cols, cols, down_cols, P("dp")),
        check_vma=False,
    )
```

```python
import functools
import math

import jax
import jax.numpy as jnp
import numpy as np
from jax import lax
from jax.experimental import pallas as pl
from jax.experimental.pallas import tpu as pltpu
from jax.sharding import PartitionSpec as P

HEAD_SIZE = 128
EPSILON = 1e-05
ROPE_BASE = 500000.0
MASKED = -1e30
F32 = jnp.float32
BF16 = jnp.bfloat16
NT = (((1,), (1,)), ((), ()))
NN = (((1,), (0,)), ((), ()))
TN = (((0,), (0,)), ((), ()))
HIDES = pl.CostEstimate(flops=1, transcendentals=0, bytes_accessed=1)


def dot(a, b, dims, out=F32):
    return lax.dot_general(a, b, dims, preferred_element_type=F32).astype(out)


def after(value, *others):
    return lax.optimization_barrier((value, *others))[0]


def arrival_order(n):
    return [
        [s for d in range(1, n) for s in (i - d, i + d) if 0 <= s < n]
        for i in range(n)
    ]


def pick(place, choices):
    distinct = []
    for value in choices:
        if not any(value is other for other in distinct):
            distinct.append(value)
    out = distinct[0]
    for value in distinct[1:]:
        here = functools.reduce(
            jnp.logical_or, [place == i for i, c in enumerate(choices) if c is value]
        )
        out = jnp.where(here, value, out)
    return out


def travel(items, work=lambda gate: ()):
    arrays = lax.optimization_barrier(tuple(array for array, _ in items))
    moved = [lax.ppermute(array, "tensor", pairs) for array, (_, pairs) in zip(arrays, items)]
    out = lax.optimization_barrier((*moved, *work(arrays[0])))
    return list(out[: len(moved)]), list(out[len(moved) :])


def line_gather(own, n, use, fill=lambda step, gate: (), along=lambda step: (), took=lambda step, arrived, filled: None):
    place = lax.axis_index("tensor")
    order = arrival_order(n)
    right = left = own
    from_left, from_right = [own], [own]
    slots, used = [own], []
    for d in range(1, n):

        def work(gate):
            return (use(d - 1, after(slots[d - 1], gate) if d > 1 else own), *fill(d, gate))

        (right, left, *more), (result, *filled) = travel(
            [
                (right, [(i, i + 1) for i in range(d - 1, n - 1)]),
                (left, [(i + 1, i) for i in range(n - d)]),
                *along(d),
            ],
            work,
        )
        used.append(result)
        took(d, more, filled)
        from_left.append(right)
        from_right.append(left)
        slots.append(
            pick(
                place,
                [
                    from_left[i - order[i][d - 1]] if order[i][d - 1] < i else from_right[order[i][d - 1] - i]
                    for i in range(n)
                ],
            )
        )
    used.append(use(n - 1, slots[-1]))
    return slots, used


def choose_kernel(count, which_ref, *refs):
    value = refs[0][...]
    for c in range(1, count):
        value = jnp.where(which_ref[0] == c, refs[c][...], value)
    total = value.astype(F32)
    for ref in refs[count:-1]:
        total = total + ref[...].astype(F32)
    refs[-1][...] = total.astype(BF16)


def chosen_sum(place, choices, sums):
    distinct = []
    for value in choices:
        if not any(value is other for other in distinct):
            distinct.append(value)
    table = [next(d for d, other in enumerate(distinct) if value is other) for value in choices]
    which = jnp.asarray(table, jnp.int32)[place][None]
    rows, width = choices[0].shape
    tile = 64 if rows % 64 == 0 else rows

    def candidate(c):
        return pl.BlockSpec((tile, width), lambda i, which: (jnp.where(which[0] == c, i, 0), 0))

    plain = pl.BlockSpec((tile, width), lambda i, which: (i, 0))
    return pl.pallas_call(
        functools.partial(choose_kernel, len(distinct)),
        grid_spec=pltpu.PrefetchScalarGridSpec(
            num_scalar_prefetch=1,
            grid=(rows // tile,),
            in_specs=[candidate(c) for c in range(len(distinct))] + [plain] * len(sums),
            out_specs=plain,
        ),
        out_shape=jax.ShapeDtypeStruct((rows, width), BF16),
        compiler_params=pltpu.CompilerParams(vmem_limit_bytes=30 << 20),
        cost_estimate=HIDES,
    )(which, *distinct, *sums)


def line_reduce(part, n, fill=lambda step, gate: (), along=lambda step: (), took=lambda step, arrived, filled: None):
    place = lax.axis_index("tensor")
    parts = [None] * n
    parts[n - 1] = lax.optimization_barrier(part(n - 1))
    order = [[i] + row for i, row in enumerate(arrival_order(n))]
    right = left = None

    def sent(k):
        ways = [order[i].index(i + n - k) for i in range(k)] + [order[i].index(i - n + k) for i in range(n - k, n)]
        return sorted(set(ways), reverse=True)

    def add(value, *sums):
        if right is None:
            return value
        return (value.astype(F32) + sum(one.astype(F32) for one in sums)).astype(BF16)

    for k in range(1, n):
        rightward = [parts[order[i].index(i + n - k)] if i < k else parts[n - k] for i in range(n)]
        leftward = [parts[order[i].index(i - n + k)] if i >= n - k else parts[n - k] for i in range(n)]
        if 2 * k <= n:
            choice = [r if i < k else l for i, (r, l) in enumerate(zip(rightward, leftward))]
            to_right = to_left = pick(place, choice) if right is None else chosen_sum(place, choice, (right, left))
        else:
            to_right, to_left = add(pick(place, rightward), right), add(pick(place, leftward), left)

        coming = [0] if k == n - 1 else [s for s in sent(k + 1) if parts[s] is None]

        def work(gate):
            return (*(part(s) for s in coming), *fill(k, gate))

        (right, left, *more), worked = travel(
            [
                (to_right, [(i, i + 1) for i in range(k)]),
                (to_left, [(n - 1 - i, n - 2 - i) for i in range(k)]),
                *along(k),
            ],
            work,
        )
        for s, one in zip(coming, worked):
            parts[s] = one
        took(k, more, worked[len(coming) :])
    return parts[0], right, left


def halves(n, pairs):
    ends = [(a, b) for a, b in pairs if a < n // 4 or a >= n - n // 4]
    return ends, [pair for pair in pairs if pair not in ends]


def joined(first, second):
    return first + second


def attend_forward(n, heads, rows, c, place_ref, *refs):
    chunks = refs[:n]
    cos_ref, sin_ref, qseg_ref, kseg_ref, o_ref, rot_ref, lse_ref, vt, acc, stat = refs[n:]
    hd = HEAD_SIZE
    kc, vc = heads * hd, (heads + 1) * hd
    for s in range(n):
        at = pl.ds(pl.multiple_of(place_ref[s] * rows, rows), rows)
        cos, sin = cos_ref[at, :], sin_ref[at, :]
        for h in range(heads + 1):
            u = chunks[s][:, h * hd : (h + 1) * hd]
            rot_ref[at, h * hd : (h + 1) * hd] = (u * cos + pltpu.roll(u, hd // 2, 1) * sin).astype(BF16)
        v = chunks[s][:, vc : vc + hd]
        rot_ref[at, vc : vc + hd] = v.astype(BF16)
        vt[:, at] = v.T.astype(BF16)

    def block(i, j, diagonal):
        qi = pl.ds(pl.multiple_of(i * rows, rows), rows)
        kj = pl.ds(pl.multiple_of(j * rows, rows), rows)
        k = rot_ref[kj, kc : kc + hd]
        allowed = kseg_ref[kj, :] == qseg_ref[:, qi]
        if diagonal:
            kr = lax.broadcasted_iota(jnp.int32, (rows, rows), 0)
            qr = lax.broadcasted_iota(jnp.int32, (rows, rows), 1)
            allowed = (allowed & (kr < qr)) | (kr == qr)
        for h in range(heads):
            q = rot_ref[qi, h * hd : (h + 1) * hd]
            scores = jnp.where(allowed, dot(k, q, NT) * c, MASKED)
            m = stat[h : h + 1, :]
            top = jnp.maximum(m, jnp.max(scores, axis=0, keepdims=True))
            p = jnp.exp2(scores - top)
            alpha = jnp.exp2(m - top)
            stat[h : h + 1, :] = top
            total = alpha * stat[8 + h : 9 + h, :] + jnp.sum(p, axis=0, keepdims=True)
            stat[8 + h : 9 + h, :] = total
            new = alpha * acc[h] + dot(vt[:, kj], p.astype(BF16), NN)
            if diagonal:
                at = pl.ds(pl.multiple_of(place_ref[n + i] * rows, rows), rows)
                o_ref[at, h * hd : (h + 1) * hd] = (new / total).T.astype(BF16)
                lse_ref[0, h : h + 1, qi] = top + jnp.log2(total)
            else:
                acc[h] = new

    @pl.loop(0, n)
    def _(i):
        stat[0:8, :] = jnp.full((8, rows), MASKED, F32)
        stat[8:16, :] = jnp.zeros((8, rows), F32)
        acc[...] = jnp.zeros_like(acc)

        @pl.loop(0, i)
        def _(j):
            block(i, j, False)

        block(i, i, True)


def attend_backward(n, heads, rows, c, place_ref, *refs):
    gas = refs[:n]
    rot_ref, o_ref, lse_ref, cos_ref, sin_ref, qseg_ref, kseg_ref, d_ref, go, dqt, delta, dk, dv, kt = refs[n:]
    hd = HEAD_SIZE
    scale = hd**-0.5
    kc, vc = heads * hd, (heads + 1) * hd
    for s in range(n):
        at = pl.ds(pl.multiple_of(place_ref[s] * rows, rows), rows)
        for h in range(heads):
            g = gas[s][:, h * hd : (h + 1) * hd]
            o = o_ref[s * rows : (s + 1) * rows, h * hd : (h + 1) * hd]
            go[at, h * hd : (h + 1) * hd] = g
            both = (g.astype(F32) * o.astype(F32)).T
            delta[h : h + 1, at] = jnp.sum(both, axis=0, keepdims=True)
        kt[:, at] = rot_ref[at, kc : kc + hd].astype(F32).T.astype(BF16)
    dqt[...] = jnp.zeros_like(dqt)

    def block(i, j, diagonal):
        qi = pl.ds(pl.multiple_of(i * rows, rows), rows)
        kj = pl.ds(pl.multiple_of(j * rows, rows), rows)
        k = rot_ref[kj, kc : kc + hd]
        v = rot_ref[kj, vc : vc + hd]
        allowed = kseg_ref[kj, :] == qseg_ref[:, qi]
        if diagonal:
            kr = lax.broadcasted_iota(jnp.int32, (rows, rows), 0)
            qr = lax.broadcasted_iota(jnp.int32, (rows, rows), 1)
            allowed = (allowed & (kr < qr)) | (kr == qr)
        for h in range(heads):
            cols = slice(h * hd, (h + 1) * hd)
            q = rot_ref[qi, cols]
            g = go[qi, cols]
            scores = jnp.where(allowed, dot(k, q, NT) * c, MASKED)
            p = jnp.exp2(scores - lse_ref[0, h : h + 1, qi])
            gp = dot(v, g, NT)
            ds = (p * (gp - delta[h : h + 1, qi])).astype(BF16)
            new_v = dot(p.astype(BF16), g, NN)
            new_k = dot(ds, q, NN)
            if diagonal and h == 0:
                dv[...] = new_v
                dk[...] = new_k
            else:
                dv[...] += new_v
                dk[...] += new_k
            dqt[h * hd : (h + 1) * hd, qi] += dot(kt[:, kj], ds, NN)

    def unrotate(u, at):
        return u * cos_ref[at, :] - pltpu.roll(u, hd // 2, 1) * sin_ref[at, :]

    @pl.loop(0, n)
    def _(j):
        block(j, j, True)

        @pl.loop(j + 1, n)
        def _(i):
            block(i, j, False)

        kj = pl.ds(pl.multiple_of(j * rows, rows), rows)
        to = pl.ds(pl.multiple_of(place_ref[n + j] * rows, rows), rows)
        for h in range(heads):
            u = dqt[h * hd : (h + 1) * hd, kj].T * scale
            d_ref[to, h * hd : (h + 1) * hd] = unrotate(u, kj).astype(BF16)
        d_ref[to, kc : kc + hd] = unrotate(dk[...] * scale, kj).astype(BF16)
        d_ref[to, vc : vc + hd] = dv[...].astype(BF16)


def attention_calls(n, rows, heads_q, heads_kv):
    heads = heads_q // heads_kv
    every = n * rows
    wide = (heads + 2) * HEAD_SIZE
    c = HEAD_SIZE**-0.5 * math.log2(math.e)
    whole = lambda shape: pl.BlockSpec(shape, lambda g, place: (0, 0))
    by_head = lambda r, w: pl.BlockSpec((r, w), lambda g, place: (0, g))
    tables = [
        whole((every, HEAD_SIZE)),
        whole((every, HEAD_SIZE)),
        whole((1, every)),
        whole((every, 1)),
    ]
    lse_spec = pl.BlockSpec((1, 8, every), lambda g, place: (g, 0, 0))
    pairs = every * every * heads_q
    params = pltpu.CompilerParams(vmem_limit_bytes=58 << 20)
    forward = pl.pallas_call(
        functools.partial(attend_forward, n, heads, rows, c),
        grid_spec=pltpu.PrefetchScalarGridSpec(
            num_scalar_prefetch=1,
            grid=(heads_kv,),
            in_specs=[by_head(rows, wide)] * n + tables,
            out_specs=[by_head(every, heads * HEAD_SIZE), by_head(every, wide), lse_spec],
            scratch_shapes=[
                pltpu.VMEM((HEAD_SIZE, every), BF16),
                pltpu.VMEM((heads, HEAD_SIZE, rows), F32),
                pltpu.VMEM((16, rows), F32),
            ],
        ),
        out_shape=[
            jax.ShapeDtypeStruct((every, heads_q * HEAD_SIZE), BF16),
            jax.ShapeDtypeStruct((every, heads_kv * wide), BF16),
            jax.ShapeDtypeStruct((heads_kv, 8, every), F32),
        ],
        compiler_params=params,
        cost_estimate=HIDES,
    )
    backward = pl.pallas_call(
        functools.partial(attend_backward, n, heads, rows, c),
        grid_spec=pltpu.PrefetchScalarGridSpec(
            num_scalar_prefetch=1,
            grid=(heads_kv,),
            in_specs=[by_head(rows, heads * HEAD_SIZE)] * n
            + [by_head(every, wide), by_head(every, heads * HEAD_SIZE), lse_spec]
            + tables,
            out_specs=by_head(every, wide),
            scratch_shapes=[
                pltpu.VMEM((every, heads * HEAD_SIZE), BF16),
                pltpu.VMEM((heads * HEAD_SIZE, every), F32),
                pltpu.VMEM((8, every), F32),
                pltpu.VMEM((rows, HEAD_SIZE), F32),
                pltpu.VMEM((rows, HEAD_SIZE), F32),
                pltpu.VMEM((HEAD_SIZE, every), BF16),
            ],
        ),
        out_shape=jax.ShapeDtypeStruct((every, heads_kv * wide), BF16),
        compiler_params=params,
        cost_estimate=pl.CostEstimate(flops=pairs * 10 * HEAD_SIZE, transcendentals=pairs, bytes_accessed=every * wide * 20),
    )
    return forward, backward


def gated_kernel(x_ref, gate_ref, up_ref, gm_ref, *refs):
    mixed_ref, dg_ref, du_ref = refs[-3:]
    x = x_ref[...]
    step = 256 if mixed_ref.shape[1] % 256 == 0 else mixed_ref.shape[1]
    for c in range(0, mixed_ref.shape[1], step):
        at = slice(c, c + step)
        gate = dot(x, gate_ref[:, at], NN)
        up = dot(x, up_ref[:, at], NN)
        gm = gm_ref[:, at]
        sig = 1.0 / (1.0 + jnp.exp(-gate))
        act = gate * sig
        mixed_ref[:, at] = (act * up).astype(BF16)
        du_ref[:, at] = (gm * act).astype(BF16)
        dg_ref[:, at] = (gm * up * sig * (1.0 + gate * (1.0 - sig))).astype(BF16)


def gated(x, w_both, gm, part, before=None):
    rows, width = x.shape
    hidden = w_both.shape[1] // 2
    tile = 512 if hidden % 512 == 0 else hidden
    tiles = hidden // tile
    weight = [pl.BlockSpec((width, tile), lambda j: (0, j)), pl.BlockSpec((width, tile), lambda j: (0, j + tiles))]
    here = pl.BlockSpec((rows, tile), lambda j: (part, j))
    before = () if before is None else tuple(before)
    return pl.pallas_call(
        gated_kernel,
        grid=(tiles,),
        in_specs=[pl.BlockSpec((rows, width), lambda j: (0, 0)), *weight, here]
        + [pl.BlockSpec(memory_space=pl.ANY)] * len(before),
        out_specs=[here] * 3,
        out_shape=[jax.ShapeDtypeStruct((2 * rows, hidden), BF16)] * 3,
        input_output_aliases={4 + i: i for i in range(len(before))},
        compiler_params=pltpu.CompilerParams(vmem_limit_bytes=50 << 20),
        cost_estimate=HIDES,
    )(x, w_both, w_both, gm, *before)


def spread_kernel(count, *refs):
    total = None
    for a_ref, w_ref in zip(refs[:count], refs[count : 2 * count]):
        term = lax.dot_general(a_ref[...], w_ref[...], NT, preferred_element_type=F32)
        total = term if total is None else total + term
    refs[-1][...] = total.astype(refs[-1].dtype)


def spread(acts, weights, part, out, cost=HIDES, piece=0, pieces=1):
    rows, hidden = acts[0].shape[0] // 2, acts[0].shape[1]
    width = weights[0][0].shape[0] // pieces
    tile = 256 if width % 256 == 0 else width
    tiles = width // tile
    count = len(acts)

    def column_block(which):
        return pl.BlockSpec((tile, hidden), lambda j: (j + piece * tiles, which))

    return pl.pallas_call(
        functools.partial(spread_kernel, count),
        grid=(tiles,),
        in_specs=[pl.BlockSpec((rows, hidden), lambda j: (part, 0))] * count
        + [column_block(which) for _, which in weights],
        out_specs=pl.BlockSpec((rows, tile), lambda j: (0, j)),
        out_shape=jax.ShapeDtypeStruct((rows, width), out),
        compiler_params=pltpu.CompilerParams(vmem_limit_bytes=50 << 20),
        cost_estimate=cost,
    )(*acts, *[array for array, _ in weights])


def norm_inverse(source):
    return lax.rsqrt(jnp.mean(source * source, axis=-1, keepdims=True) + EPSILON)


def norm_back_kernel(places, masked, gain_ref, source_ref, straight_ref, *refs):
    grads, refs = refs[: len(places)], refs[len(places) :]
    source = source_ref[...].astype(F32)
    width = source.shape[1]
    inverse = lax.rsqrt(jnp.mean(source * source, axis=-1, keepdims=True) + EPSILON)
    pieces = []
    for half in range(2):
        at = slice(half * width // 2, (half + 1) * width // 2)
        terms = [
            ref[:, at] if count == 2 else ref[...]
            for ref, (first, count) in zip(grads, places)
            if first <= half < first + count
        ]
        pieces.append(sum(term.astype(F32) for term in terms))
    scaled = jnp.concatenate(pieces, axis=1) * gain_ref[...]
    unit_rows = source * inverse
    grad = inverse * (scaled - unit_rows * jnp.mean(scaled * unit_rows, axis=-1, keepdims=True))
    straight = straight_ref[...].astype(F32)
    if masked:
        straight = straight * refs[0][...]
    total = straight + grad
    if masked:
        refs[1][...] = total
        refs[2][...] = total.astype(BF16)
    else:
        refs[0][...] = total


def norm_back(grads, source, gain, straight, mask, low):
    rows, width = source.shape
    tile = 32 if rows % 32 == 0 else rows
    block = lambda wide: pl.BlockSpec((tile, wide), lambda i: (i, 0))
    masked = mask is not None
    out_shape = [jax.ShapeDtypeStruct((rows, width), F32)] + [jax.ShapeDtypeStruct((rows, width), BF16)] * low
    return pl.pallas_call(
        functools.partial(norm_back_kernel, [place for _, *place in grads], masked),
        grid=(rows // tile,),
        in_specs=[pl.BlockSpec((1, width), lambda i: (0, 0)), block(width), block(width)]
        + [block(array.shape[1]) for array, _, _ in grads]
        + [block(1)] * masked,
        out_specs=[block(width)] * len(out_shape) if low else block(width),
        out_shape=out_shape if low else out_shape[0],
        compiler_params=pltpu.CompilerParams(vmem_limit_bytes=40 << 20),
        cost_estimate=HIDES,
    )(gain[None, :], source, straight, *[array for array, _, _ in grads], *([mask] if masked else []))


def turn_kernel(x_ref, o_ref):
    o_ref[...] = x_ref[...].astype(F32).T


def turned(array, first, size):
    rows = array.shape[0]
    return pl.pallas_call(
        turn_kernel,
        grid=(size // HEAD_SIZE,),
        in_specs=[pl.BlockSpec((rows, HEAD_SIZE), lambda j: (0, j + first // HEAD_SIZE))],
        out_specs=pl.BlockSpec((HEAD_SIZE, rows), lambda j: (j, 0)),
        out_shape=jax.ShapeDtypeStruct((size, rows), F32),
        cost_estimate=HIDES,
    )(array)


def shards(
    tokens,
    cotangent,
    segments,
    positions,
    counts,
    query_weight,
    key_projection_weight,
    value_projection_weight,
    out_weight,
    attn_gain,
    gate_weight,
    up_weight,
    down_weight,
    mlp_gain,
):
    n = lax.axis_size("tensor")
    place = lax.axis_index("tensor")
    rows, width = tokens.shape
    every = rows * n
    heads_q = query_weight.shape[1] // HEAD_SIZE
    heads_kv = key_projection_weight.shape[1] // HEAD_SIZE
    heads = heads_q // heads_kv
    qw, hd = heads * HEAD_SIZE, HEAD_SIZE
    wide = qw + 2 * hd
    slices = n // 2

    def gather(shard):
        return lax.all_gather(shard, "dp", axis=0, tiled=True)

    partners = halves(n, [(i, i ^ 1) for i in range(n)])
    outward = [halves(n, [((i + 2 * k) % n, i) for i in range(n)]) for k in range(1, slices)]
    homeward = [halves(n, [(i, (i + 2 * k) % n) for i in range(n)]) for k in range(1, slices)]

    def to_others(shard, half):
        return [(shard, pairs[half]) for pairs in outward]

    def to_owners(sums, half):
        return [(one, pairs[half]) for one, pairs in zip(sums, homeward)]

    live_count = counts[0]
    own_index = place * rows + jnp.arange(rows, dtype=jnp.int32)
    live = (own_index < live_count).astype(F32)[:, None]
    labels = lax.all_gather(jnp.stack([segments, positions]), "tensor", axis=1, tiled=True)
    seg_all, place_all = labels[0], labels[1]
    index_all = jnp.arange(every, dtype=jnp.int32)
    key_seg = jnp.where(index_all < live_count, seg_all, -1)[:, None]
    query_seg = seg_all[None, :]
    freqs = ROPE_BASE ** (-(jnp.arange(hd // 2, dtype=F32) * 2.0) / hd)
    angles = place_all.astype(F32)[:, None] * freqs[None, :]
    cos, sin = jnp.cos(angles), jnp.sin(angles)
    cos = jnp.concatenate([cos, cos], axis=1)
    sin = jnp.concatenate([-sin, sin], axis=1)
    order = np.array([[i] + row for i, row in enumerate(arrival_order(n))], np.int32)
    where_is = np.argsort(order, axis=1).astype(np.int32)
    slot_table = jnp.asarray(np.concatenate([order, where_is], axis=1))[place]
    attend, attend_back = attention_calls(n, rows, heads_q, heads_kv)
    tables = (cos, sin, query_seg, key_seg)

    gains = lax.all_gather(jnp.stack([attn_gain, mlp_gain]), "dp", axis=1, tiled=True).astype(F32)
    gain_one, gain_two = gains[0], gains[1]

    source = tokens.astype(F32)
    inv_one = norm_inverse(source)
    normed_one = (source * inv_one * gain_one).astype(BF16)

    def attention_weights(gate):
        query, key, value = lax.optimization_barrier((query_weight, key_projection_weight, value_projection_weight, gate))[:3]
        return jnp.concatenate(
            [
                part
                for g in range(heads_kv)
                for part in (
                    query[:, g * qw : (g + 1) * qw],
                    key[:, g * hd : (g + 1) * hd],
                    value[:, g * hd : (g + 1) * hd],
                )
            ],
            axis=1,
        )

    own_qkv = attention_weights(normed_one)
    w_qkv = gather(own_qkv)
    shards_here, early = [], []

    def shard_layouts(step, gate):
        if step != 1:
            return ()
        both = jnp.concatenate([after(gate_weight, gate), up_weight], axis=1)
        masked = (after(cotangent, gate).astype(F32) * live).astype(BF16)
        return (after(out_weight, gate).T, after(down_weight, gate).T, both, masked, *tables)

    def took_rows(step, arrived, filled):
        early.extend(arrived)
        if step == 1:
            shards_here.extend(filled[:4])

    more = slices - 1
    slots_one, projected = line_gather(
        after(normed_one, labels),
        n,
        lambda s, shard: dot(shard, w_qkv, NN),
        shard_layouts,
        lambda step: {
            n - 2: [(shards_here[3], partners[0])] if shards_here else (),
            n - 1: to_others(shards_here[2], 0) if shards_here else (),
        }.get(step, ()),
        took_rows,
    )
    low_ends, both_ends = early[0], early[1:]
    out_t, down_t, both_weight, grad_low = shards_here
    w_out, w_down, w_both = gather(out_t), [gather(down_t)], [gather(both_weight)]
    projected[n - 1] = after(projected[n - 1], w_out, w_down[0])

    def attention(gate):
        return attend(slot_table, *projected, *tables)

    downs = after(down_t, projected[n - 1])
    moved, (attended, rotated, lse) = travel([(downs, a + b) for a, b in outward], attention)
    w_down += [gather(shard) for shard in moved]
    grad_mixed, lows = [], []

    def while_out(step, gate):
        if step == 1:
            return (w_both[0],)
        if step == n - 1:
            theirs = joined(low_ends, lows[0])
            lows.append(theirs)
            return tuple(dot(jnp.concatenate([grad_low, theirs], axis=0), w, NN) for w in w_down)
        return ()

    def along_out(step):
        if step == 1:
            return to_others(both_weight, 1)
        if step == 2:
            return [(grad_low, partners[1])]
        return ()

    def took_out(step, arrived, filled):
        if step == 1:
            for a, b, (by_ends, _) in zip(both_ends, arrived, outward):
                choice = [a if any(i == to for _, to in by_ends) else b for i in range(n)]
                w_both.append(gather(chosen_sum(place, choice, ())))
        elif step == n - 1:
            grad_mixed.extend(filled)
        else:
            lows.extend(arrived)

    summed = line_reduce(
        lambda s: dot(attended[s * rows : (s + 1) * rows], w_out, NT, BF16), n, while_out, along_out, took_out
    )
    hidden = source + sum(term.astype(F32) for term in summed)
    grad_two = jnp.concatenate([grad_low, lows[1]], axis=0)

    inv_two = norm_inverse(hidden)
    normed_two = (hidden * inv_two * gain_two).astype(BF16)

    def own_rows(gate):
        made = [one for w, gm in zip(w_both, grad_mixed) for one in gated(gate, w, gm, 0)]
        return [spread(made[1::3] + made[2::3], weights, 0, F32, HIDES, 0, 2), *made]

    swap = partners[0] + partners[1]
    weights = [(w, 0) for w in w_both] + [(w, 1) for w in w_both]
    (two_theirs,), (ours_first, *mine) = travel([(normed_two, swap)], own_rows)
    two = jnp.concatenate([normed_two, two_theirs], axis=0)
    mixed, grad_gate, grad_up, d_down = [None] * slices, [None] * slices, [None] * slices, [None] * slices
    rows_in = two_theirs
    for k in range(slices - 1, -1, -1):
        mixed[k], grad_gate[k], grad_up[k] = gated(rows_in, w_both[k], grad_mixed[k], 1, mine[3 * k : 3 * k + 3])
        if k > 0:
            d_down[k] = dot(grad_two, mixed[k], TN, BF16)
            rows_in = after(two_theirs, d_down[k])
    grads = grad_gate + grad_up
    d_up, d_gate = [None] * slices, [None] * slices

    def second_half(gate):
        return (
            spread([after(grads[0], gate)] + grads[1:], weights, 1, BF16, HIDES, 1, 2),
            *(dot(two, after(g, gate), TN, BF16) for g in grad_up[1:]),
        )

    def gate_weights(gate):
        return (
            spread([after(grads[0], gate)] + grads[1:], weights, 0, F32, HIDES, 1, 2),
            *(dot(two, after(g, gate), TN, BF16) for g in grad_gate[1:]),
        )

    theirs = spread(grads, weights, 1, BF16, HIDES, 0, 2)
    (from_first,), (theirs, *d_up[1:]) = travel([(theirs, swap)], second_half)
    (from_second,), (ours_second, *d_gate[1:]) = travel([(theirs, swap)], gate_weights)
    grad_hidden, grad_hidden_low = norm_back(
        [(ours_first, 0, 1), (ours_second, 1, 1), (from_first, 0, 1), (from_second, 1, 1)], hidden, gain_two, cotangent, live, True
    )

    def owner_sum(partial):
        return lax.psum_scatter(partial, "dp", scatter_dimension=0, tiled=True)

    results, early = [], []

    def d_of(left, right, gate):
        return dot(left, after(right, gate), TN, BF16)

    def result_rows(part, out, gate, cost=HIDES):
        return spread([after(mixed[0], gate), *mixed[1:]], [(w, 0) for w in w_down], part, out, cost)

    def while_gather(step, gate):
        if step == 1:
            flops = 2 * rows * width * slices * gate_weight.shape[1]
            cost = pl.CostEstimate(flops=flops, transcendentals=0, bytes_accessed=flops // rows)
            return (result_rows(1, BF16, gate, cost), d_of(grad_two, mixed[0], gate))
        if step == 2:
            return (result_rows(0, F32, gate), d_of(two, grad_up[0], gate), *joined_sums())
        if step == n - 1:
            return (d_of(two, grad_gate[0], gate),)
        return ()

    def took_gather(step, arrived, filled):
        early.extend(arrived)
        if step == 1:
            results.append(filled[0])
            d_down[0] = filled[1]
        elif step == 2:
            results.append(filled[0])
            d_up[0] = filled[1]
            sums.extend(filled[2:])
        elif step == n - 1:
            d_gate[0] = filled[0]

    sums = []

    def joined_sums():
        return [jnp.concatenate([owner_sum(a), owner_sum(b)], axis=1) for a, b in zip(d_down[1:], d_up[1:])]

    slots_back, grad_attended = line_gather(
        grad_hidden_low,
        n,
        lambda s, shard: dot(shard, w_out, NN, BF16),
        while_gather,
        lambda step: {
            2: [(results[0], partners[0])] if results else (),
            n - 1: to_owners(sums, 0),
        }.get(step, ()),
        took_gather,
    )
    result_ends, sum_ends = early[0], early[1:]

    def attention_back(gate):
        return (
            attend_back(after(slot_table, gate), *grad_attended, rotated, attended, lse, *tables),
            d_of(jnp.concatenate(slots_back, axis=0), attended, gate),
            sum_down,
        )

    sums_gate = [owner_sum(d) for d in d_gate[1:]]
    sum_down, sum_up, sum_gate = owner_sum(d_down[0]), owner_sum(d_up[0]), owner_sum(d_gate[0])
    leaving = [after(one, grad_attended[n - 1]) for one in sums_gate]
    back_gate, (grad_qkv, d_out, _) = travel(
        [(one, a + b) for one, (a, b) in zip(leaving, homeward)], attention_back
    )
    back_down, back_up, outputs, d_attention = [], [], [], []
    all_heads = own_qkv.shape[1]

    def columns(array, offset, size):
        return jnp.concatenate(
            [array[:, g * wide + offset : g * wide + offset + size] for g in range(heads_kv)], axis=1
        ).astype(F32)


    def while_reduce(step, gate):
        if step == 1:
            d_qkv = d_of(jnp.concatenate(slots_one, axis=0), grad_qkv, gate)
            return (jnp.concatenate([d_qkv, d_out], axis=1), sum_up)
        if step == 2:
            return (sum_gate,)
        if step == n - 1:
            from_partner = joined(result_ends, outputs[0])
            result = hidden + (results[1] + after(from_partner, gate).astype(F32))
            sum_attention = owner_sum(d_attention[0])
            return (
                (result * live).astype(BF16),
                turned(sum_attention, all_heads, out_weight.shape[0]),
                *(columns(sum_attention, *place) for place in ((0, qw), (qw, hd), (qw + hd, hd))),
                sum_attention,
            )
        return ()

    def along_reduce(step):
        if step == 1:
            return to_owners(sums, 1)
        if step == 2:
            return [(results[0], partners[1])]
        return ()

    def took_reduce(step, arrived, filled):
        if step == 1:
            for a, b in zip(sum_ends, arrived):
                back = joined(a, b)
                back_down.append(back[:, : down_t.shape[1]])
                back_up.append(back[:, down_t.shape[1] :])
            d_attention.append(filled[0])
        elif step == 2:
            outputs.extend(arrived)
        elif step == n - 1:
            outputs.extend(filled)

    grad_normed_one = line_reduce(
        lambda s: dot(grad_qkv[s * rows : (s + 1) * rows], w_qkv, NT, BF16),
        n,
        while_reduce,
        along_reduce,
        took_reduce,
    )
    _, output, grad_out_w, grad_query_w, grad_key_w, grad_value_w, sum_attention = outputs

    def whole(first, back):
        return sum((one.astype(F32) for one in back), first.astype(F32))

    grad_down_w = whole(sum_down, back_down).T
    grad_gate_w = whole(sum_gate, back_gate)
    grad_up_w = whole(sum_up, back_up)
    grad_qkv_w = sum_attention[:, :all_heads].astype(F32)
    def along_row(weight, grad):
        return jnp.sum(weight.astype(F32) * grad, axis=1)

    gain_parts = jnp.stack(
        [
            along_row(own_qkv, grad_qkv_w),
            along_row(gate_weight, grad_gate_w) + along_row(up_weight, grad_up_w),
        ]
    )
    gain_own = lax.psum(gain_parts, "tensor") / jnp.stack([attn_gain, mlp_gain]).astype(F32)

    grad_tokens = norm_back([(term, 0, 2) for term in grad_normed_one], tokens, gain_one, grad_hidden, None, False)

    return (
        output,
        grad_tokens,
        grad_query_w,
        grad_key_w,
        grad_value_w,
        grad_out_w,
        gain_own[0],
        grad_gate_w,
        grad_up_w,
        grad_down_w,
        gain_own[1],
    )


def solution(mesh):
    rows = P(("dp", "tensor"), None)
    row = P(("dp", "tensor"))
    down_cols = P("tensor", "dp")
    cols = P("dp", "tensor")
    return jax.shard_map(
        shards,
        mesh=mesh,
        in_specs=(rows, rows, row, row, P("dp"), cols, cols, cols, down_cols, P("dp"), cols, cols, down_cols, P("dp")),
        out_specs=(rows, rows, cols, cols, cols, down_cols, P("dp"), cols, cols, down_cols, P("dp")),
        check_vma=False,
    )
```

```python
import functools
import math

import jax
import jax.numpy as jnp
import numpy as np
from jax import lax
from jax.experimental import pallas as pl
from jax.experimental.pallas import tpu as pltpu
from jax.sharding import PartitionSpec as P

HEAD_SIZE = 128
EPSILON = 1e-05
ROPE_BASE = 500000.0
MASKED = -1e30
F32 = jnp.float32
BF16 = jnp.bfloat16
NT = (((1,), (1,)), ((), ()))
NN = (((1,), (0,)), ((), ()))
TN = (((0,), (0,)), ((), ()))
HIDES = pl.CostEstimate(flops=1, transcendentals=0, bytes_accessed=1)


def dot(a, b, dims, out=F32):
    return lax.dot_general(a, b, dims, preferred_element_type=F32).astype(out)


def after(value, *others):
    return lax.optimization_barrier((value, *others))[0]


def arrival_order(n):
    return [
        [s for d in range(1, n) for s in (i - d, i + d) if 0 <= s < n]
        for i in range(n)
    ]


def pick(place, choices):
    distinct = []
    for value in choices:
        if not any(value is other for other in distinct):
            distinct.append(value)
    out = distinct[0]
    for value in distinct[1:]:
        here = functools.reduce(
            jnp.logical_or, [place == i for i, c in enumerate(choices) if c is value]
        )
        out = jnp.where(here, value, out)
    return out


def travel(items, work=lambda gate: ()):
    arrays = lax.optimization_barrier(tuple(array for array, _ in items))
    moved = [lax.ppermute(array, "tensor", pairs) for array, (_, pairs) in zip(arrays, items)]
    out = lax.optimization_barrier((*moved, *work(arrays[0])))
    return list(out[: len(moved)]), list(out[len(moved) :])


def line_gather(own, n, use, fill=lambda step, gate: (), along=lambda step: (), took=lambda step, arrived, filled: None):
    place = lax.axis_index("tensor")
    order = arrival_order(n)
    right = left = own
    from_left, from_right = [own], [own]
    slots, used = [own], []
    for d in range(1, n):

        def work(gate):
            return (use(d - 1, after(slots[d - 1], gate) if d > 1 else own), *fill(d, gate))

        (right, left, *more), (result, *filled) = travel(
            [
                (right, [(i, i + 1) for i in range(d - 1, n - 1)]),
                (left, [(i + 1, i) for i in range(n - d)]),
                *along(d),
            ],
            work,
        )
        used.append(result)
        took(d, more, filled)
        from_left.append(right)
        from_right.append(left)
        slots.append(
            pick(
                place,
                [
                    from_left[i - order[i][d - 1]] if order[i][d - 1] < i else from_right[order[i][d - 1] - i]
                    for i in range(n)
                ],
            )
        )
    used.append(use(n - 1, slots[-1]))
    return slots, used


def line_reduce(part, n, fill=lambda step, gate: (), along=lambda step: (), took=lambda step, arrived, filled: None):
    place = lax.axis_index("tensor")
    parts = [None] * n
    parts[n - 1] = lax.optimization_barrier(part(n - 1))
    order = [[i] + row for i, row in enumerate(arrival_order(n))]
    right = left = None

    def sent(k):
        ways = [order[i].index(i + n - k) for i in range(k)] + [order[i].index(i - n + k) for i in range(n - k, n)]
        return sorted(set(ways), reverse=True)

    def add(value, *sums):
        if right is None:
            return value
        return (value.astype(F32) + sum(one.astype(F32) for one in sums)).astype(BF16)

    for k in range(1, n):
        rightward = [parts[order[i].index(i + n - k)] if i < k else parts[n - k] for i in range(n)]
        leftward = [parts[order[i].index(i - n + k)] if i >= n - k else parts[n - k] for i in range(n)]
        if 2 * k <= n:
            choice = [r if i < k else l for i, (r, l) in enumerate(zip(rightward, leftward))]
            to_right = to_left = add(pick(place, choice), right, left)
        else:
            to_right, to_left = add(pick(place, rightward), right), add(pick(place, leftward), left)

        coming = [0] if k == n - 1 else [s for s in sent(k + 1) if parts[s] is None]

        def work(gate):
            return (*(part(s) for s in coming), *fill(k, gate))

        (right, left, *more), worked = travel(
            [
                (to_right, [(i, i + 1) for i in range(k)]),
                (to_left, [(n - 1 - i, n - 2 - i) for i in range(k)]),
                *along(k),
            ],
            work,
        )
        for s, one in zip(coming, worked):
            parts[s] = one
        took(k, more, worked[len(coming) :])
    return parts[0], right, left


def halves(n, pairs):
    ends = [(a, b) for a, b in pairs if a < n // 4 or a >= n - n // 4]
    return ends, [pair for pair in pairs if pair not in ends]


def joined(first, second):
    return first + second


def attend_forward(n, heads, rows, c, place_ref, *refs):
    chunks = refs[:n]
    cos_ref, sin_ref, qseg_ref, kseg_ref, o_ref, rot_ref, lse_ref, vt, acc, stat = refs[n:]
    hd = HEAD_SIZE
    kc, vc = heads * hd, (heads + 1) * hd
    for s in range(n):
        at = pl.ds(pl.multiple_of(place_ref[s] * rows, rows), rows)
        cos, sin = cos_ref[at, :], sin_ref[at, :]
        for h in range(heads + 1):
            u = chunks[s][:, h * hd : (h + 1) * hd]
            rot_ref[at, h * hd : (h + 1) * hd] = (u * cos + pltpu.roll(u, hd // 2, 1) * sin).astype(BF16)
        v = chunks[s][:, vc : vc + hd]
        rot_ref[at, vc : vc + hd] = v.astype(BF16)
        vt[:, at] = v.T.astype(BF16)

    def block(i, j, diagonal):
        qi = pl.ds(pl.multiple_of(i * rows, rows), rows)
        kj = pl.ds(pl.multiple_of(j * rows, rows), rows)
        k = rot_ref[kj, kc : kc + hd]
        allowed = kseg_ref[kj, :] == qseg_ref[:, qi]
        if diagonal:
            kr = lax.broadcasted_iota(jnp.int32, (rows, rows), 0)
            qr = lax.broadcasted_iota(jnp.int32, (rows, rows), 1)
            allowed = (allowed & (kr < qr)) | (kr == qr)
        for h in range(heads):
            q = rot_ref[qi, h * hd : (h + 1) * hd]
            scores = jnp.where(allowed, dot(k, q, NT) * c, MASKED)
            m = stat[h : h + 1, :]
            top = jnp.maximum(m, jnp.max(scores, axis=0, keepdims=True))
            p = jnp.exp2(scores - top)
            alpha = jnp.exp2(m - top)
            stat[h : h + 1, :] = top
            total = alpha * stat[8 + h : 9 + h, :] + jnp.sum(p, axis=0, keepdims=True)
            stat[8 + h : 9 + h, :] = total
            new = alpha * acc[h] + dot(vt[:, kj], p.astype(BF16), NN)
            if diagonal:
                at = pl.ds(pl.multiple_of(place_ref[n + i] * rows, rows), rows)
                o_ref[at, h * hd : (h + 1) * hd] = (new / total).T.astype(BF16)
                lse_ref[0, h : h + 1, qi] = top + jnp.log2(total)
            else:
                acc[h] = new

    @pl.loop(0, n)
    def _(i):
        stat[0:8, :] = jnp.full((8, rows), MASKED, F32)
        stat[8:16, :] = jnp.zeros((8, rows), F32)
        acc[...] = jnp.zeros_like(acc)

        @pl.loop(0, i)
        def _(j):
            block(i, j, False)

        block(i, i, True)


def attend_backward(n, heads, rows, c, place_ref, *refs):
    gas = refs[:n]
    rot_ref, o_ref, lse_ref, cos_ref, sin_ref, qseg_ref, kseg_ref, d_ref, go, dqt, delta, dk, dv, kt = refs[n:]
    hd = HEAD_SIZE
    scale = hd**-0.5
    kc, vc = heads * hd, (heads + 1) * hd
    for s in range(n):
        at = pl.ds(pl.multiple_of(place_ref[s] * rows, rows), rows)
        for h in range(heads):
            g = gas[s][:, h * hd : (h + 1) * hd]
            o = o_ref[s * rows : (s + 1) * rows, h * hd : (h + 1) * hd]
            go[at, h * hd : (h + 1) * hd] = g
            both = (g.astype(F32) * o.astype(F32)).T
            delta[h : h + 1, at] = jnp.sum(both, axis=0, keepdims=True)
        kt[:, at] = rot_ref[at, kc : kc + hd].astype(F32).T.astype(BF16)
    dqt[...] = jnp.zeros_like(dqt)

    def block(i, j, diagonal):
        qi = pl.ds(pl.multiple_of(i * rows, rows), rows)
        kj = pl.ds(pl.multiple_of(j * rows, rows), rows)
        k = rot_ref[kj, kc : kc + hd]
        v = rot_ref[kj, vc : vc + hd]
        allowed = kseg_ref[kj, :] == qseg_ref[:, qi]
        if diagonal:
            kr = lax.broadcasted_iota(jnp.int32, (rows, rows), 0)
            qr = lax.broadcasted_iota(jnp.int32, (rows, rows), 1)
            allowed = (allowed & (kr < qr)) | (kr == qr)
        for h in range(heads):
            cols = slice(h * hd, (h + 1) * hd)
            q = rot_ref[qi, cols]
            g = go[qi, cols]
            scores = jnp.where(allowed, dot(k, q, NT) * c, MASKED)
            p = jnp.exp2(scores - lse_ref[0, h : h + 1, qi])
            gp = dot(v, g, NT)
            ds = (p * (gp - delta[h : h + 1, qi])).astype(BF16)
            new_v = dot(p.astype(BF16), g, NN)
            new_k = dot(ds, q, NN)
            if diagonal and h == 0:
                dv[...] = new_v
                dk[...] = new_k
            else:
                dv[...] += new_v
                dk[...] += new_k
            dqt[h * hd : (h + 1) * hd, qi] += dot(kt[:, kj], ds, NN)

    def unrotate(u, at):
        return u * cos_ref[at, :] - pltpu.roll(u, hd // 2, 1) * sin_ref[at, :]

    @pl.loop(0, n)
    def _(j):
        block(j, j, True)

        @pl.loop(j + 1, n)
        def _(i):
            block(i, j, False)

        kj = pl.ds(pl.multiple_of(j * rows, rows), rows)
        to = pl.ds(pl.multiple_of(place_ref[n + j] * rows, rows), rows)
        for h in range(heads):
            u = dqt[h * hd : (h + 1) * hd, kj].T * scale
            d_ref[to, h * hd : (h + 1) * hd] = unrotate(u, kj).astype(BF16)
        d_ref[to, kc : kc + hd] = unrotate(dk[...] * scale, kj).astype(BF16)
        d_ref[to, vc : vc + hd] = dv[...].astype(BF16)


def attention_calls(n, rows, heads_q, heads_kv):
    heads = heads_q // heads_kv
    every = n * rows
    wide = (heads + 2) * HEAD_SIZE
    c = HEAD_SIZE**-0.5 * math.log2(math.e)
    whole = lambda shape: pl.BlockSpec(shape, lambda g, place: (0, 0))
    by_head = lambda r, w: pl.BlockSpec((r, w), lambda g, place: (0, g))
    tables = [
        whole((every, HEAD_SIZE)),
        whole((every, HEAD_SIZE)),
        whole((1, every)),
        whole((every, 1)),
    ]
    lse_spec = pl.BlockSpec((1, 8, every), lambda g, place: (g, 0, 0))
    pairs = every * every * heads_q
    params = pltpu.CompilerParams(vmem_limit_bytes=58 << 20)
    forward = pl.pallas_call(
        functools.partial(attend_forward, n, heads, rows, c),
        grid_spec=pltpu.PrefetchScalarGridSpec(
            num_scalar_prefetch=1,
            grid=(heads_kv,),
            in_specs=[by_head(rows, wide)] * n + tables,
            out_specs=[by_head(every, heads * HEAD_SIZE), by_head(every, wide), lse_spec],
            scratch_shapes=[
                pltpu.VMEM((HEAD_SIZE, every), BF16),
                pltpu.VMEM((heads, HEAD_SIZE, rows), F32),
                pltpu.VMEM((16, rows), F32),
            ],
        ),
        out_shape=[
            jax.ShapeDtypeStruct((every, heads_q * HEAD_SIZE), BF16),
            jax.ShapeDtypeStruct((every, heads_kv * wide), BF16),
            jax.ShapeDtypeStruct((heads_kv, 8, every), F32),
        ],
        compiler_params=params,
        cost_estimate=HIDES,
    )
    backward = pl.pallas_call(
        functools.partial(attend_backward, n, heads, rows, c),
        grid_spec=pltpu.PrefetchScalarGridSpec(
            num_scalar_prefetch=1,
            grid=(heads_kv,),
            in_specs=[by_head(rows, heads * HEAD_SIZE)] * n
            + [by_head(every, wide), by_head(every, heads * HEAD_SIZE), lse_spec]
            + tables,
            out_specs=by_head(every, wide),
            scratch_shapes=[
                pltpu.VMEM((every, heads * HEAD_SIZE), BF16),
                pltpu.VMEM((heads * HEAD_SIZE, every), F32),
                pltpu.VMEM((8, every), F32),
                pltpu.VMEM((rows, HEAD_SIZE), F32),
                pltpu.VMEM((rows, HEAD_SIZE), F32),
                pltpu.VMEM((HEAD_SIZE, every), BF16),
            ],
        ),
        out_shape=jax.ShapeDtypeStruct((every, heads_kv * wide), BF16),
        compiler_params=params,
        cost_estimate=pl.CostEstimate(flops=pairs * 10 * HEAD_SIZE, transcendentals=pairs, bytes_accessed=every * wide * 20),
    )
    return forward, backward


def gated_kernel(x_ref, gate_ref, up_ref, gm_ref, *refs):
    mixed_ref, dg_ref, du_ref = refs[-3:]
    x = x_ref[...]
    step = 256 if mixed_ref.shape[1] % 256 == 0 else mixed_ref.shape[1]
    for c in range(0, mixed_ref.shape[1], step):
        at = slice(c, c + step)
        gate = dot(x, gate_ref[:, at], NN)
        up = dot(x, up_ref[:, at], NN)
        gm = gm_ref[:, at]
        sig = 1.0 / (1.0 + jnp.exp(-gate))
        act = gate * sig
        mixed_ref[:, at] = (act * up).astype(BF16)
        du_ref[:, at] = (gm * act).astype(BF16)
        dg_ref[:, at] = (gm * up * sig * (1.0 + gate * (1.0 - sig))).astype(BF16)


def gated(x, w_both, gm, part, before=None):
    rows, width = x.shape
    hidden = w_both.shape[1] // 2
    tile = 512 if hidden % 512 == 0 else hidden
    tiles = hidden // tile
    weight = [pl.BlockSpec((width, tile), lambda j: (0, j)), pl.BlockSpec((width, tile), lambda j: (0, j + tiles))]
    here = pl.BlockSpec((rows, tile), lambda j: (part, j))
    before = () if before is None else tuple(before)
    return pl.pallas_call(
        gated_kernel,
        grid=(tiles,),
        in_specs=[pl.BlockSpec((rows, width), lambda j: (0, 0)), *weight, here]
        + [pl.BlockSpec(memory_space=pl.ANY)] * len(before),
        out_specs=[here] * 3,
        out_shape=[jax.ShapeDtypeStruct((2 * rows, hidden), BF16)] * 3,
        input_output_aliases={4 + i: i for i in range(len(before))},
        compiler_params=pltpu.CompilerParams(vmem_limit_bytes=50 << 20),
        cost_estimate=HIDES,
    )(x, w_both, w_both, gm, *before)


def spread_kernel(count, *refs):
    total = None
    for a_ref, w_ref in zip(refs[:count], refs[count : 2 * count]):
        term = lax.dot_general(a_ref[...], w_ref[...], NT, preferred_element_type=F32)
        total = term if total is None else total + term
    refs[-1][...] = total.astype(refs[-1].dtype)


def spread(acts, weights, part, out, cost=HIDES, piece=0, pieces=1):
    rows, hidden = acts[0].shape[0] // 2, acts[0].shape[1]
    width = weights[0][0].shape[0] // pieces
    tile = 256 if width % 256 == 0 else width
    tiles = width // tile
    count = len(acts)

    def column_block(which):
        return pl.BlockSpec((tile, hidden), lambda j: (j + piece * tiles, which))

    return pl.pallas_call(
        functools.partial(spread_kernel, count),
        grid=(tiles,),
        in_specs=[pl.BlockSpec((rows, hidden), lambda j: (part, 0))] * count
        + [column_block(which) for _, which in weights],
        out_specs=pl.BlockSpec((rows, tile), lambda j: (0, j)),
        out_shape=jax.ShapeDtypeStruct((rows, width), out),
        compiler_params=pltpu.CompilerParams(vmem_limit_bytes=50 << 20),
        cost_estimate=cost,
    )(*acts, *[array for array, _ in weights])


def norm_inverse(source):
    return lax.rsqrt(jnp.mean(source * source, axis=-1, keepdims=True) + EPSILON)


def norm_back_kernel(places, masked, gain_ref, source_ref, straight_ref, *refs):
    grads, refs = refs[: len(places)], refs[len(places) :]
    source = source_ref[...].astype(F32)
    width = source.shape[1]
    inverse = lax.rsqrt(jnp.mean(source * source, axis=-1, keepdims=True) + EPSILON)
    pieces = []
    for half in range(2):
        at = slice(half * width // 2, (half + 1) * width // 2)
        terms = [
            ref[:, at] if count == 2 else ref[...]
            for ref, (first, count) in zip(grads, places)
            if first <= half < first + count
        ]
        pieces.append(sum(term.astype(F32) for term in terms))
    scaled = jnp.concatenate(pieces, axis=1) * gain_ref[...]
    unit_rows = source * inverse
    grad = inverse * (scaled - unit_rows * jnp.mean(scaled * unit_rows, axis=-1, keepdims=True))
    straight = straight_ref[...].astype(F32)
    if masked:
        straight = straight * refs[0][...]
    total = straight + grad
    if masked:
        refs[1][...] = total
        refs[2][...] = total.astype(BF16)
    else:
        refs[0][...] = total


def norm_back(grads, source, gain, straight, mask, low):
    rows, width = source.shape
    tile = 128 if rows % 128 == 0 else rows
    block = lambda wide: pl.BlockSpec((tile, wide), lambda i: (i, 0))
    masked = mask is not None
    out_shape = [jax.ShapeDtypeStruct((rows, width), F32)] + [jax.ShapeDtypeStruct((rows, width), BF16)] * low
    return pl.pallas_call(
        functools.partial(norm_back_kernel, [place for _, *place in grads], masked),
        grid=(rows // tile,),
        in_specs=[pl.BlockSpec((1, width), lambda i: (0, 0)), block(width), block(width)]
        + [block(array.shape[1]) for array, _, _ in grads]
        + [block(1)] * masked,
        out_specs=[block(width)] * len(out_shape) if low else block(width),
        out_shape=out_shape if low else out_shape[0],
        compiler_params=pltpu.CompilerParams(vmem_limit_bytes=40 << 20),
        cost_estimate=HIDES,
    )(gain[None, :], source, straight, *[array for array, _, _ in grads], *([mask] if masked else []))


def turn_kernel(x_ref, o_ref):
    o_ref[...] = x_ref[...].astype(F32).T


def turned(array, first, size):
    rows = array.shape[0]
    return pl.pallas_call(
        turn_kernel,
        grid=(size // HEAD_SIZE,),
        in_specs=[pl.BlockSpec((rows, HEAD_SIZE), lambda j: (0, j + first // HEAD_SIZE))],
        out_specs=pl.BlockSpec((HEAD_SIZE, rows), lambda j: (j, 0)),
        out_shape=jax.ShapeDtypeStruct((size, rows), F32),
        cost_estimate=HIDES,
    )(array)


def shards(
    tokens,
    cotangent,
    segments,
    positions,
    counts,
    query_weight,
    key_projection_weight,
    value_projection_weight,
    out_weight,
    attn_gain,
    gate_weight,
    up_weight,
    down_weight,
    mlp_gain,
):
    n = lax.axis_size("tensor")
    place = lax.axis_index("tensor")
    rows, width = tokens.shape
    every = rows * n
    heads_q = query_weight.shape[1] // HEAD_SIZE
    heads_kv = key_projection_weight.shape[1] // HEAD_SIZE
    heads = heads_q // heads_kv
    qw, hd = heads * HEAD_SIZE, HEAD_SIZE
    wide = qw + 2 * hd
    slices = n // 2

    def gather(shard):
        return lax.all_gather(shard, "dp", axis=0, tiled=True)

    partners = halves(n, [(i, i ^ 1) for i in range(n)])
    outward = [halves(n, [((i + 2 * k) % n, i) for i in range(n)]) for k in range(1, slices)]
    homeward = [halves(n, [(i, (i + 2 * k) % n) for i in range(n)]) for k in range(1, slices)]

    def to_others(shard, half):
        return [(shard, pairs[half]) for pairs in outward]

    def to_owners(sums, half):
        return [(one, pairs[half]) for one, pairs in zip(sums, homeward)]

    live_count = counts[0]
    own_index = place * rows + jnp.arange(rows, dtype=jnp.int32)
    live = (own_index < live_count).astype(F32)[:, None]
    labels = lax.all_gather(jnp.stack([segments, positions]), "tensor", axis=1, tiled=True)
    seg_all, place_all = labels[0], labels[1]
    index_all = jnp.arange(every, dtype=jnp.int32)
    key_seg = jnp.where(index_all < live_count, seg_all, -1)[:, None]
    query_seg = seg_all[None, :]
    freqs = ROPE_BASE ** (-(jnp.arange(hd // 2, dtype=F32) * 2.0) / hd)
    angles = place_all.astype(F32)[:, None] * freqs[None, :]
    cos, sin = jnp.cos(angles), jnp.sin(angles)
    cos = jnp.concatenate([cos, cos], axis=1)
    sin = jnp.concatenate([-sin, sin], axis=1)
    order = np.array([[i] + row for i, row in enumerate(arrival_order(n))], np.int32)
    where_is = np.argsort(order, axis=1).astype(np.int32)
    slot_table = jnp.asarray(np.concatenate([order, where_is], axis=1))[place]
    attend, attend_back = attention_calls(n, rows, heads_q, heads_kv)
    tables = (cos, sin, query_seg, key_seg)

    gains = lax.all_gather(jnp.stack([attn_gain, mlp_gain]), "dp", axis=1, tiled=True).astype(F32)
    gain_one, gain_two = gains[0], gains[1]

    source = tokens.astype(F32)
    inv_one = norm_inverse(source)
    normed_one = (source * inv_one * gain_one).astype(BF16)

    def attention_weights(gate):
        query, key, value = lax.optimization_barrier((query_weight, key_projection_weight, value_projection_weight, gate))[:3]
        return jnp.concatenate(
            [
                part
                for g in range(heads_kv)
                for part in (
                    query[:, g * qw : (g + 1) * qw],
                    key[:, g * hd : (g + 1) * hd],
                    value[:, g * hd : (g + 1) * hd],
                )
            ],
            axis=1,
        )

    own_qkv = attention_weights(normed_one)
    w_qkv = gather(own_qkv)
    shards_here, early = [], []

    def shard_layouts(step, gate):
        if step != 1:
            return ()
        both = jnp.concatenate([after(gate_weight, gate), up_weight], axis=1)
        masked = (after(cotangent, gate).astype(F32) * live).astype(BF16)
        return (after(out_weight, gate).T, after(down_weight, gate).T, both, masked, *tables)

    def took_rows(step, arrived, filled):
        early.extend(arrived)
        if step == 1:
            shards_here.extend(filled[:4])

    more = slices - 1
    slots_one, projected = line_gather(
        after(normed_one, labels),
        n,
        lambda s, shard: dot(shard, w_qkv, NN),
        shard_layouts,
        lambda step: {
            n - 2: [(shards_here[3], partners[0])] if shards_here else (),
            n - 1: to_others(shards_here[2], 0) if shards_here else (),
        }.get(step, ()),
        took_rows,
    )
    low_ends, both_ends = early[0], early[1:]
    out_t, down_t, both_weight, grad_low = shards_here
    w_out, w_down, w_both = gather(out_t), [gather(down_t)], [gather(both_weight)]
    projected[n - 1] = after(projected[n - 1], w_out, w_down[0])

    def attention(gate):
        return attend(slot_table, *projected, *tables)

    downs = after(down_t, projected[n - 1])
    moved, (attended, rotated, lse) = travel([(downs, a + b) for a, b in outward], attention)
    w_down += [gather(shard) for shard in moved]
    grad_mixed, lows = [], []

    def while_out(step, gate):
        if step == 1:
            return (w_both[0],)
        if step == n - 1:
            theirs = joined(low_ends, lows[0])
            lows.append(theirs)
            return tuple(dot(jnp.concatenate([grad_low, theirs], axis=0), w, NN) for w in w_down)
        return ()

    def along_out(step):
        if step == 1:
            return to_others(both_weight, 1)
        if step == 2:
            return [(grad_low, partners[1])]
        return ()

    def took_out(step, arrived, filled):
        if step == 1:
            w_both.extend(gather(joined(a, b)) for a, b in zip(both_ends, arrived))
        elif step == n - 1:
            grad_mixed.extend(filled)
        else:
            lows.extend(arrived)

    summed = line_reduce(
        lambda s: dot(attended[s * rows : (s + 1) * rows], w_out, NT, BF16), n, while_out, along_out, took_out
    )
    hidden = source + sum(term.astype(F32) for term in summed)
    grad_two = jnp.concatenate([grad_low, lows[1]], axis=0)

    inv_two = norm_inverse(hidden)
    normed_two = (hidden * inv_two * gain_two).astype(BF16)

    def own_rows(gate):
        made = [one for w, gm in zip(w_both, grad_mixed) for one in gated(gate, w, gm, 0)]
        return [spread(made[1::3] + made[2::3], weights, 0, F32, HIDES, 0, 2), *made]

    swap = partners[0] + partners[1]
    weights = [(w, 0) for w in w_both] + [(w, 1) for w in w_both]
    (two_theirs,), (ours_first, *mine) = travel([(normed_two, swap)], own_rows)
    two = jnp.concatenate([normed_two, two_theirs], axis=0)
    mixed, grad_gate, grad_up, d_down = [None] * slices, [None] * slices, [None] * slices, [None] * slices
    rows_in = two_theirs
    for k in range(slices - 1, -1, -1):
        mixed[k], grad_gate[k], grad_up[k] = gated(rows_in, w_both[k], grad_mixed[k], 1, mine[3 * k : 3 * k + 3])
        if k > 0:
            d_down[k] = dot(grad_two, mixed[k], TN, BF16)
            rows_in = after(two_theirs, d_down[k])
    grads = grad_gate + grad_up
    d_up, d_gate = [None] * slices, [None] * slices

    def second_half(gate):
        return (
            spread([after(grads[0], gate)] + grads[1:], weights, 1, BF16, HIDES, 1, 2),
            *(dot(two, after(g, gate), TN, BF16) for g in grad_up[1:]),
        )

    def gate_weights(gate):
        return (
            spread([after(grads[0], gate)] + grads[1:], weights, 0, F32, HIDES, 1, 2),
            *(dot(two, after(g, gate), TN, BF16) for g in grad_gate[1:]),
        )

    theirs = spread(grads, weights, 1, BF16, HIDES, 0, 2)
    (from_first,), (theirs, *d_up[1:]) = travel([(theirs, swap)], second_half)
    (from_second,), (ours_second, *d_gate[1:]) = travel([(theirs, swap)], gate_weights)
    grad_hidden, grad_hidden_low = norm_back(
        [(ours_first, 0, 1), (ours_second, 1, 1), (from_first, 0, 1), (from_second, 1, 1)], hidden, gain_two, cotangent, live, True
    )

    def owner_sum(partial):
        return lax.psum_scatter(partial, "dp", scatter_dimension=0, tiled=True)

    results, early = [], []

    def d_of(left, right, gate):
        return dot(left, after(right, gate), TN, BF16)

    def result_rows(part, out, gate, cost=HIDES):
        return spread([after(mixed[0], gate), *mixed[1:]], [(w, 0) for w in w_down], part, out, cost)

    def while_gather(step, gate):
        if step == 1:
            flops = 2 * rows * width * slices * gate_weight.shape[1]
            cost = pl.CostEstimate(flops=flops, transcendentals=0, bytes_accessed=flops // rows)
            return (result_rows(1, BF16, gate, cost), d_of(grad_two, mixed[0], gate))
        if step == 2:
            return (result_rows(0, F32, gate), d_of(two, grad_up[0], gate), *joined_sums())
        if step == n - 1:
            return (d_of(two, grad_gate[0], gate),)
        return ()

    def took_gather(step, arrived, filled):
        early.extend(arrived)
        if step == 1:
            results.append(filled[0])
            d_down[0] = filled[1]
        elif step == 2:
            results.append(filled[0])
            d_up[0] = filled[1]
            sums.extend(filled[2:])
        elif step == n - 1:
            d_gate[0] = filled[0]

    sums = []

    def joined_sums():
        return [jnp.concatenate([owner_sum(a), owner_sum(b)], axis=1) for a, b in zip(d_down[1:], d_up[1:])]

    slots_back, grad_attended = line_gather(
        grad_hidden_low,
        n,
        lambda s, shard: dot(shard, w_out, NN, BF16),
        while_gather,
        lambda step: {
            2: [(results[0], partners[0])] if results else (),
            n - 1: to_owners(sums, 0),
        }.get(step, ()),
        took_gather,
    )
    result_ends, sum_ends = early[0], early[1:]

    def attention_back(gate):
        return (
            attend_back(after(slot_table, gate), *grad_attended, rotated, attended, lse, *tables),
            sum_down,
        )

    sums_gate = [owner_sum(d) for d in d_gate[1:]]
    sum_down, sum_up, sum_gate = owner_sum(d_down[0]), owner_sum(d_up[0]), owner_sum(d_gate[0])
    leaving = [after(one, grad_attended[n - 1]) for one in sums_gate]
    back_gate, (grad_qkv, _) = travel(
        [(one, a + b) for one, (a, b) in zip(leaving, homeward)], attention_back
    )
    back_down, back_up, outputs, d_attention = [], [], [], []

    def columns(array, offset, size):
        return jnp.concatenate(
            [array[:, g * wide + offset : g * wide + offset + size] for g in range(heads_kv)], axis=1
        ).astype(F32)


    def while_reduce(step, gate):
        if step == 1:
            return (d_of(jnp.concatenate(slots_one, axis=0), grad_qkv, gate), sum_up)
        if step == 2:
            return (d_of(jnp.concatenate(slots_back, axis=0), attended, gate), sum_gate)
        if step == n - 1:
            from_partner = joined(result_ends, outputs[0])
            result = hidden + (results[1] + after(from_partner, gate).astype(F32))
            sum_attention = owner_sum(d_attention[0])
            return (
                (result * live).astype(BF16),
                *(columns(sum_attention, *place) for place in ((0, qw), (qw, hd), (qw + hd, hd))),
                sum_attention,
            )
        return ()

    def along_reduce(step):
        if step == 1:
            return to_owners(sums, 1)
        if step == 2:
            return [(results[0], partners[1])]
        return ()

    def took_reduce(step, arrived, filled):
        if step == 1:
            for a, b in zip(sum_ends, arrived):
                back = joined(a, b)
                back_down.append(back[:, : down_t.shape[1]])
                back_up.append(back[:, down_t.shape[1] :])
            d_attention.append(filled[0])
        elif step == 2:
            outputs.extend(arrived)
            d_attention.append(filled[0])
        elif step == n - 1:
            outputs.extend(filled)

    grad_normed_one = line_reduce(
        lambda s: dot(grad_qkv[s * rows : (s + 1) * rows], w_qkv, NT, BF16),
        n,
        while_reduce,
        along_reduce,
        took_reduce,
    )
    _, output, grad_query_w, grad_key_w, grad_value_w, sum_attention = outputs

    def whole(first, back):
        return sum((one.astype(F32) for one in back), first.astype(F32))

    grad_down_w = whole(sum_down, back_down).T
    grad_gate_w = whole(sum_gate, back_gate)
    grad_up_w = whole(sum_up, back_up)
    grad_qkv_w = sum_attention.astype(F32)
    def along_row(weight, grad):
        return jnp.sum(weight.astype(F32) * grad, axis=1)

    gain_parts = jnp.stack(
        [
            along_row(own_qkv, grad_qkv_w),
            along_row(gate_weight, grad_gate_w) + along_row(up_weight, grad_up_w),
        ]
    )
    gain_own = lax.psum(gain_parts, "tensor") / jnp.stack([attn_gain, mlp_gain]).astype(F32)

    grad_tokens = norm_back([(term, 0, 2) for term in grad_normed_one], tokens, gain_one, grad_hidden, None, False)
    grad_out_w = turned(after(owner_sum(d_attention[1]), grad_tokens), 0, out_weight.shape[0])

    return (
        output,
        grad_tokens,
        grad_query_w,
        grad_key_w,
        grad_value_w,
        grad_out_w,
        gain_own[0],
        grad_gate_w,
        grad_up_w,
        grad_down_w,
        gain_own[1],
    )


def solution(mesh):
    rows = P(("dp", "tensor"), None)
    row = P(("dp", "tensor"))
    down_cols = P("tensor", "dp")
    cols = P("dp", "tensor")
    return jax.shard_map(
        shards,
        mesh=mesh,
        in_specs=(rows, rows, row, row, P("dp"), cols, cols, cols, down_cols, P("dp"), cols, cols, down_cols, P("dp")),
        out_specs=(rows, rows, cols, cols, cols, down_cols, P("dp"), cols, cols, down_cols, P("dp")),
        check_vma=False,
    )
```

```python
import functools
import math

import jax
import jax.numpy as jnp
import numpy as np
from jax import lax
from jax.experimental import pallas as pl
from jax.experimental.pallas import tpu as pltpu
from jax.sharding import PartitionSpec as P

HEAD_SIZE = 128
EPSILON = 1e-05
ROPE_BASE = 500000.0
MASKED = -1e30
F32 = jnp.float32
BF16 = jnp.bfloat16
NT = (((1,), (1,)), ((), ()))
NN = (((1,), (0,)), ((), ()))
TN = (((0,), (0,)), ((), ()))
HIDES = pl.CostEstimate(flops=1, transcendentals=0, bytes_accessed=1)


def dot(a, b, dims, out=F32):
    return lax.dot_general(a, b, dims, preferred_element_type=F32).astype(out)


def after(value, *others):
    return lax.optimization_barrier((value, *others))[0]


def arrival_order(n):
    return [
        [s for d in range(1, n) for s in (i - d, i + d) if 0 <= s < n]
        for i in range(n)
    ]


def pick(place, choices):
    distinct = []
    for value in choices:
        if not any(value is other for other in distinct):
            distinct.append(value)
    out = distinct[0]
    for value in distinct[1:]:
        here = functools.reduce(
            jnp.logical_or, [place == i for i, c in enumerate(choices) if c is value]
        )
        out = jnp.where(here, value, out)
    return out


def travel(items, work=lambda gate: ()):
    arrays = lax.optimization_barrier(tuple(array for array, _ in items))
    moved = [lax.ppermute(array, "tensor", pairs) for array, (_, pairs) in zip(arrays, items)]
    out = lax.optimization_barrier((*moved, *work(arrays[0])))
    return list(out[: len(moved)]), list(out[len(moved) :])


def line_gather(own, n, use, fill=lambda step, gate: (), along=lambda step: (), took=lambda step, arrived, filled: None):
    place = lax.axis_index("tensor")
    order = arrival_order(n)
    right = left = own
    from_left, from_right = [own], [own]
    slots, used = [own], []
    for d in range(1, n):

        def work(gate):
            return (use(d - 1, after(slots[d - 1], gate) if d > 1 else own), *fill(d, gate))

        (right, left, *more), (result, *filled) = travel(
            [
                (right, [(i, i + 1) for i in range(d - 1, n - 1)]),
                (left, [(i + 1, i) for i in range(n - d)]),
                *along(d),
            ],
            work,
        )
        used.append(result)
        took(d, more, filled)
        from_left.append(right)
        from_right.append(left)
        slots.append(
            pick(
                place,
                [
                    from_left[i - order[i][d - 1]] if order[i][d - 1] < i else from_right[order[i][d - 1] - i]
                    for i in range(n)
                ],
            )
        )
    used.append(use(n - 1, slots[-1]))
    return slots, used


def line_reduce(part, n, fill=lambda step, gate: (), along=lambda step: (), took=lambda step, arrived, filled: None):
    place = lax.axis_index("tensor")
    parts = [None] * n
    parts[n - 1] = lax.optimization_barrier(part(n - 1))
    order = [[i] + row for i, row in enumerate(arrival_order(n))]
    right = left = None

    def sent(k):
        ways = [order[i].index(i + n - k) for i in range(k)] + [order[i].index(i - n + k) for i in range(n - k, n)]
        return sorted(set(ways), reverse=True)

    def add(value, *sums):
        if right is None:
            return value
        return (value.astype(F32) + sum(one.astype(F32) for one in sums)).astype(BF16)

    for k in range(1, n):
        rightward = [parts[order[i].index(i + n - k)] if i < k else parts[n - k] for i in range(n)]
        leftward = [parts[order[i].index(i - n + k)] if i >= n - k else parts[n - k] for i in range(n)]
        if 2 * k <= n:
            choice = [r if i < k else l for i, (r, l) in enumerate(zip(rightward, leftward))]
            to_right = to_left = add(pick(place, choice), right, left)
        else:
            to_right, to_left = add(pick(place, rightward), right), add(pick(place, leftward), left)

        coming = [0] if k == n - 1 else [s for s in sent(k + 1) if parts[s] is None]

        def work(gate):
            return (*(part(s) for s in coming), *fill(k, gate))

        (right, left, *more), worked = travel(
            [
                (to_right, [(i, i + 1) for i in range(k)]),
                (to_left, [(n - 1 - i, n - 2 - i) for i in range(k)]),
                *along(k),
            ],
            work,
        )
        for s, one in zip(coming, worked):
            parts[s] = one
        took(k, more, worked[len(coming) :])
    return parts[0], right, left


def halves(n, pairs):
    ends = [(a, b) for a, b in pairs if a < n // 4 or a >= n - n // 4]
    return ends, [pair for pair in pairs if pair not in ends]


def joined(first, second):
    return first + second


def attend_forward(n, heads, rows, c, place_ref, *refs):
    chunks = refs[:n]
    cos_ref, sin_ref, qseg_ref, kseg_ref, o_ref, rot_ref, lse_ref, vt, acc, stat = refs[n:]
    hd = HEAD_SIZE
    kc, vc = heads * hd, (heads + 1) * hd
    for s in range(n):
        at = pl.ds(pl.multiple_of(place_ref[s] * rows, rows), rows)
        cos, sin = cos_ref[at, :], sin_ref[at, :]
        for h in range(heads + 1):
            u = chunks[s][:, h * hd : (h + 1) * hd]
            rot_ref[at, h * hd : (h + 1) * hd] = (u * cos + pltpu.roll(u, hd // 2, 1) * sin).astype(BF16)
        v = chunks[s][:, vc : vc + hd]
        rot_ref[at, vc : vc + hd] = v.astype(BF16)
        vt[:, at] = v.T.astype(BF16)

    def block(i, j, diagonal):
        qi = pl.ds(pl.multiple_of(i * rows, rows), rows)
        kj = pl.ds(pl.multiple_of(j * rows, rows), rows)
        k = rot_ref[kj, kc : kc + hd]
        allowed = kseg_ref[kj, :] == qseg_ref[:, qi]
        if diagonal:
            kr = lax.broadcasted_iota(jnp.int32, (rows, rows), 0)
            qr = lax.broadcasted_iota(jnp.int32, (rows, rows), 1)
            allowed = (allowed & (kr < qr)) | (kr == qr)
        for h in range(heads):
            q = rot_ref[qi, h * hd : (h + 1) * hd]
            scores = jnp.where(allowed, dot(k, q, NT) * c, MASKED)
            m = stat[h : h + 1, :]
            top = jnp.maximum(m, jnp.max(scores, axis=0, keepdims=True))
            p = jnp.exp2(scores - top)
            alpha = jnp.exp2(m - top)
            stat[h : h + 1, :] = top
            total = alpha * stat[8 + h : 9 + h, :] + jnp.sum(p, axis=0, keepdims=True)
            stat[8 + h : 9 + h, :] = total
            new = alpha * acc[h] + dot(vt[:, kj], p.astype(BF16), NN)
            if diagonal:
                at = pl.ds(pl.multiple_of(place_ref[n + i] * rows, rows), rows)
                o_ref[at, h * hd : (h + 1) * hd] = (new / total).T.astype(BF16)
                lse_ref[0, h : h + 1, qi] = top + jnp.log2(total)
            else:
                acc[h] = new

    @pl.loop(0, n)
    def _(i):
        stat[0:8, :] = jnp.full((8, rows), MASKED, F32)
        stat[8:16, :] = jnp.zeros((8, rows), F32)
        acc[...] = jnp.zeros_like(acc)

        @pl.loop(0, i)
        def _(j):
            block(i, j, False)

        block(i, i, True)


def attend_backward(n, heads, rows, c, place_ref, *refs):
    gas = refs[:n]
    rot_ref, o_ref, lse_ref, cos_ref, sin_ref, qseg_ref, kseg_ref, d_ref, go, dqt, delta, dk, dv, kt = refs[n:]
    hd = HEAD_SIZE
    scale = hd**-0.5
    kc, vc = heads * hd, (heads + 1) * hd
    for s in range(n):
        at = pl.ds(pl.multiple_of(place_ref[s] * rows, rows), rows)
        for h in range(heads):
            g = gas[s][:, h * hd : (h + 1) * hd]
            o = o_ref[s * rows : (s + 1) * rows, h * hd : (h + 1) * hd]
            go[at, h * hd : (h + 1) * hd] = g
            both = (g.astype(F32) * o.astype(F32)).T
            delta[h : h + 1, at] = jnp.sum(both, axis=0, keepdims=True)
        kt[:, at] = rot_ref[at, kc : kc + hd].astype(F32).T.astype(BF16)
    dqt[...] = jnp.zeros_like(dqt)

    def block(i, j, diagonal):
        qi = pl.ds(pl.multiple_of(i * rows, rows), rows)
        kj = pl.ds(pl.multiple_of(j * rows, rows), rows)
        k = rot_ref[kj, kc : kc + hd]
        v = rot_ref[kj, vc : vc + hd]
        allowed = kseg_ref[kj, :] == qseg_ref[:, qi]
        if diagonal:
            kr = lax.broadcasted_iota(jnp.int32, (rows, rows), 0)
            qr = lax.broadcasted_iota(jnp.int32, (rows, rows), 1)
            allowed = (allowed & (kr < qr)) | (kr == qr)
        for h in range(heads):
            cols = slice(h * hd, (h + 1) * hd)
            q = rot_ref[qi, cols]
            g = go[qi, cols]
            scores = jnp.where(allowed, dot(k, q, NT) * c, MASKED)
            p = jnp.exp2(scores - lse_ref[0, h : h + 1, qi])
            gp = dot(v, g, NT)
            ds = (p * (gp - delta[h : h + 1, qi])).astype(BF16)
            new_v = dot(p.astype(BF16), g, NN)
            new_k = dot(ds, q, NN)
            if diagonal and h == 0:
                dv[...] = new_v
                dk[...] = new_k
            else:
                dv[...] += new_v
                dk[...] += new_k
            dqt[h * hd : (h + 1) * hd, qi] += dot(kt[:, kj], ds, NN)

    def unrotate(u, at):
        return u * cos_ref[at, :] - pltpu.roll(u, hd // 2, 1) * sin_ref[at, :]

    @pl.loop(0, n)
    def _(j):
        block(j, j, True)

        @pl.loop(j + 1, n)
        def _(i):
            block(i, j, False)

        kj = pl.ds(pl.multiple_of(j * rows, rows), rows)
        to = pl.ds(pl.multiple_of(place_ref[n + j] * rows, rows), rows)
        for h in range(heads):
            u = dqt[h * hd : (h + 1) * hd, kj].T * scale
            d_ref[to, h * hd : (h + 1) * hd] = unrotate(u, kj).astype(BF16)
        d_ref[to, kc : kc + hd] = unrotate(dk[...] * scale, kj).astype(BF16)
        d_ref[to, vc : vc + hd] = dv[...].astype(BF16)


def attention_calls(n, rows, heads_q, heads_kv):
    heads = heads_q // heads_kv
    every = n * rows
    wide = (heads + 2) * HEAD_SIZE
    c = HEAD_SIZE**-0.5 * math.log2(math.e)
    whole = lambda shape: pl.BlockSpec(shape, lambda g, place: (0, 0))
    by_head = lambda r, w: pl.BlockSpec((r, w), lambda g, place: (0, g))
    tables = [
        whole((every, HEAD_SIZE)),
        whole((every, HEAD_SIZE)),
        whole((1, every)),
        whole((every, 1)),
    ]
    lse_spec = pl.BlockSpec((1, 8, every), lambda g, place: (g, 0, 0))
    pairs = every * every * heads_q
    params = pltpu.CompilerParams(vmem_limit_bytes=58 << 20)
    forward = pl.pallas_call(
        functools.partial(attend_forward, n, heads, rows, c),
        grid_spec=pltpu.PrefetchScalarGridSpec(
            num_scalar_prefetch=1,
            grid=(heads_kv,),
            in_specs=[by_head(rows, wide)] * n + tables,
            out_specs=[by_head(every, heads * HEAD_SIZE), by_head(every, wide), lse_spec],
            scratch_shapes=[
                pltpu.VMEM((HEAD_SIZE, every), BF16),
                pltpu.VMEM((heads, HEAD_SIZE, rows), F32),
                pltpu.VMEM((16, rows), F32),
            ],
        ),
        out_shape=[
            jax.ShapeDtypeStruct((every, heads_q * HEAD_SIZE), BF16),
            jax.ShapeDtypeStruct((every, heads_kv * wide), BF16),
            jax.ShapeDtypeStruct((heads_kv, 8, every), F32),
        ],
        compiler_params=params,
        cost_estimate=HIDES,
    )
    backward = pl.pallas_call(
        functools.partial(attend_backward, n, heads, rows, c),
        grid_spec=pltpu.PrefetchScalarGridSpec(
            num_scalar_prefetch=1,
            grid=(heads_kv,),
            in_specs=[by_head(rows, heads * HEAD_SIZE)] * n
            + [by_head(every, wide), by_head(every, heads * HEAD_SIZE), lse_spec]
            + tables,
            out_specs=by_head(every, wide),
            scratch_shapes=[
                pltpu.VMEM((every, heads * HEAD_SIZE), BF16),
                pltpu.VMEM((heads * HEAD_SIZE, every), F32),
                pltpu.VMEM((8, every), F32),
                pltpu.VMEM((rows, HEAD_SIZE), F32),
                pltpu.VMEM((rows, HEAD_SIZE), F32),
                pltpu.VMEM((HEAD_SIZE, every), BF16),
            ],
        ),
        out_shape=jax.ShapeDtypeStruct((every, heads_kv * wide), BF16),
        compiler_params=params,
        cost_estimate=pl.CostEstimate(flops=pairs * 10 * HEAD_SIZE, transcendentals=pairs, bytes_accessed=every * wide * 20),
    )
    return forward, backward


def gated_kernel(x_ref, gate_ref, up_ref, gm_ref, *refs):
    mixed_ref, dg_ref, du_ref = refs[-3:]
    x = x_ref[...]
    step = 256 if mixed_ref.shape[1] % 256 == 0 else mixed_ref.shape[1]
    for c in range(0, mixed_ref.shape[1], step):
        at = slice(c, c + step)
        gate = dot(x, gate_ref[:, at], NN)
        up = dot(x, up_ref[:, at], NN)
        gm = gm_ref[:, at]
        sig = 1.0 / (1.0 + jnp.exp(-gate))
        act = gate * sig
        mixed_ref[:, at] = (act * up).astype(BF16)
        du_ref[:, at] = (gm * act).astype(BF16)
        dg_ref[:, at] = (gm * up * sig * (1.0 + gate * (1.0 - sig))).astype(BF16)


def gated(x, w_both, gm, part, before=None):
    rows, width = x.shape
    hidden = w_both.shape[1] // 2
    tile = 512 if hidden % 512 == 0 else hidden
    tiles = hidden // tile
    weight = [pl.BlockSpec((width, tile), lambda j: (0, j)), pl.BlockSpec((width, tile), lambda j: (0, j + tiles))]
    here = pl.BlockSpec((rows, tile), lambda j: (part, j))
    before = () if before is None else tuple(before)
    return pl.pallas_call(
        gated_kernel,
        grid=(tiles,),
        in_specs=[pl.BlockSpec((rows, width), lambda j: (0, 0)), *weight, here]
        + [pl.BlockSpec(memory_space=pl.ANY)] * len(before),
        out_specs=[here] * 3,
        out_shape=[jax.ShapeDtypeStruct((2 * rows, hidden), BF16)] * 3,
        input_output_aliases={4 + i: i for i in range(len(before))},
        compiler_params=pltpu.CompilerParams(vmem_limit_bytes=50 << 20),
        cost_estimate=HIDES,
    )(x, w_both, w_both, gm, *before)


def spread_kernel(count, *refs):
    total = None
    for a_ref, w_ref in zip(refs[:count], refs[count : 2 * count]):
        term = lax.dot_general(a_ref[...], w_ref[...], NT, preferred_element_type=F32)
        total = term if total is None else total + term
    refs[-1][...] = total.astype(refs[-1].dtype)


def spread(acts, weights, part, out, cost=HIDES, piece=0, pieces=1):
    rows, hidden = acts[0].shape[0] // 2, acts[0].shape[1]
    width = weights[0][0].shape[0] // pieces
    tile = 256 if width % 256 == 0 else width
    tiles = width // tile
    count = len(acts)

    def column_block(which):
        return pl.BlockSpec((tile, hidden), lambda j: (j + piece * tiles, which))

    return pl.pallas_call(
        functools.partial(spread_kernel, count),
        grid=(tiles,),
        in_specs=[pl.BlockSpec((rows, hidden), lambda j: (part, 0))] * count
        + [column_block(which) for _, which in weights],
        out_specs=pl.BlockSpec((rows, tile), lambda j: (0, j)),
        out_shape=jax.ShapeDtypeStruct((rows, width), out),
        compiler_params=pltpu.CompilerParams(vmem_limit_bytes=50 << 20),
        cost_estimate=cost,
    )(*acts, *[array for array, _ in weights])


def norm_inverse(source):
    return lax.rsqrt(jnp.mean(source * source, axis=-1, keepdims=True) + EPSILON)


def norm_back_kernel(places, masked, gain_ref, source_ref, straight_ref, *refs):
    grads, refs = refs[: len(places)], refs[len(places) :]
    source = source_ref[...].astype(F32)
    width = source.shape[1]
    inverse = lax.rsqrt(jnp.mean(source * source, axis=-1, keepdims=True) + EPSILON)
    pieces = []
    for half in range(2):
        at = slice(half * width // 2, (half + 1) * width // 2)
        terms = [
            ref[:, at] if count == 2 else ref[...]
            for ref, (first, count) in zip(grads, places)
            if first <= half < first + count
        ]
        pieces.append(sum(term.astype(F32) for term in terms))
    scaled = jnp.concatenate(pieces, axis=1) * gain_ref[...]
    unit_rows = source * inverse
    grad = inverse * (scaled - unit_rows * jnp.mean(scaled * unit_rows, axis=-1, keepdims=True))
    straight = straight_ref[...].astype(F32)
    if masked:
        straight = straight * refs[0][...]
    total = straight + grad
    if masked:
        refs[1][...] = total
        refs[2][...] = total.astype(BF16)
    else:
        refs[0][...] = total


def norm_back(grads, source, gain, straight, mask, low):
    rows, width = source.shape
    tile = 128 if rows % 128 == 0 else rows
    block = lambda wide: pl.BlockSpec((tile, wide), lambda i: (i, 0))
    masked = mask is not None
    out_shape = [jax.ShapeDtypeStruct((rows, width), F32)] + [jax.ShapeDtypeStruct((rows, width), BF16)] * low
    return pl.pallas_call(
        functools.partial(norm_back_kernel, [place for _, *place in grads], masked),
        grid=(rows // tile,),
        in_specs=[pl.BlockSpec((1, width), lambda i: (0, 0)), block(width), block(width)]
        + [block(array.shape[1]) for array, _, _ in grads]
        + [block(1)] * masked,
        out_specs=[block(width)] * len(out_shape) if low else block(width),
        out_shape=out_shape if low else out_shape[0],
        compiler_params=pltpu.CompilerParams(vmem_limit_bytes=40 << 20),
        cost_estimate=HIDES,
    )(gain[None, :], source, straight, *[array for array, _, _ in grads], *([mask] if masked else []))


def turn_kernel(x_ref, o_ref):
    o_ref[...] = x_ref[...].astype(F32).T


def turned(array, first, size):
    rows = array.shape[0]
    return pl.pallas_call(
        turn_kernel,
        grid=(size // HEAD_SIZE,),
        in_specs=[pl.BlockSpec((rows, HEAD_SIZE), lambda j: (0, j + first // HEAD_SIZE))],
        out_specs=pl.BlockSpec((HEAD_SIZE, rows), lambda j: (j, 0)),
        out_shape=jax.ShapeDtypeStruct((size, rows), F32),
        cost_estimate=HIDES,
    )(array)


def shards(
    tokens,
    cotangent,
    segments,
    positions,
    counts,
    query_weight,
    key_projection_weight,
    value_projection_weight,
    out_weight,
    attn_gain,
    gate_weight,
    up_weight,
    down_weight,
    mlp_gain,
):
    n = lax.axis_size("tensor")
    place = lax.axis_index("tensor")
    rows, width = tokens.shape
    every = rows * n
    heads_q = query_weight.shape[1] // HEAD_SIZE
    heads_kv = key_projection_weight.shape[1] // HEAD_SIZE
    heads = heads_q // heads_kv
    qw, hd = heads * HEAD_SIZE, HEAD_SIZE
    wide = qw + 2 * hd
    slices = n // 2

    def gather(shard):
        return lax.all_gather(shard, "dp", axis=0, tiled=True)

    partners = halves(n, [(i, i ^ 1) for i in range(n)])
    outward = [halves(n, [((i + 2 * k) % n, i) for i in range(n)]) for k in range(1, slices)]
    homeward = [halves(n, [(i, (i + 2 * k) % n) for i in range(n)]) for k in range(1, slices)]

    def to_others(shard, half):
        return [(shard, pairs[half]) for pairs in outward]

    def to_owners(sums, half):
        return [(one, pairs[half]) for one, pairs in zip(sums, homeward)]

    live_count = counts[0]
    own_index = place * rows + jnp.arange(rows, dtype=jnp.int32)
    live = (own_index < live_count).astype(F32)[:, None]
    labels = lax.all_gather(jnp.stack([segments, positions]), "tensor", axis=1, tiled=True)
    seg_all, place_all = labels[0], labels[1]
    index_all = jnp.arange(every, dtype=jnp.int32)
    key_seg = jnp.where(index_all < live_count, seg_all, -1)[:, None]
    query_seg = seg_all[None, :]
    freqs = ROPE_BASE ** (-(jnp.arange(hd // 2, dtype=F32) * 2.0) / hd)
    angles = place_all.astype(F32)[:, None] * freqs[None, :]
    cos, sin = jnp.cos(angles), jnp.sin(angles)
    cos = jnp.concatenate([cos, cos], axis=1)
    sin = jnp.concatenate([-sin, sin], axis=1)
    order = np.array([[i] + row for i, row in enumerate(arrival_order(n))], np.int32)
    where_is = np.argsort(order, axis=1).astype(np.int32)
    slot_table = jnp.asarray(np.concatenate([order, where_is], axis=1))[place]
    attend, attend_back = attention_calls(n, rows, heads_q, heads_kv)
    tables = (cos, sin, query_seg, key_seg)

    gains = lax.all_gather(jnp.stack([attn_gain, mlp_gain]), "dp", axis=1, tiled=True).astype(F32)
    gain_one, gain_two = gains[0], gains[1]

    source = tokens.astype(F32)
    inv_one = norm_inverse(source)
    normed_one = (source * inv_one * gain_one).astype(BF16)

    def attention_weights(gate):
        query, key, value = lax.optimization_barrier((query_weight, key_projection_weight, value_projection_weight, gate))[:3]
        return jnp.concatenate(
            [
                part
                for g in range(heads_kv)
                for part in (
                    query[:, g * qw : (g + 1) * qw],
                    key[:, g * hd : (g + 1) * hd],
                    value[:, g * hd : (g + 1) * hd],
                )
            ],
            axis=1,
        )

    own_qkv = attention_weights(normed_one)
    w_qkv = gather(own_qkv)
    shards_here, early = [], []

    def shard_layouts(step, gate):
        if step != 1:
            return ()
        both = jnp.concatenate([after(gate_weight, gate), up_weight], axis=1)
        masked = (after(cotangent, gate).astype(F32) * live).astype(BF16)
        return (after(out_weight, gate).T, after(down_weight, gate).T, both, masked, *tables)

    def took_rows(step, arrived, filled):
        early.extend(arrived)
        if step == 1:
            shards_here.extend(filled[:4])

    more = slices - 1
    slots_one, projected = line_gather(
        after(normed_one, labels),
        n,
        lambda s, shard: dot(shard, w_qkv, NN),
        shard_layouts,
        lambda step: {
            n - 2: [(shards_here[3], partners[0])] if shards_here else (),
            n - 1: to_others(shards_here[2], 0) if shards_here else (),
        }.get(step, ()),
        took_rows,
    )
    low_ends, both_ends = early[0], early[1:]
    out_t, down_t, both_weight, grad_low = shards_here
    w_out, w_down, w_both = gather(out_t), [gather(down_t)], [gather(both_weight)]
    projected[n - 1] = after(projected[n - 1], w_out, w_down[0])

    def attention(gate):
        return attend(slot_table, *projected, *tables)

    downs = after(down_t, projected[n - 1])
    moved, (attended, rotated, lse) = travel([(downs, a + b) for a, b in outward], attention)
    w_down += [gather(shard) for shard in moved]
    grad_mixed, lows = [], []

    def while_out(step, gate):
        if step == 1:
            return (w_both[0],)
        if step == n - 1:
            theirs = joined(low_ends, lows[0])
            lows.append(theirs)
            return tuple(dot(jnp.concatenate([grad_low, theirs], axis=0), w, NN) for w in w_down)
        return ()

    def along_out(step):
        if step == 1:
            return to_others(both_weight, 1)
        if step == 2:
            return [(grad_low, partners[1])]
        return ()

    def took_out(step, arrived, filled):
        if step == 1:
            w_both.extend(gather(joined(a, b)) for a, b in zip(both_ends, arrived))
        elif step == n - 1:
            grad_mixed.extend(filled)
        else:
            lows.extend(arrived)

    summed = line_reduce(
        lambda s: dot(attended[s * rows : (s + 1) * rows], w_out, NT, BF16), n, while_out, along_out, took_out
    )
    hidden = source + sum(term.astype(F32) for term in summed)
    grad_two = jnp.concatenate([grad_low, lows[1]], axis=0)

    inv_two = norm_inverse(hidden)
    normed_two = (hidden * inv_two * gain_two).astype(BF16)

    def own_rows(gate):
        made = [one for w, gm in zip(w_both, grad_mixed) for one in gated(gate, w, gm, 0)]
        return [spread(made[1::3] + made[2::3], weights, 0, F32, HIDES, 0, 2), *made]

    swap = partners[0] + partners[1]
    weights = [(w, 0) for w in w_both] + [(w, 1) for w in w_both]
    (two_theirs,), (ours_first, *mine) = travel([(normed_two, swap)], own_rows)
    two = jnp.concatenate([normed_two, two_theirs], axis=0)
    mixed, grad_gate, grad_up, d_down = [None] * slices, [None] * slices, [None] * slices, [None] * slices
    rows_in = two_theirs
    for k in range(slices - 1, -1, -1):
        mixed[k], grad_gate[k], grad_up[k] = gated(rows_in, w_both[k], grad_mixed[k], 1, mine[3 * k : 3 * k + 3])
        if k > 0:
            d_down[k] = dot(grad_two, mixed[k], TN, BF16)
            rows_in = after(two_theirs, d_down[k])
    grads = grad_gate + grad_up
    d_up, d_gate = [None] * slices, [None] * slices

    def second_half(gate):
        return (
            spread([after(grads[0], gate)] + grads[1:], weights, 1, BF16, HIDES, 1, 2),
            *(dot(two, after(g, gate), TN, BF16) for g in grad_up[1:]),
        )

    def gate_weights(gate):
        return (
            spread([after(grads[0], gate)] + grads[1:], weights, 0, F32, HIDES, 1, 2),
            *(dot(two, after(g, gate), TN, BF16) for g in grad_gate[1:]),
        )

    theirs = spread(grads, weights, 1, BF16, HIDES, 0, 2)
    (from_first,), (theirs, *d_up[1:]) = travel([(theirs, swap)], second_half)
    (from_second,), (ours_second, *d_gate[1:]) = travel([(theirs, swap)], gate_weights)
    grad_hidden, grad_hidden_low = norm_back(
        [(ours_first, 0, 1), (ours_second, 1, 1), (from_first, 0, 1), (from_second, 1, 1)], hidden, gain_two, cotangent, live, True
    )

    def owner_sum(partial):
        return lax.psum_scatter(partial, "dp", scatter_dimension=0, tiled=True)

    results, early = [], []

    def d_of(left, right, gate):
        return dot(left, after(right, gate), TN, BF16)

    def result_rows(part, out, gate, cost=HIDES):
        return spread([after(mixed[0], gate), *mixed[1:]], [(w, 0) for w in w_down], part, out, cost)

    def while_gather(step, gate):
        if step == 1:
            flops = 2 * rows * width * slices * gate_weight.shape[1]
            cost = pl.CostEstimate(flops=flops, transcendentals=0, bytes_accessed=flops // rows)
            return (result_rows(1, BF16, gate, cost), d_of(grad_two, mixed[0], gate))
        if step == 2:
            return (result_rows(0, F32, gate), d_of(two, grad_up[0], gate), *joined_sums())
        if step == n - 1:
            return (d_of(two, grad_gate[0], gate),)
        return ()

    def took_gather(step, arrived, filled):
        early.extend(arrived)
        if step == 1:
            results.append(filled[0])
            d_down[0] = filled[1]
        elif step == 2:
            results.append(filled[0])
            d_up[0] = filled[1]
            sums.extend(filled[2:])
        elif step == n - 1:
            d_gate[0] = filled[0]

    sums = []

    def joined_sums():
        return [jnp.concatenate([owner_sum(a), owner_sum(b)], axis=1) for a, b in zip(d_down[1:], d_up[1:])]

    slots_back, grad_attended = line_gather(
        grad_hidden_low,
        n,
        lambda s, shard: dot(shard, w_out, NN, BF16),
        while_gather,
        lambda step: {
            2: [(results[0], partners[0])] if results else (),
            n - 1: to_owners(sums, 0),
        }.get(step, ()),
        took_gather,
    )
    result_ends, sum_ends = early[0], early[1:]

    def attention_back(gate):
        return (
            attend_back(after(slot_table, gate), *grad_attended, rotated, attended, lse, *tables),
            d_of(jnp.concatenate(slots_back, axis=0), attended, gate),
            sum_down,
        )

    sums_gate = [owner_sum(d) for d in d_gate[1:]]
    sum_down, sum_up, sum_gate = owner_sum(d_down[0]), owner_sum(d_up[0]), owner_sum(d_gate[0])
    leaving = [after(one, grad_attended[n - 1]) for one in sums_gate]
    back_gate, (grad_qkv, d_out, _) = travel(
        [(one, a + b) for one, (a, b) in zip(leaving, homeward)], attention_back
    )
    back_down, back_up, outputs, d_attention = [], [], [], []
    all_heads = own_qkv.shape[1]

    def columns(array, offset, size):
        return jnp.concatenate(
            [array[:, g * wide + offset : g * wide + offset + size] for g in range(heads_kv)], axis=1
        ).astype(F32)


    def while_reduce(step, gate):
        if step == 1:
            d_qkv = d_of(jnp.concatenate(slots_one, axis=0), grad_qkv, gate)
            return (jnp.concatenate([d_qkv, d_out], axis=1), sum_up)
        if step == 2:
            return (sum_gate,)
        if step == n - 1:
            from_partner = joined(result_ends, outputs[0])
            result = hidden + (results[1] + after(from_partner, gate).astype(F32))
            sum_attention = owner_sum(d_attention[0])
            return (
                (result * live).astype(BF16),
                turned(sum_attention, all_heads, out_weight.shape[0]),
                *(columns(sum_attention, *place) for place in ((0, qw), (qw, hd), (qw + hd, hd))),
                sum_attention,
            )
        return ()

    def along_reduce(step):
        if step == 1:
            return to_owners(sums, 1)
        if step == 2:
            return [(results[0], partners[1])]
        return ()

    def took_reduce(step, arrived, filled):
        if step == 1:
            for a, b in zip(sum_ends, arrived):
                back = joined(a, b)
                back_down.append(back[:, : down_t.shape[1]])
                back_up.append(back[:, down_t.shape[1] :])
            d_attention.append(filled[0])
        elif step == 2:
            outputs.extend(arrived)
        elif step == n - 1:
            outputs.extend(filled)

    grad_normed_one = line_reduce(
        lambda s: dot(grad_qkv[s * rows : (s + 1) * rows], w_qkv, NT, BF16),
        n,
        while_reduce,
        along_reduce,
        took_reduce,
    )
    _, output, grad_out_w, grad_query_w, grad_key_w, grad_value_w, sum_attention = outputs

    def whole(first, back):
        return sum((one.astype(F32) for one in back), first.astype(F32))

    grad_down_w = whole(sum_down, back_down).T
    grad_gate_w = whole(sum_gate, back_gate)
    grad_up_w = whole(sum_up, back_up)
    grad_qkv_w = sum_attention[:, :all_heads].astype(F32)
    def along_row(weight, grad):
        return jnp.sum(weight.astype(F32) * grad, axis=1)

    gain_parts = jnp.stack(
        [
            along_row(own_qkv, grad_qkv_w),
            along_row(gate_weight, grad_gate_w) + along_row(up_weight, grad_up_w),
        ]
    )
    gain_own = lax.psum(gain_parts, "tensor") / jnp.stack([attn_gain, mlp_gain]).astype(F32)

    grad_tokens = norm_back([(term, 0, 2) for term in grad_normed_one], tokens, gain_one, grad_hidden, None, False)

    return (
        output,
        grad_tokens,
        grad_query_w,
        grad_key_w,
        grad_value_w,
        grad_out_w,
        gain_own[0],
        grad_gate_w,
        grad_up_w,
        grad_down_w,
        gain_own[1],
    )


def solution(mesh):
    rows = P(("dp", "tensor"), None)
    row = P(("dp", "tensor"))
    down_cols = P("tensor", "dp")
    cols = P("dp", "tensor")
    return jax.shard_map(
        shards,
        mesh=mesh,
        in_specs=(rows, rows, row, row, P("dp"), cols, cols, cols, down_cols, P("dp"), cols, cols, down_cols, P("dp")),
        out_specs=(rows, rows, cols, cols, cols, down_cols, P("dp"), cols, cols, down_cols, P("dp")),
        check_vma=False,
    )
```
